128 devices in a mesh: tile: 16 (over x, y), view: 8 (over z, core).
Axes of the slice: x: 4, y: 4, z: 4, core: 2. Of those that a mesh axis runs over, the one named last changes fastest.
Arguments:
- estimate: float32 [2, 224, 448, 128], P(None, 'view', 'tile'), may hold values from 0.25 to 4
- view_data: bfloat16 [8, 16, 3, 2, 58, 58, 128], P('view', 'tile'), may hold values from 0.25 to 4
- psf: float32 [6, 3, 31], replicated, may hold values from 0 to 0.5, as said below
- background: float32 [6], replicated, may hold values from 0.1 to 1
- slot_brick: int32 [8, 16, 3], P('view', 'tile'), may hold values from 0 to 15, as said below
- slot_view: int32 [8, 16, 3], P('view', 'tile'), may hold values from 0 to 5, as said below
- intersection: int32 [8, 16, 6], P('view', 'tile'), may hold values from 0 to 1, as said below
Outputs:
- updated: float32 [2, 224, 448, 128], P(None, 'view', 'tile')
The draws below stay inside these ranges and needn't reach their ends.
Inputs may be any that keep to these rules, and one draw needn't show every extreme that they name: `slot_brick`: within a group, the jobs are exactly the pairs (brick, view) that intersection marks, each once; every brick has at least one view and one brick of each group has all 6; the jobs of a group fill its workers' 3 slots exactly. `slot_view`: the view of each job, consistent with intersection. `intersection`: each brick's row has between 1 and 6 ones. `psf`: all taps are positive.
All inputs are finite; a program needn't handle non-finite values.
Results may differ from the reference program's by a relative error of at most 0.0003.
Values may be sent and summed in bfloat16 or wider, within the bound.
No kernel may reach another device: no remote copies, remote signals or barrier semaphores. Data moves between devices by JAX's collectives and lax.ppermute only.
A program may use at most 128 MiB of HBM per device.

```python
import math
import jax
import jax.numpy as jnp
from jax import lax

C = 2
VIEWS = 6
TAPS = 31
HALO = 15
BX = 28
BY = 28
NZ = 128
SLOTS = 3
PX = 58
PY = 58
NX = 224
NY = 448
N_TILE = 16
N_VIEW = 8


def group_tables(group_key):
    bricks = N_TILE
    full_key, fill_key, order_key, perm_key = jax.random.split(group_key, 4)
    full_brick = jax.random.randint(full_key, (), 0, bricks)
    counts = jnp.where(jnp.arange(bricks) == full_brick, VIEWS, 1).astype(jnp.int32)
    extra = bricks * SLOTS - bricks - VIEWS + 1

    def add_one(index, counts):
        scores = jax.random.randint(jax.random.fold_in(fill_key, index), (bricks,), 0, 1 << 20) * bricks + jnp.arange(bricks)
        scores = jnp.where(counts < VIEWS, scores, -1)
        return counts + (jnp.arange(bricks) == jnp.argmax(scores)).astype(jnp.int32)
    counts = lax.fori_loop(0, extra, add_one, counts)

    def one_permutation(perm_piece):
        return jax.random.permutation(perm_piece, VIEWS)
    perms = jax.vmap(one_permutation)(jax.random.split(perm_key, bricks))
    ranks = jnp.argsort(perms, axis=1)
    intersection = (ranks < counts[:, None]).astype(jnp.int32)
    pairs = bricks * VIEWS
    scores = jax.random.randint(order_key, (pairs,), 0, 1 << 20) * pairs + jnp.arange(pairs)
    scores = jnp.where(intersection.reshape(pairs) > 0, scores, scores + (1 << 20) * pairs)
    order = jnp.argsort(scores)[:bricks * SLOTS]
    slot_brick = (order // VIEWS).reshape(bricks, SLOTS).astype(jnp.int32)
    slot_view = (order % VIEWS).reshape(bricks, SLOTS).astype(jnp.int32)
    return (slot_brick, slot_view, intersection)


def job_tables(key):
    group_keys = jax.random.split(jax.random.fold_in(key, 7), N_VIEW)
    return jax.vmap(group_tables)(group_keys)


def draw_slot_brick(key, part):
    return job_tables(key)[0]


def draw_slot_view(key, part):
    return job_tables(key)[1]


def draw_intersection(key, part):
    return job_tables(key)[2]


def draw_psf(key, part):
    width_key, rough_key = jax.random.split(jax.random.fold_in(key, 11))
    widths = jnp.exp(jax.random.uniform(width_key, (VIEWS, 3, 1), jnp.float32, math.log(1.5), math.log(5.0)))
    reach = (jnp.arange(TAPS) - (TAPS - 1) // 2).astype(jnp.float32)
    rough = jax.random.uniform(rough_key, (VIEWS, 3, TAPS), jnp.float32, 0.6, 1.4)
    return jnp.exp(-0.5 * (reach / widths) ** 2) * rough / (widths * 2.5066283)


def steps_of(stream_key, shape, cuts, least, largest):
    gain, own = 1.0, jax.random.fold_in(stream_key, 6)
    for dim, shards_of in cuts:
        steps = jnp.exp(jax.random.uniform(jax.random.fold_in(own, dim), (shards_of,), jnp.float32, least / len(cuts), largest / len(cuts)))
        gain = gain * jnp.repeat(steps, shape[dim] // shards_of).reshape([-1 if axis == dim else 1 for axis in range(len(shape))])
    return gain


def setup_inputs(seed: int = 0) -> dict:
    key_of = jax.random.split(jax.random.key(seed), 8)
    estimate = jnp.clip(jnp.exp(math.log(4.0) - 2.7725887 * jax.random.uniform(key_of[0], (C, NX, NY, NZ), jnp.float32) ** steps_of(key_of[0], (C, NX, NY, NZ), ((1, 8), (2, 16)), -0.2, 0.2)), 0.25, 4.0)
    view_data = jnp.clip(jnp.exp(math.log(4.0) - 2.7725887 * jax.random.uniform(key_of[1], (N_VIEW, N_TILE, SLOTS, C, PX, PY, NZ), jnp.float32) ** steps_of(key_of[1], (N_VIEW, N_TILE, SLOTS, C, PX, PY, NZ), ((0, 8), (1, 16)), -0.2, 0.2)), 0.25, 4.0).astype(jnp.bfloat16)
    psf = draw_psf(jax.random.fold_in(key_of[7], 71), 0)
    background = jnp.clip(jnp.exp(jax.random.uniform(key_of[3], (VIEWS,), jnp.float32, math.log(0.1), math.log(1.0))), 0.1, 1.0)
    slot_brick = draw_slot_brick(jax.random.fold_in(key_of[7], 71), 0)
    slot_view = draw_slot_view(jax.random.fold_in(key_of[7], 71), 0)
    intersection = draw_intersection(jax.random.fold_in(key_of[7], 71), 0)
    return {"estimate": estimate, "view_data": view_data, "psf": psf, "background": background, "slot_brick": slot_brick, "slot_view": slot_view, "intersection": intersection}


def banded(kernel_taps, order, rim_width):
    offsets = jnp.arange(order)[None, :] - jnp.arange(order)[:, None] + rim_width
    matches = offsets[:, :, None] == jnp.arange(kernel_taps.shape[0])[None, None, :]
    return jnp.sum(jnp.where(matches, kernel_taps[None, None, :], 0.0), axis=2)


def forward_blur(block, kernels, rim_width):
    band_x = banded(kernels[0], block.shape[1], rim_width)
    band_y = banded(kernels[1], block.shape[2], rim_width)
    band_z = banded(kernels[2], block.shape[3], rim_width)
    result = jnp.einsum('cxyz,wz->cxyw', block, band_z, precision=lax.Precision.HIGHEST)
    result = jnp.einsum('cxyz,vy->cxvz', result, band_y, precision=lax.Precision.HIGHEST)
    return jnp.einsum('cxyz,ux->cuyz', result, band_x, precision=lax.Precision.HIGHEST)


def backward_blur(ratio, kernels, rim_width, brick_x, brick_y):
    band_x = banded(kernels[0], ratio.shape[1], rim_width)[:, rim_width:rim_width + brick_x]
    band_y = banded(kernels[1], ratio.shape[2], rim_width)[:, rim_width:rim_width + brick_y]
    band_z = banded(kernels[2], ratio.shape[3], rim_width)
    result = jnp.einsum('cxyz,xu->cuyz', ratio, band_x, precision=lax.Precision.HIGHEST)
    result = jnp.einsum('cxyz,yv->cxvz', result, band_y, precision=lax.Precision.HIGHEST)
    return jnp.einsum('cxyz,zw->cxyw', result, band_z, precision=lax.Precision.HIGHEST)


def reference(estimate, view_data, psf, background, slot_brick, slot_view, intersection):
    est_wire = estimate.astype(jnp.bfloat16)
    padded = jnp.pad(est_wire, ((0, 0), (HALO, HALO), (HALO, HALO), (0, 0)))
    job_count = N_VIEW * N_TILE * SLOTS
    measured_all = view_data.reshape(job_count, C, PX, PY, NZ)
    groups_all = (jnp.arange(job_count) // (N_TILE * SLOTS)).astype(jnp.int32)
    bricks_all = slot_brick.reshape(job_count).astype(jnp.int32)
    views_all = slot_view.reshape(job_count).astype(jnp.int32)
    anchor = jnp.int32(0)

    def apply_job(summed, job_item):
        measured, group_index, brick_index, view_index = job_item
        start_x = (group_index * BX).astype(jnp.int32)
        start_y = (brick_index * BY).astype(jnp.int32)
        block = lax.dynamic_slice(padded, (anchor, start_x, start_y, anchor), (C, PX, PY, NZ)).astype(jnp.float32)
        kernels = lax.dynamic_index_in_dim(psf, view_index, 0, keepdims=False)
        backdrop = lax.dynamic_index_in_dim(background, view_index, 0, keepdims=False)
        predicted = forward_blur(block, kernels, HALO) + backdrop
        ratio = measured.astype(jnp.float32) / predicted
        factor = backward_blur(ratio, kernels, HALO, BX, BY)
        previous = lax.dynamic_slice(summed, (anchor, start_x, start_y, anchor), (C, BX, BY, NZ))
        summed = lax.dynamic_update_slice(summed, previous + factor, (anchor, start_x, start_y, anchor))
        return summed, None

    summed = jnp.zeros((C, NX, NY, NZ), jnp.float32)
    summed, unused = lax.scan(apply_job, summed, (measured_all, groups_all, bricks_all, views_all))
    views_seen = jnp.sum(intersection, axis=2).astype(jnp.float32)
    seen_field = jnp.repeat(jnp.repeat(views_seen, BX, axis=0), BY, axis=1)
    return estimate * summed / seen_field[None, :, :, None]
```

```python
import functools

import jax
import jax.numpy as jnp
from jax import lax
from jax.experimental import pallas as pl
from jax.experimental.pallas import tpu as pltpu
from jax.sharding import PartitionSpec as P

F32, BF16, I32 = jnp.float32, jnp.bfloat16, jnp.int32
HALO = 15
SIDE = 28
WIN = SIDE + 2 * HALO
PADW = 64
PADS = 32
RIM = 16
RING = 4


def torus_step(array, dx, dy):
    pairs = [
        (x * RING + y, ((x + dx) % RING) * RING + (y + dy) % RING)
        for x in range(RING)
        for y in range(RING)
    ]
    return lax.ppermute(array, "tile", pairs)


def ring_gather(arrays, axes):
    step = lambda a, axis, d: torus_step(a, d if axis == 0 else 0, d if axis == 1 else 0)
    near = [(step(a, ax, 1), step(a, ax, -1)) for a, ax in zip(arrays, axes)]
    far = []
    for (lower, upper), ax in zip(near, axes):
        half = lower.shape[0] // 2
        far.append((step(lower[:half], ax, 1), step(upper[half:], ax, -1)))
    return [
        jnp.concatenate([a, lo, up, f0, f1], axis=0)
        for a, (lo, up), (f0, f1) in zip(arrays, near, far)
    ]


def place_of(brick, me, x_first):
    def rank(delta):
        delta = delta % RING
        return jnp.where(delta == 3, 1, jnp.where(delta == 1, 2, jnp.where(delta == 2, 3, 0)))

    in_x = rank(brick // RING - me // RING)
    in_y = rank(brick % RING - me % RING)
    return (in_y * RING + in_x if x_first else in_x * RING + in_y).astype(I32)


def window_table(bricks, me, x_first):
    count = RING * RING
    before = jnp.maximum(bricks - 1, 0)
    after = jnp.minimum(bricks + 1, count - 1)
    return jnp.stack(
        [
            place_of(before, me, x_first),
            place_of(bricks, me, x_first),
            place_of(after, me, x_first),
            (bricks > 0).astype(I32),
            (bricks < count - 1).astype(I32),
        ]
    )


def margin_kernel(table, prev_ref, own_ref, next_ref, out_ref):
    side, slot = pl.program_id(0), pl.program_id(1)
    item = side * pl.num_programs(1) + slot
    has_prev, has_next = table[3, item] > 0, table[4, item] > 0

    def move(first):
        zero = jnp.zeros((HALO, RIM, 128), F32)
        rows = slice(first, first + RIM)
        prev = prev_ref[SIDE - HALO : SIDE, rows, :].astype(F32)
        out_ref[0, 0, 0:HALO] = jnp.where(has_prev, prev, zero).astype(BF16)
        out_ref[0, 0, HALO : HALO + SIDE] = own_ref[:, rows, :]
        after = next_ref[0:HALO, rows, :].astype(F32)
        out_ref[0, 0, HALO + SIDE : WIN] = jnp.where(has_next, after, zero).astype(BF16)

    pl.when(side == 0)(functools.partial(move, SIDE - RIM))
    pl.when(side == 1)(functools.partial(move, 0))


def brick_spec(which, item_of):
    return pl.BlockSpec(
        (SIDE, PADS, 128), lambda *args: (args[-1][which, item_of(*args[:-1])], 0, 0)
    )


def margins(gathered, table):
    slots = table.shape[1] // 2
    specs = [brick_spec(i, lambda side, slot: side * slots + slot) for i in range(3)]
    return pl.pallas_call(
        margin_kernel,
        grid_spec=pltpu.PrefetchScalarGridSpec(
            num_scalar_prefetch=1,
            grid=(2, slots),
            in_specs=specs,
            out_specs=pl.BlockSpec(
                (1, 1, WIN, RIM, 128), lambda side, slot, table: (side, slot, 0, 0, 0)
            ),
        ),
        out_shape=jax.ShapeDtypeStruct((2, slots, WIN, RIM, 128), BF16),
        name="margins",
    )(table, gathered, gathered, gathered)


def split(value):
    high = value.astype(BF16)
    low = (value - high.astype(F32)).astype(BF16)
    return high, low


def stacked(first, second):
    (h0, l0), (h1, l1) = split(first), split(second)
    high = jnp.concatenate([h0, h1], axis=1)
    low = jnp.concatenate([l0, l1], axis=1)
    return jnp.concatenate([high, low, high], axis=0)


def dot(a, b):
    return jnp.dot(a, b, preferred_element_type=F32)


def job_kernel(
    table, prev_ref, own_ref, next_ref, top_ref, bottom_ref, data_ref, back_ref,
    mz_ref, mx_ref, my_ref, myt_ref, mxt_ref, mzt_ref, out_ref,
    block, blurred_x, back_y, back_x,
):
    slot = pl.program_id(0)
    has_prev, has_next = table[3, slot] > 0, table[4, slot] > 0
    mid = slice(RIM, RIM + PADS)

    @pl.when(slot == 0)
    def _():
        block[WIN:] = jnp.zeros_like(block[WIN:])
        blurred_x[WIN * PADW :] = jnp.zeros_like(blurred_x[WIN * PADW :])
        back_y[WIN * PADS :] = jnp.zeros_like(back_y[WIN * PADS :])
        back_x[SIDE * PADS :] = jnp.zeros_like(back_x[SIDE * PADS :])

    zero = jnp.zeros((HALO, PADS, 128), F32)
    block[0:WIN, 0:RIM, :] = top_ref[0]
    block[0:WIN, RIM + PADS :, :] = bottom_ref[0]
    prev = prev_ref[SIDE - HALO : SIDE].astype(F32)
    block[0:HALO, mid, :] = jnp.where(has_prev, prev, zero).astype(BF16)
    block[HALO : HALO + SIDE, mid, :] = own_ref[...]
    after = next_ref[0:HALO].astype(F32)
    block[HALO + SIDE : WIN, mid, :] = jnp.where(has_next, after, zero).astype(BF16)

    mz, mx, my = mz_ref[0], mx_ref[0], my_ref[0]
    myt, mxt, mzt = myt_ref[0], mxt_ref[0], mzt_ref[0]
    backdrop = back_ref[slot]

    def along_zx(i, carry):
        rows = block[pl.ds(2 * i, 2)].reshape(2 * PADW, 128)
        in_z = dot(jnp.concatenate([rows, rows], axis=1), mz)
        in_x = dot(mx, stacked(in_z[:PADW], in_z[PADW:]))
        start = pl.multiple_of(2 * i * PADW, 2 * PADW)
        blurred_x[pl.ds(start, PADW), :] = in_x[:, :128]
        blurred_x[pl.ds(start + PADW, PADW), :] = in_x[:, 128:]
        return carry

    lax.fori_loop(0, WIN // 2, along_zx, 0, unroll=UNROLL)

    valid = lax.broadcasted_iota(I32, (PADW, 256), 0) < WIN

    def along_y(i, carry):
        u = 2 * i
        lines = [blurred_x[pl.ds(u + j, PADW, stride=PADW), :] for j in range(2)]
        predicted = dot(my, stacked(*lines)) + backdrop
        seen = jnp.concatenate([data_ref[0, 0, u], data_ref[0, 0, u + 1]], axis=1)
        ratio = jnp.where(valid, seen.astype(F32) / predicted, 0.0)
        in_y = dot(myt, stacked(ratio[:, :128], ratio[:, 128:]))
        start = pl.multiple_of(u * PADS, 2 * PADS)
        back_y[pl.ds(start, PADS), :] = in_y[:, :128]
        back_y[pl.ds(start + PADS, PADS), :] = in_y[:, 128:]
        return carry

    lax.fori_loop(0, WIN // 2, along_y, 0, unroll=UNROLL)

    def along_x(i, carry):
        y = 2 * i
        lines = [back_y[pl.ds(y + j, PADW, stride=PADS), :] for j in range(2)]
        in_x = dot(mxt, stacked(*lines))
        start = pl.multiple_of(y * PADS, 2 * PADS)
        back_x[pl.ds(start, PADS), :] = in_x[:, :128]
        back_x[pl.ds(start + PADS, PADS), :] = in_x[:, 128:]
        return carry

    lax.fori_loop(0, SIDE // 2, along_x, 0, unroll=UNROLL)

    group = 4
    for i in range(SIDE // group):
        lines = [back_x[pl.ds(group * i + j, PADS, stride=PADS), :] for j in range(group)]
        high, low = split(jnp.concatenate(lines, axis=0))
        factor = dot(jnp.concatenate([high, low, high], axis=1), mzt)
        for j in range(group):
            x = group * i + j
            first = (x % 2) * SIDE
            out_ref[x // 2, 0, first : first + SIDE, :] = factor[j * PADS : j * PADS + SIDE]
    for k in range(SIDE // 2, 16):
        out_ref[k, 0] = jnp.zeros_like(out_ref[k, 0])


UNROLL = 4


def run_jobs(channel, gathered, table, top, bottom, view_data, backdrops, mats):
    slots = table.shape[1]
    per_slot = lambda shape: pl.BlockSpec(
        (1,) + shape, lambda slot, table: (slot,) + (0,) * len(shape)
    )
    specs = [brick_spec(i, lambda slot: slot) for i in range(3)]
    specs += [per_slot((WIN, RIM, 128))] * 2
    specs += [
        pl.BlockSpec((1, 1, WIN, PADW, 128), lambda slot, table: (slot, channel, 0, 0, 0)),
        pl.BlockSpec(memory_space=pltpu.SMEM),
    ]
    specs += [per_slot(m.shape[1:]) for m in mats]
    return pl.pallas_call(
        job_kernel,
        grid_spec=pltpu.PrefetchScalarGridSpec(
            num_scalar_prefetch=1,
            grid=(slots,),
            in_specs=specs,
            out_specs=pl.BlockSpec((16, 1, 2 * SIDE, 128), lambda slot, table: (0, slot, 0, 0)),
            scratch_shapes=[
                pltpu.VMEM((PADW, PADW, 128), BF16),
                pltpu.VMEM((PADW * PADW, 128), F32),
                pltpu.VMEM((PADW * PADS, 128), F32),
                pltpu.VMEM((PADS * PADS, 128), F32),
            ],
        ),
        out_shape=jax.ShapeDtypeStruct((16, slots, 2 * SIDE, 128), F32),
        compiler_params=pltpu.CompilerParams(vmem_limit_bytes=40 << 20),
        name="jobs",
    )(table, gathered, gathered, gathered, top, bottom, view_data, backdrops, *mats)


def bands(taps, positions_out, positions_in):
    offsets = positions_in[None, :] - positions_out[:, None] + HALO
    sel = offsets[None, :, :, None] == jnp.arange(taps.shape[1])[None, None, None, :]
    return jnp.sum(jnp.where(sel, taps[:, None, None, :], 0.0), axis=3)


def high_low(matrix):
    high = lax.reduce_precision(matrix, 8, 7)
    return high.astype(BF16), (matrix - high).astype(BF16)


def job_matrices(taps):
    none = -1000
    far = 1000
    line = jnp.arange(128)
    row = jnp.arange(PADW)
    win_in = jnp.where(row < WIN, row, none)
    win_out = jnp.where(row < WIN, row, far)
    short = jnp.arange(PADS)
    inner_out = jnp.where(short < SIDE, short + HALO, far)
    x_in = jnp.where(row < RIM + SIDE, row - 1, row - 1 - (PADS - SIDE))
    x_in = jnp.where((row >= RIM + SIDE) & (row < RIM + PADS), none, x_in)
    x_in = jnp.where((x_in < 0) | (x_in >= WIN), none, x_in)
    forward = lambda t, out, inp: bands(t, out, inp)
    backward = lambda t, out, inp: jnp.swapaxes(bands(t, inp, out), 1, 2)
    three = lambda pair: jnp.concatenate([pair[0], pair[0], pair[1]], axis=2)
    mz = high_low(jnp.swapaxes(forward(taps[:, 2], line, line), 1, 2))
    mzt = high_low(jnp.swapaxes(backward(taps[:, 2], line, line), 1, 2))
    win_in_far = jnp.where(row < WIN, row, far)
    inner_none = jnp.where(short < SIDE, short + HALO, none)
    return (
        jnp.concatenate(mz, axis=1),
        three(high_low(forward(taps[:, 0], win_out, x_in))),
        three(high_low(forward(taps[:, 1], win_out, win_in))),
        three(high_low(backward(taps[:, 1], inner_none, win_in_far))),
        three(high_low(backward(taps[:, 0], inner_none, win_in_far))),
        jnp.concatenate([mzt[0], mzt[0], mzt[1]], axis=1),
    )


def add_kernel(owners, parts_ref, out_ref):
    out_ref[...] = jnp.zeros_like(out_ref)
    slots = parts_ref.shape[1]
    for w in range(parts_ref.shape[0]):
        for s in range(slots):
            b = owners[w * slots + s]
            out_ref[b] += parts_ref[w, s]


def add_up(owners, parts):
    return pl.pallas_call(
        add_kernel,
        in_specs=[pl.BlockSpec(memory_space=pltpu.SMEM), pl.BlockSpec(memory_space=pltpu.VMEM)],
        out_specs=pl.BlockSpec(memory_space=pltpu.VMEM),
        out_shape=jax.ShapeDtypeStruct((16,) + parts.shape[2:], F32),
        name="add_up",
    )(owners, parts)


def update_kernel(count, est_ref, *refs):
    out_ref = refs[-1]
    seen = count[0].astype(F32)
    for c, total in enumerate(refs[:-1]):
        for k in range(SIDE // 2):
            for j in range(2):
                rows = total[k, j * SIDE : (j + 1) * SIDE, :]
                out_ref[c, 2 * k + j] = est_ref[c, 2 * k + j] * rows / seen


def update(count, estimate, totals):
    vmem = pl.BlockSpec(memory_space=pltpu.VMEM)
    return pl.pallas_call(
        update_kernel,
        in_specs=[pl.BlockSpec(memory_space=pltpu.SMEM)] + [vmem] * (1 + len(totals)),
        out_specs=vmem,
        out_shape=jax.ShapeDtypeStruct(estimate.shape, F32),
        compiler_params=pltpu.CompilerParams(vmem_limit_bytes=24 << 20),
        name="update",
    )(count, estimate, *totals)


def pick(table, rows):
    return jnp.stack([lax.dynamic_index_in_dim(table, r, 0, keepdims=False) for r in rows])


def on_device(estimate, view_data, psf, background, slot_brick, slot_view, intersection):
    me = lax.axis_index("tile").astype(I32)
    groups = lax.axis_size("view")
    upward = [(i, i + 1) for i in range(groups - 1)]
    downward = [(j, i) for i, j in upward]
    bricks, views = slot_brick[0, 0], slot_view[0, 0]

    wire = estimate.astype(BF16).transpose(0, 2, 1, 3)
    wire = jnp.pad(wire, ((0, 0), (0, 0), (0, PADS - SIDE), (0, 0)))
    above = lax.ppermute(bricks, "view", downward)
    below = lax.ppermute(bricks, "view", upward)
    gathered = ring_gather([wire[0], wire[1]], (0, 1))
    gathered = ring_gather(gathered, (1, 0))

    taps = pick(psf, views)
    backdrops = pick(background, views)
    mats = job_matrices(taps)
    owners = lax.all_gather(bricks, "tile", axis=0, tiled=True)
    count = jnp.sum(intersection[0, 0]).reshape(1)

    totals = []
    for channel in range(2):
        x_first = channel == 0
        wanted = window_table(jnp.concatenate([above, below]), me, x_first)
        edge = margins(gathered[channel], wanted)
        top = lax.ppermute(edge[0], "view", upward)
        bottom = lax.ppermute(edge[1], "view", downward)
        factors = run_jobs(
            channel,
            gathered[channel],
            window_table(bricks, me, x_first),
            top,
            bottom,
            view_data[0, 0],
            backdrops,
            mats,
        )
        parts = lax.all_to_all(factors, "tile", 0, 0, tiled=True)
        summed = add_up(owners, parts)
        totals.append(lax.all_to_all(summed, "tile", 0, 0, tiled=True))
    return update(count, estimate, totals)


def solution(mesh):
    placed = (
        P(None, "view", "tile", None),
        P("view", "tile", None, None, None, None, None),
        P(),
        P(),
        P("view", "tile", None),
        P("view", "tile", None),
        P("view", "tile", None),
    )
    return jax.shard_map(
        on_device,
        mesh=mesh,
        in_specs=placed,
        out_specs=P(None, "view", "tile", None),
        check_vma=False,
    )
```

```python
import functools

import jax
import jax.numpy as jnp
from jax import lax
from jax.experimental import pallas as pl
from jax.experimental.pallas import tpu as pltpu
from jax.sharding import PartitionSpec as P

F32, BF16, I32 = jnp.float32, jnp.bfloat16, jnp.int32
HALO = 15
SIDE = 28
WIN = SIDE + 2 * HALO
PADW = 64
PADS = 32
RIM = 16
RING = 4


def far_memory(*arrays):
    return [pltpu.with_memory_space_constraint(a, pltpu.HBM) for a in arrays]


def torus_step(array, dx, dy):
    pairs = [
        (x * RING + y, ((x + dx) % RING) * RING + (y + dy) % RING)
        for x in range(RING)
        for y in range(RING)
    ]
    return lax.ppermute(array, "tile", pairs)


def ring_gather(arrays, axes):
    step = lambda a, axis, d: torus_step(a, d if axis == 0 else 0, d if axis == 1 else 0)
    near = [(step(a, ax, 1), step(a, ax, -1)) for a, ax in zip(arrays, axes)]
    far = []
    for (lower, upper), ax in zip(near, axes):
        half = lower.shape[0] // 2
        far.append((step(lower[:half], ax, 1), step(upper[half:], ax, -1)))
    return [[a, *n, *f] for a, n, f in zip(arrays, near, far)]


def place_of(brick, me, x_first):
    def rank(delta):
        delta = delta % RING
        return jnp.where(delta == 3, 1, jnp.where(delta == 1, 2, jnp.where(delta == 2, 3, 0)))

    in_x = rank(brick // RING - me // RING)
    in_y = rank(brick % RING - me % RING)
    return (in_y * RING + in_x if x_first else in_x * RING + in_y).astype(I32)


def window_table(bricks, me, x_first):
    count = RING * RING
    near = [jnp.maximum(bricks - 1, 0), bricks, jnp.minimum(bricks + 1, count - 1)]
    return jnp.stack([place_of(b, me, x_first) for b in near])


WINDOWS = ((SIDE - HALO, HALO, 0), (0, SIDE, HALO), (0, HALO, HALO + SIDE))


def copy_window(parts, which, place, rows, target, sem):
    first, count, _ = WINDOWS[which]
    base = 0
    for part in parts:
        held = part.shape[0] // SIDE

        @pl.when((place >= base) & (place < base + held))
        def _(part=part, base=base):
            source = part.at[pl.ds((place - base) * SIDE + first, count), rows]
            pltpu.make_async_copy(source, target, sem).start()

        base += held


def wait_window(parts, which, rows, target, sem):
    count = WINDOWS[which][1]
    pltpu.make_async_copy(parts[0].at[pl.ds(0, count), rows], target, sem).wait()


def margin_kernel(*refs):
    tables, refs = refs[:2], refs[2:]
    sems, refs = refs[-1], refs[:-1]
    gathered, outs = (refs[:PARTS], refs[PARTS : 2 * PARTS]), refs[2 * PARTS :]
    slots = outs[0].shape[0]
    everything = []
    for channel, (table, parts) in enumerate(zip(tables, gathered)):
        for side in range(2):
            rows = pl.ds(RIM, RIM) if side == 0 else pl.ds(0, RIM)
            for slot in range(slots):
                item = side * slots + slot
                for which, (_, count, to) in enumerate(WINDOWS):
                    target = outs[2 * channel + side].at[slot, pl.ds(to, count)]
                    sem = sems.at[channel, item, which]
                    copy_window(parts, which, table[which, item], rows, target, sem)
                    everything.append((parts, which, rows, target, sem))
    for item in everything:
        wait_window(*item)


PARTS = 5


def margins(gathered, tables):
    slots = tables[0].shape[1] // 2
    hbm, smem = pl.BlockSpec(memory_space=pltpu.HBM), pl.BlockSpec(memory_space=pltpu.SMEM)
    return pl.pallas_call(
        margin_kernel,
        in_specs=[smem] * 2 + [hbm] * (2 * PARTS),
        out_specs=[hbm] * 4,
        out_shape=[pltpu.HBM((slots, WIN, RIM, 128), BF16)] * 4,
        scratch_shapes=[pltpu.SemaphoreType.DMA((2, 2 * slots, 3))],
        compiler_params=pltpu.CompilerParams(vmem_limit_bytes=1 << 20),
        name="margins",
    )(*tables, *far_memory(*gathered[0], *gathered[1]))


def split(value):
    high = value.astype(BF16)
    low = (value - high.astype(F32)).astype(BF16)
    return high, low


def pair(first, second):
    (h0, l0), (h1, l1) = split(first), split(second)
    return jnp.concatenate([h0, h1], axis=1), jnp.concatenate([l0, l1], axis=1)


def three_term(matrix, high, low):
    return dot(matrix, jnp.concatenate([high, low, high], axis=0))


def dot(a, b):
    return jnp.dot(a, b, preferred_element_type=F32)


def job_kernel(channel, table, backdrops, *refs):
    parts, refs = refs[:PARTS], refs[PARTS:]
    top_ref, bottom_ref, data_ref, mz_ref, mx_ref, my_ref, myt_ref, mxt_ref, mzt_ref, out_ref = refs[:10]
    blocks, seen_data, z_high, z_low, blurred_x, back_y, back_x, sems = refs[10:]
    slot, slots = pl.program_id(0), pl.num_programs(0)
    mid = pl.ds(RIM, PADS)

    def others(which_slot, buffer):
        span = pl.ds(0, WIN)
        return (
            (top_ref.at[which_slot], blocks.at[buffer, span, pl.ds(0, RIM)], sems.at[buffer, 3]),
            (bottom_ref.at[which_slot], blocks.at[buffer, span, pl.ds(RIM + PADS, RIM)], sems.at[buffer, 4]),
            (data_ref.at[which_slot, channel], seen_data.at[buffer], sems.at[buffer, 5]),
        )

    def fetch(which_slot, buffer):
        for which, (_, count, to) in enumerate(WINDOWS):
            target = blocks.at[buffer, pl.ds(to, count), mid]
            place = table[which, which_slot]
            copy_window(parts, which, place, pl.ds(0, PADS), target, sems.at[buffer, which])
        for source, target, sem in others(which_slot, buffer):
            pltpu.make_async_copy(source, target, sem).start()

    buffer = lax.rem(slot, 2)

    @pl.when(slot == 0)
    def _():
        fetch(0, 0)
        blurred_x[WIN * PW :] = jnp.zeros_like(blurred_x[WIN * PW :])
        back_y[WIN * PS :] = jnp.zeros_like(back_y[WIN * PS :])
        back_x[SIDE * PS :] = jnp.zeros_like(back_x[SIDE * PS :])

    @pl.when(slot + 1 < slots)
    def _():
        fetch(slot + 1, 1 - buffer)

    for which, (_, count, to) in enumerate(WINDOWS):
        target = blocks.at[buffer, pl.ds(to, count), mid]
        wait_window(parts, which, pl.ds(0, PADS), target, sems.at[buffer, which])
    for source, target, sem in others(slot, buffer):
        pltpu.make_async_copy(source, target, sem).wait()

    mz, mx, my = mz_ref[0], mx_ref[0], my_ref[0]
    myt, mxt, mzt = myt_ref[0], mxt_ref[0], mzt_ref[0]
    backdrop = backdrops[table[3, slot]]

    def along_z(i, carry):
        start = i * CHUNK
        rows = blocks[buffer, pl.ds(start, CHUNK)].reshape(CHUNK * PADW, 128)
        in_z = dot(jnp.concatenate([rows, rows], axis=1), mz)
        high, low = split(in_z)
        z_high[pl.ds(start, CHUNK)] = high.reshape(CHUNK, PADW, 128)
        z_low[pl.ds(start, CHUNK)] = low.reshape(CHUNK, PADW, 128)
        return carry

    lax.fori_loop(0, -(-WIN // CHUNK), along_z, 0, unroll=UZ)

    def along_x_first(i, carry):
        y = 2 * i
        high = jnp.concatenate([z_high[y], z_high[y + 1]], axis=1)
        low = jnp.concatenate([z_low[y], z_low[y + 1]], axis=1)
        in_x = three_term(mx, high, low)
        start = pl.multiple_of(y * PW, 16)
        blurred_x[pl.ds(start, PADW), :] = in_x[:, :128]
        blurred_x[pl.ds(start + PW, PADW), :] = in_x[:, 128:]
        return carry

    lax.fori_loop(0, WIN // 2, along_x_first, 0, unroll=UNROLL)

    def along_y(i, carry):
        u = 2 * i
        lines = [blurred_x[pl.ds(u + j, PADW, stride=PW), :] for j in range(2)]
        predicted = three_term(my, *pair(*lines)) + backdrop
        seen = jnp.concatenate([seen_data[buffer, u], seen_data[buffer, u + 1]], axis=1)
        ratio = seen.astype(F32) / predicted
        in_y = three_term(myt, *pair(ratio[:, :128], ratio[:, 128:]))
        start = pl.multiple_of(u * PS, 16)
        back_y[pl.ds(start, PADS), :] = in_y[:, :128]
        back_y[pl.ds(start + PS, PADS), :] = in_y[:, 128:]
        return carry

    lax.fori_loop(0, WIN // 2, along_y, 0, unroll=UNROLL)

    def along_x(i, carry):
        y = 2 * i
        lines = [back_y[pl.ds(y + j, PADW, stride=PS), :] for j in range(2)]
        in_x = three_term(mxt, *pair(*lines))
        start = pl.multiple_of(y * PS, 16)
        back_x[pl.ds(start, PADS), :] = in_x[:, :128]
        back_x[pl.ds(start + PS, PADS), :] = in_x[:, 128:]
        return carry

    lax.fori_loop(0, SIDE // 2, along_x, 0, unroll=UNROLL)

    group = 4
    for i in range(SIDE // group):
        lines = [back_x[pl.ds(group * i + j, PADS, stride=PS), :] for j in range(group)]
        high, low = split(jnp.concatenate(lines, axis=0))
        factor = dot(jnp.concatenate([high, low, high], axis=1), mzt)
        for j in range(group):
            x = group * i + j
            first = (x % 2) * SIDE
            out_ref[x // 2, 0, first : first + SIDE, :] = factor[j * PADS : j * PADS + SIDE]
    for k in range(SIDE // 2, 16):
        out_ref[k, 0] = jnp.zeros_like(out_ref[k, 0])


UNROLL = 29
CHUNK = 29
PEXTRA = 8
SEXTRA = 8
PW = PADW + PEXTRA
PS = PADS + SEXTRA
UZ = 1


def run_jobs(channel, parts, table, top, bottom, view_data, backdrops, mats):
    slots = table.shape[1]
    hbm = pl.BlockSpec(memory_space=pltpu.HBM)
    smem = pl.BlockSpec(memory_space=pltpu.SMEM)
    specs = [smem, smem] + [hbm] * (len(parts) + 3)
    specs += [pl.BlockSpec((1,) + m.shape[1:], lambda slot: (slot, 0, 0)) for m in mats]
    return pl.pallas_call(
        functools.partial(job_kernel, channel),
        grid=(slots,),
        in_specs=specs,
        out_specs=pl.BlockSpec((16, 1, 2 * SIDE, 128), lambda slot: (0, slot, 0, 0)),
        scratch_shapes=[
            pltpu.VMEM((2, WIN, PADW, 128), BF16),
            pltpu.VMEM((2, WIN, PADW, 128), BF16),
            pltpu.VMEM((WIN, PADW, 128), BF16),
            pltpu.VMEM((WIN, PADW, 128), BF16),
            pltpu.VMEM((PADW * PW, 128), F32),
            pltpu.VMEM((PADW * PS, 128), F32),
            pltpu.VMEM((PADS * PS, 128), F32),
            pltpu.SemaphoreType.DMA((2, 6)),
        ],
        out_shape=pltpu.HBM((16, slots, 2 * SIDE, 128), F32),
        compiler_params=pltpu.CompilerParams(vmem_limit_bytes=18 << 20),
        cost_estimate=pl.CostEstimate(
            flops=slots * 2 * 128 * (WIN * PADW * (256 + 192 + 192 + 96) + 2 * SIDE * PADS * 192),
            transcendentals=slots * WIN * PADW * 128,
            bytes_accessed=slots * (2 * WIN * PADW * 128 * 2 + 16 * 2 * SIDE * 128 * 4),
        ),
        name="jobs",
    )(table, backdrops, *far_memory(*parts, top, bottom, view_data, *mats))


def bands(taps, positions_out, positions_in):
    offsets = positions_in[None, :] - positions_out[:, None] + HALO
    sel = offsets[None, :, :, None] == jnp.arange(taps.shape[1])[None, None, None, :]
    return jnp.sum(jnp.where(sel, taps[:, None, None, :], 0.0), axis=3)


def high_low(matrix):
    high = lax.reduce_precision(matrix, 8, 7)
    return high.astype(BF16), (matrix - high).astype(BF16)


def job_matrices(taps, bricks):
    none = -1000
    far = 1000
    line = jnp.arange(128)
    row = jnp.arange(PADW)
    win_in = jnp.where(row < WIN, row, none)
    win_out = jnp.where(row < WIN, row, far)
    short = jnp.arange(PADS)
    inner_out = jnp.where(short < SIDE, short + HALO, far)
    x_in = jnp.where(row < RIM + 16, row - 1, row - 5)
    x_in = jnp.where((row >= RIM + 16) & (row < RIM + 20), none, x_in)
    x_in = jnp.where((x_in < 0) | (x_in >= WIN), none, x_in)
    inside = (row >= HALO)[None, :] | (bricks > 0)[:, None]
    inside &= (row < HALO + SIDE)[None, :] | (bricks < RING * RING - 1)[:, None]
    forward = lambda t, out, inp: bands(t, out, inp)
    backward = lambda t, out, inp: jnp.swapaxes(bands(t, inp, out), 1, 2)
    three = lambda pair: jnp.concatenate([pair[0], pair[0], pair[1]], axis=2)
    mz = high_low(jnp.swapaxes(forward(taps[:, 2], line, line), 1, 2))
    mzt = high_low(jnp.swapaxes(backward(taps[:, 2], line, line), 1, 2))
    win_in_far = jnp.where(row < WIN, row, far)
    inner_none = jnp.where(short < SIDE, short + HALO, none)
    return (
        jnp.concatenate(mz, axis=1),
        three(high_low(forward(taps[:, 0], win_out, x_in))),
        three(high_low(jnp.where(inside[:, None, :], forward(taps[:, 1], win_out, win_in), 0.0))),
        three(high_low(backward(taps[:, 1], inner_none, win_in_far))),
        three(high_low(backward(taps[:, 0], inner_none, win_in_far))),
        jnp.concatenate([mzt[0], mzt[0], mzt[1]], axis=1),
    )


def add_kernel(owners, parts_ref, out_ref):
    out_ref[...] = jnp.zeros_like(out_ref)
    slots = parts_ref.shape[1]
    for w in range(parts_ref.shape[0]):
        for s in range(slots):
            b = owners[w * slots + s]
            out_ref[b] += parts_ref[w, s]


def add_up(owners, parts):
    return pl.pallas_call(
        add_kernel,
        in_specs=[pl.BlockSpec(memory_space=pltpu.SMEM), pl.BlockSpec(memory_space=pltpu.VMEM)],
        out_specs=pl.BlockSpec(memory_space=pltpu.VMEM),
        out_shape=pltpu.HBM((16,) + parts.shape[2:], F32),
        compiler_params=pltpu.CompilerParams(vmem_limit_bytes=8 << 20),
        name="add_up",
    )(owners, parts)


def update_kernel(count, est_ref, *refs):
    out_ref = refs[-1]
    seen = count[0].astype(F32)
    for c, total in enumerate(refs[:-1]):
        for k in range(SIDE // 2):
            for j in range(2):
                rows = total[k, j * SIDE : (j + 1) * SIDE, :]
                out_ref[c, 2 * k + j] = est_ref[c, 2 * k + j] * rows / seen


def update(count, estimate, totals):
    vmem = pl.BlockSpec(memory_space=pltpu.VMEM)
    return pl.pallas_call(
        update_kernel,
        in_specs=[pl.BlockSpec(memory_space=pltpu.SMEM)] + [vmem] * (1 + len(totals)),
        out_specs=vmem,
        out_shape=jax.ShapeDtypeStruct(estimate.shape, F32),
        compiler_params=pltpu.CompilerParams(vmem_limit_bytes=12 << 20),
        name="update",
    )(count, estimate, *totals)


def on_device(estimate, view_data, psf, background, slot_brick, slot_view, intersection):
    me = lax.axis_index("tile").astype(I32)
    groups, workers = lax.axis_size("view"), lax.axis_size("tile")
    upward = [(i, i + 1) for i in range(groups - 1)]
    downward = [(j, i) for i, j in upward]
    bricks, views = slot_brick[0, 0], slot_view[0, 0]
    slots = bricks.shape[0]

    wire = estimate.astype(BF16).transpose(0, 2, 1, 3)
    wire = jnp.concatenate([wire[:, :, :RIM], wire[:, :, SIDE - RIM :]], axis=2)
    rings = ring_gather([wire[0], wire[1]], (0, 1))
    above = lax.ppermute(bricks, "view", downward)
    below = lax.ppermute(bricks, "view", upward)
    spread = jnp.broadcast_to(jnp.pad(bricks, (0, 128 - slots))[None, None], (workers, 8, 128))
    owners = lax.all_to_all(spread, "tile", 0, 0, tiled=True)[:, 0, :slots].reshape(-1)

    taps = jnp.stack([lax.dynamic_index_in_dim(psf, v, 0, keepdims=False) for v in views])
    mats = job_matrices(taps, bricks)
    data = jnp.pad(view_data[0, 0], ((0, 0),) * 3 + ((0, PADW - WIN), (0, 0)))
    count = jnp.sum(intersection[0, 0]).reshape(1)
    tables = []
    for x_first in (True, False):
        wanted = window_table(jnp.concatenate([above, below]), me, x_first)
        mine = jnp.concatenate([window_table(bricks, me, x_first), views[None]])
        tables.append((wanted, mine))

    rings = [jnp.concatenate(parts, axis=0) for parts in rings]
    rings, mats, data, tables, owners, count = lax.optimization_barrier(
        (rings, mats, data, tables, owners, count)
    )
    gathered = ring_gather(rings, (1, 0))

    rims = margins(gathered, [wanted for wanted, _ in tables])
    edges = [
        (lax.ppermute(rims[2 * c], "view", upward), lax.ppermute(rims[2 * c + 1], "view", downward))
        for c in range(2)
    ]
    edges = lax.optimization_barrier(edges)
    totals = []
    for channel in range(2):
        factors = run_jobs(
            channel, gathered[channel], tables[channel][1], *edges[channel], data, background, mats
        )
        parts = lax.all_to_all(factors, "tile", 0, 0, tiled=True)
        summed = add_up(owners, parts)
        totals.append(lax.all_to_all(summed, "tile", 0, 0, tiled=True))
    return update(count, estimate, totals)


def solution(mesh):
    placed = (
        P(None, "view", "tile", None),
        P("view", "tile", None, None, None, None, None),
        P(),
        P(),
        P("view", "tile", None),
        P("view", "tile", None),
        P("view", "tile", None),
    )
    return jax.shard_map(
        on_device,
        mesh=mesh,
        in_specs=placed,
        out_specs=P(None, "view", "tile", None),
        check_vma=False,
    )
```

```python
import functools

import jax
import jax.numpy as jnp
from jax import lax
from jax.experimental import pallas as pl
from jax.experimental.pallas import tpu as pltpu
from jax.sharding import PartitionSpec as P

F32, BF16, I32 = jnp.float32, jnp.bfloat16, jnp.int32
HALO = 15
SIDE = 28
WIN = SIDE + 2 * HALO
PADW = 64
PADS = 32
RIM = 16
RING = 4


def far_memory(*arrays):
    return [pltpu.with_memory_space_constraint(a, pltpu.HBM) for a in arrays]


def torus_step(array, dx, dy):
    pairs = [
        (x * RING + y, ((x + dx) % RING) * RING + (y + dy) % RING)
        for x in range(RING)
        for y in range(RING)
    ]
    return lax.ppermute(array, "tile", pairs)


def along(axis, step):
    return (step, 0) if axis == 0 else (0, step)


def ring_near(arrays, axes):
    return [
        [a, torus_step(a, *along(ax, 1)), torus_step(a, *along(ax, -1))]
        for a, ax in zip(arrays, axes)
    ]


def ring_far(near, axes):
    result = []
    for (own, lower, upper), ax in zip(near, axes):
        half = lower.shape[0] // 2
        far = [torus_step(lower[:half], *along(ax, 1)), torus_step(upper[half:], *along(ax, -1))]
        result.append([own, lower, upper, *far])
    return result


def place_of(brick, me, x_first):
    def rank(delta):
        delta = delta % RING
        return jnp.where(delta == 3, 1, jnp.where(delta == 1, 2, jnp.where(delta == 2, 3, 0)))

    in_x = rank(brick // RING - me // RING)
    in_y = rank(brick % RING - me % RING)
    return (in_y * RING + in_x if x_first else in_x * RING + in_y).astype(I32)


def window_table(bricks, me, x_first):
    count = RING * RING
    near = [jnp.maximum(bricks - 1, 0), bricks, jnp.minimum(bricks + 1, count - 1)]
    return jnp.stack([place_of(b, me, x_first) for b in near])


WINDOWS = ((SIDE - HALO, HALO, 0), (0, SIDE, HALO), (0, HALO, HALO + SIDE))


def copy_window(parts, which, place, rows, target, sem):
    first, count, _ = WINDOWS[which]
    base = 0
    for part in parts:
        held = part.shape[0] // SIDE

        @pl.when((place >= base) & (place < base + held))
        def _(part=part, base=base):
            source = part.at[pl.ds((place - base) * SIDE + first, count), rows]
            pltpu.make_async_copy(source, target, sem).start()

        base += held


def wait_window(parts, which, rows, target, sem):
    count = WINDOWS[which][1]
    pltpu.make_async_copy(parts[0].at[pl.ds(0, count), rows], target, sem).wait()


def margin_kernel(*refs):
    tables, refs = refs[:2], refs[2:]
    refs, (stage, sems) = refs[:-2], refs[-2:]
    gathered, outs = (refs[:PARTS], refs[PARTS : 2 * PARTS]), refs[2 * PARTS :]
    slots = outs[0].shape[0]
    copies = []
    for channel, (table, parts) in enumerate(zip(tables, gathered)):
        for side in range(2):
            rows = pl.ds(RIM, RIM) if side == 0 else pl.ds(0, RIM)
            for slot in range(slots):
                item = side * slots + slot
                waits = []
                for which, (_, count, to) in enumerate(WINDOWS):
                    target = stage.at[channel, item, pl.ds(to, count)]
                    sem = sems.at[channel, item, which]
                    copy_window(parts, which, table[which, item], rows, target, sem)
                    waits.append((parts, which, rows, target, sem))
                out = pltpu.make_async_copy(
                    stage.at[channel, item],
                    outs[2 * channel + side].at[slot],
                    sems.at[channel, item, 3],
                )
                copies.append((waits, out))
    for waits, out in copies:
        for item in waits:
            wait_window(*item)
        out.start()
    for _, out in copies:
        out.wait()


PARTS = 5


def margins(gathered, tables):
    slots = tables[0].shape[1] // 2
    hbm, smem = pl.BlockSpec(memory_space=pltpu.HBM), pl.BlockSpec(memory_space=pltpu.SMEM)
    return pl.pallas_call(
        margin_kernel,
        in_specs=[smem] * 2 + [hbm] * (2 * PARTS),
        out_specs=[hbm] * 4,
        out_shape=[pltpu.HBM((slots, WIN, RIM, 128), BF16)] * 4,
        scratch_shapes=[
            pltpu.VMEM((2, 2 * slots, WIN, RIM, 128), BF16),
            pltpu.SemaphoreType.DMA((2, 2 * slots, 4)),
        ],
        compiler_params=pltpu.CompilerParams(vmem_limit_bytes=4 << 20),
        name="margins",
    )(*tables, *far_memory(*gathered[0], *gathered[1]))


def split(value):
    high = value.astype(BF16)
    low = (value - high.astype(F32)).astype(BF16)
    return high, low


def pair(first, second):
    (h0, l0), (h1, l1) = split(first), split(second)
    return jnp.concatenate([h0, h1], axis=1), jnp.concatenate([l0, l1], axis=1)


def three_term(matrix, high, low):
    return dot(matrix, jnp.concatenate([high, low, high], axis=0))


def dot(a, b):
    return jnp.dot(a, b, preferred_element_type=F32)


def job_kernel(channel, table, backdrops, *refs):
    parts, refs = refs[:PARTS], refs[PARTS:]
    top_ref, bottom_ref, data_ref, mz_ref, mx_ref, my_ref, myt_ref, mxt_ref, mzt_ref, out_ref = refs[:10]
    blocks, seen_data, z_high, z_low, blurred_x, back_y, back_x, sems = refs[10:]
    slot, slots = pl.program_id(0), pl.num_programs(0)
    mid = pl.ds(RIM, PADS)

    def others(which_slot, buffer):
        span = pl.ds(0, WIN)
        return (
            (top_ref.at[which_slot], blocks.at[buffer, span, pl.ds(0, RIM)], sems.at[buffer, 3]),
            (bottom_ref.at[which_slot], blocks.at[buffer, span, pl.ds(RIM + PADS, RIM)], sems.at[buffer, 4]),
            (data_ref.at[which_slot, channel], seen_data.at[buffer], sems.at[buffer, 5]),
        )

    def fetch(which_slot, buffer):
        for which, (_, count, to) in enumerate(WINDOWS):
            target = blocks.at[buffer, pl.ds(to, count), mid]
            place = table[which, which_slot]
            copy_window(parts, which, place, pl.ds(0, PADS), target, sems.at[buffer, which])
        for source, target, sem in others(which_slot, buffer):
            pltpu.make_async_copy(source, target, sem).start()

    buffer = lax.rem(slot, 2)

    @pl.when(slot == 0)
    def _():
        fetch(0, 0)
        blurred_x[WIN * PW :] = jnp.zeros_like(blurred_x[WIN * PW :])
        back_y[WIN * PS :] = jnp.zeros_like(back_y[WIN * PS :])
        back_x[SIDE * PS :] = jnp.zeros_like(back_x[SIDE * PS :])

    @pl.when(slot + 1 < slots)
    def _():
        fetch(slot + 1, 1 - buffer)

    for which, (_, count, to) in enumerate(WINDOWS):
        target = blocks.at[buffer, pl.ds(to, count), mid]
        wait_window(parts, which, pl.ds(0, PADS), target, sems.at[buffer, which])
    for source, target, sem in others(slot, buffer):
        pltpu.make_async_copy(source, target, sem).wait()

    mz, mx, my = mz_ref[0], mx_ref[0], my_ref[0]
    myt, mxt, mzt = myt_ref[0], mxt_ref[0], mzt_ref[0]
    backdrop = backdrops[table[3, slot]]

    def along_z(i, carry):
        start = i * CHUNK
        rows = blocks[buffer, pl.ds(start, CHUNK)].reshape(CHUNK * PADW, 128)
        in_z = dot(jnp.concatenate([rows, rows], axis=1), mz)
        high, low = split(in_z)
        z_high[pl.ds(start, CHUNK)] = high.reshape(CHUNK, PADW, 128)
        z_low[pl.ds(start, CHUNK)] = low.reshape(CHUNK, PADW, 128)
        return carry

    lax.fori_loop(0, -(-WIN // CHUNK), along_z, 0, unroll=UZ)

    def along_x_first(i, carry):
        y = 2 * i
        high = jnp.concatenate([z_high[y], z_high[y + 1]], axis=1)
        low = jnp.concatenate([z_low[y], z_low[y + 1]], axis=1)
        in_x = three_term(mx, high, low)
        start = pl.multiple_of(y * PW, 16)
        blurred_x[pl.ds(start, PADW), :] = in_x[:, :128]
        blurred_x[pl.ds(start + PW, PADW), :] = in_x[:, 128:]
        return carry

    lax.fori_loop(0, WIN // 2, along_x_first, 0, unroll=UNROLL)

    past = jnp.zeros((PADW - WIN, 256), F32)

    def along_y(i, carry):
        u = 2 * i
        lines = [blurred_x[pl.ds(u + j, PADW, stride=PW), :] for j in range(2)]
        predicted = three_term(my, *pair(*lines)) + backdrop
        seen = jnp.concatenate([seen_data[buffer, u], seen_data[buffer, u + 1]], axis=1)
        ratio = jnp.concatenate([seen.astype(F32) / predicted[:WIN], past], axis=0)
        in_y = three_term(myt, *pair(ratio[:, :128], ratio[:, 128:]))
        start = pl.multiple_of(u * PS, 16)
        back_y[pl.ds(start, PADS), :] = in_y[:, :128]
        back_y[pl.ds(start + PS, PADS), :] = in_y[:, 128:]
        return carry

    lax.fori_loop(0, WIN // 2, along_y, 0, unroll=UNROLL)

    def along_x(i, carry):
        y = 2 * i
        lines = [back_y[pl.ds(y + j, PADW, stride=PS), :] for j in range(2)]
        in_x = three_term(mxt, *pair(*lines))
        start = pl.multiple_of(y * PS, 16)
        back_x[pl.ds(start, PADS), :] = in_x[:, :128]
        back_x[pl.ds(start + PS, PADS), :] = in_x[:, 128:]
        return carry

    lax.fori_loop(0, SIDE // 2, along_x, 0, unroll=UNROLL)

    group = 4
    for i in range(SIDE // group):
        lines = [back_x[pl.ds(group * i + j, PADS, stride=PS), :] for j in range(group)]
        high, low = split(jnp.concatenate(lines, axis=0))
        factor = dot(jnp.concatenate([high, low, high], axis=1), mzt)
        for j in range(group):
            x = group * i + j
            first = (x % 2) * SIDE
            out_ref[x // 2, 0, first : first + SIDE, :] = factor[j * PADS : j * PADS + SIDE]
    for k in range(SIDE // 2, 16):
        out_ref[k, 0] = jnp.zeros_like(out_ref[k, 0])


UNROLL = 29
CHUNK = 29
PEXTRA = 8
SEXTRA = 8
PW = PADW + PEXTRA
PS = PADS + SEXTRA
UZ = 1


def run_jobs(channel, parts, table, top, bottom, view_data, backdrops, mats):
    slots = table.shape[1]
    hbm = pl.BlockSpec(memory_space=pltpu.HBM)
    smem = pl.BlockSpec(memory_space=pltpu.SMEM)
    specs = [smem, smem] + [hbm] * (len(parts) + 3)
    specs += [pl.BlockSpec((1,) + m.shape[1:], lambda slot: (slot, 0, 0)) for m in mats]
    return pl.pallas_call(
        functools.partial(job_kernel, channel),
        grid=(slots,),
        in_specs=specs,
        out_specs=pl.BlockSpec((16, 1, 2 * SIDE, 128), lambda slot: (0, slot, 0, 0)),
        scratch_shapes=[
            pltpu.VMEM((2, WIN, PADW, 128), BF16),
            pltpu.VMEM((2, WIN, WIN, 128), BF16),
            pltpu.VMEM((WIN, PADW, 128), BF16),
            pltpu.VMEM((WIN, PADW, 128), BF16),
            pltpu.VMEM((PADW * PW, 128), F32),
            pltpu.VMEM((PADW * PS, 128), F32),
            pltpu.VMEM((PADS * PS, 128), F32),
            pltpu.SemaphoreType.DMA((2, 6)),
        ],
        out_shape=pltpu.HBM((16, slots, 2 * SIDE, 128), F32),
        compiler_params=pltpu.CompilerParams(vmem_limit_bytes=18 << 20),
        cost_estimate=pl.CostEstimate(
            flops=slots * 2 * 128 * (WIN * PADW * (256 + 192 + 192 + 96) + 2 * SIDE * PADS * 192),
            transcendentals=slots * WIN * PADW * 128,
            bytes_accessed=slots * (2 * WIN * PADW * 128 * 2 + 16 * 2 * SIDE * 128 * 4),
        ),
        name="jobs",
    )(table, backdrops, *far_memory(*parts, top, bottom, view_data, *mats))


def bands(taps, positions_out, positions_in):
    offsets = positions_in[None, :] - positions_out[:, None] + HALO
    sel = offsets[None, :, :, None] == jnp.arange(taps.shape[1])[None, None, None, :]
    return jnp.sum(jnp.where(sel, taps[:, None, None, :], 0.0), axis=3)


def high_low(matrix):
    high = lax.reduce_precision(matrix, 8, 7)
    return high.astype(BF16), (matrix - high).astype(BF16)


def job_matrices(taps, bricks):
    none = -1000
    far = 1000
    line = jnp.arange(128)
    row = jnp.arange(PADW)
    win_in = jnp.where(row < WIN, row, none)
    win_out = jnp.where(row < WIN, row, far)
    short = jnp.arange(PADS)
    inner_out = jnp.where(short < SIDE, short + HALO, far)
    x_in = jnp.where(row < RIM + 16, row - 1, row - 5)
    x_in = jnp.where((row >= RIM + 16) & (row < RIM + 20), none, x_in)
    x_in = jnp.where((x_in < 0) | (x_in >= WIN), none, x_in)
    inside = (row >= HALO)[None, :] | (bricks > 0)[:, None]
    inside &= (row < HALO + SIDE)[None, :] | (bricks < RING * RING - 1)[:, None]
    forward = lambda t, out, inp: bands(t, out, inp)
    backward = lambda t, out, inp: jnp.swapaxes(bands(t, inp, out), 1, 2)
    three = lambda pair: jnp.concatenate([pair[0], pair[0], pair[1]], axis=2)
    mz = high_low(jnp.swapaxes(forward(taps[:, 2], line, line), 1, 2))
    mzt = high_low(jnp.swapaxes(backward(taps[:, 2], line, line), 1, 2))
    win_in_far = jnp.where(row < WIN, row, far)
    inner_none = jnp.where(short < SIDE, short + HALO, none)
    return (
        jnp.concatenate(mz, axis=1),
        three(high_low(forward(taps[:, 0], win_out, x_in))),
        three(high_low(jnp.where(inside[:, None, :], forward(taps[:, 1], win_out, win_in), 0.0))),
        three(high_low(backward(taps[:, 1], inner_none, win_in_far))),
        three(high_low(backward(taps[:, 0], inner_none, win_in_far))),
        jnp.concatenate([mzt[0], mzt[0], mzt[1]], axis=1),
    )


def add_kernel(owners, *refs):
    out_ref = refs[-1]
    out_ref[...] = jnp.zeros_like(out_ref)
    workers, slots = refs[0].shape[:2]
    for channel, parts_ref in enumerate(refs[:-1]):
        for w in range(workers):
            for s in range(slots):
                out_ref[owners[w * slots + s], channel] += parts_ref[w, s]


def add_up(owners, parts):
    vmem, smem = pl.BlockSpec(memory_space=pltpu.VMEM), pl.BlockSpec(memory_space=pltpu.SMEM)
    return pl.pallas_call(
        add_kernel,
        in_specs=[smem] + [vmem] * len(parts),
        out_specs=vmem,
        out_shape=pltpu.HBM((16, len(parts)) + parts[0].shape[2:], F32),
        compiler_params=pltpu.CompilerParams(vmem_limit_bytes=8 << 20),
        name="add_up",
    )(owners, *parts)


def update_kernel(count, est_ref, total, out_ref):
    seen = count[0].astype(F32)
    for c in range(out_ref.shape[0]):
        for k in range(SIDE // 2):
            for j in range(2):
                rows = total[k, c, j * SIDE : (j + 1) * SIDE, :]
                out_ref[c, 2 * k + j] = est_ref[c, 2 * k + j] * rows / seen


def update(count, estimate, total):
    vmem, smem = pl.BlockSpec(memory_space=pltpu.VMEM), pl.BlockSpec(memory_space=pltpu.SMEM)
    return pl.pallas_call(
        update_kernel,
        in_specs=[smem, vmem, vmem],
        out_specs=vmem,
        out_shape=jax.ShapeDtypeStruct(estimate.shape, F32),
        compiler_params=pltpu.CompilerParams(vmem_limit_bytes=12 << 20),
        name="update",
    )(count, estimate, total)


def on_device(estimate, view_data, psf, background, slot_brick, slot_view, intersection):
    me = lax.axis_index("tile").astype(I32)
    groups, workers = lax.axis_size("view"), lax.axis_size("tile")
    upward = [(i, i + 1) for i in range(groups - 1)]
    downward = [(j, i) for i, j in upward]
    bricks, views = slot_brick[0, 0], slot_view[0, 0]
    slots = bricks.shape[0]

    wire = estimate.astype(BF16).transpose(0, 2, 1, 3)
    note = jnp.pad(bricks.astype(BF16)[None, None], ((0, 0), (0, SIDE - 1), (0, 128 - slots)))
    note = jnp.broadcast_to(note, (wire.shape[0],) + note.shape[1:])
    wire = jnp.concatenate([wire[:, :, :RIM], note[:, :, None], wire[:, :, SIDE - RIM + 1 :]], axis=2)
    near = ring_near([wire[0], wire[1]], (0, 1))
    near, bricks = lax.optimization_barrier((near, bricks))
    above = lax.ppermute(bricks, "view", downward)
    below = lax.ppermute(bricks, "view", upward)
    rings = [jnp.concatenate(parts, axis=0) for parts in ring_far(near, (0, 1))]
    rings, view_data, psf, views, bricks = lax.optimization_barrier(
        (rings, view_data, psf, views, bricks)
    )
    near = ring_near(rings, (1, 0))

    taps = jnp.stack([lax.dynamic_index_in_dim(psf, v, 0, keepdims=False) for v in views])
    mats = job_matrices(taps, bricks)
    data = view_data[0, 0]
    count = jnp.sum(intersection[0, 0]).reshape(1)
    tables = []
    for x_first in (True, False):
        wanted = window_table(jnp.concatenate([above, below]), me, x_first)
        mine = jnp.concatenate([window_table(bricks, me, x_first), views[None]])
        tables.append((wanted, mine))
    near, mats, data, tables, count = lax.optimization_barrier((near, mats, data, tables, count))
    gathered = ring_far(near, (1, 0))

    rims = margins(gathered, [wanted for wanted, _ in tables])
    edges = [
        (lax.ppermute(rims[2 * c], "view", upward), lax.ppermute(rims[2 * c + 1], "view", downward))
        for c in range(2)
    ]
    edges = lax.optimization_barrier(edges)
    notes = jnp.concatenate([p[::SIDE, RIM, :slots] for p in gathered[0]], axis=0)
    places = place_of(jnp.arange(workers), me, True)
    match = places[:, None] == jnp.arange(workers)[None, :]
    owners = jnp.sum(jnp.where(match[:, :, None], notes.astype(F32)[None], 0.0), axis=1)
    owners = owners.astype(I32).reshape(-1)

    parts = []
    for channel in range(2):
        factors = run_jobs(
            channel, gathered[channel], tables[channel][1], *edges[channel], data, background, mats
        )
        parts.append(lax.all_to_all(factors, "tile", 0, 0, tiled=True))
    total = lax.all_to_all(add_up(owners, parts), "tile", 0, 0, tiled=True)
    return update(count, estimate, total)


def solution(mesh):
    placed = (
        P(None, "view", "tile", None),
        P("view", "tile", None, None, None, None, None),
        P(),
        P(),
        P("view", "tile", None),
        P("view", "tile", None),
        P("view", "tile", None),
    )
    return jax.shard_map(
        on_device,
        mesh=mesh,
        in_specs=placed,
        out_specs=P(None, "view", "tile", None),
        check_vma=False,
    )
```

```python
import functools

import jax
import jax.numpy as jnp
from jax import lax
from jax.experimental import pallas as pl
from jax.experimental.pallas import tpu as pltpu
from jax.sharding import PartitionSpec as P

F32, BF16, I32, I16 = jnp.float32, jnp.bfloat16, jnp.int32, jnp.int16
HALO = 15
SIDE = 28
WIN = SIDE + 2 * HALO
PADW = 64
PADS = 32
RIM = 16
RING = 4


def far_memory(*arrays):
    return [pltpu.with_memory_space_constraint(a, pltpu.HBM) for a in arrays]


def gathered_memory(parts):
    return [parts[0]] + far_memory(*parts[1:])


def torus_step(array, dx, dy):
    pairs = [
        (x * RING + y, ((x + dx) % RING) * RING + (y + dy) % RING)
        for x in range(RING)
        for y in range(RING)
    ]
    return lax.ppermute(array, "tile", pairs)


def along(axis, step):
    return (step, 0) if axis == 0 else (0, step)


def ring_near(arrays, axes):
    return [
        [a, torus_step(a, *along(ax, 1)), torus_step(a, *along(ax, -1))]
        for a, ax in zip(arrays, axes)
    ]


def ring_far(near, axes):
    result = []
    for (own, lower, upper), ax in zip(near, axes):
        half = lower.shape[0] // 2
        far = [torus_step(lower[:half], *along(ax, 1)), torus_step(upper[half:], *along(ax, -1))]
        result.append([own, lower, upper, *far])
    return result


def rank(delta):
    delta = lax.rem(delta + RING, RING)
    return jnp.where(delta == 3, 1, jnp.where(delta == 1, 2, jnp.where(delta == 2, 3, 0)))


def place_of(brick, me, x_first):
    in_x = rank(lax.div(brick, RING) - lax.div(me, RING))
    in_y = rank(lax.rem(brick, RING) - lax.rem(me, RING))
    return in_y * RING + in_x if x_first else in_x * RING + in_y


def window_place(which, brick, me, x_first):
    return place_of(jnp.clip(brick + which - 1, 0, RING * RING - 1), me, x_first)


WINDOWS = ((SIDE - HALO, HALO, 0), (0, SIDE, HALO), (0, HALO, HALO + SIDE))


def copy_window(parts, which, place, rows, target, sem):
    first, count, _ = WINDOWS[which]
    base = 0
    for part in parts:
        held = part.shape[0] // SIDE

        @pl.when((place >= base) & (place < base + held))
        def _(part=part, base=base):
            source = part.at[pl.ds((place - base) * SIDE + first, count), rows]
            pltpu.make_async_copy(source, target, sem).start()

        base += held


def wait_window(parts, which, rows, target, sem):
    count = WINDOWS[which][1]
    pltpu.make_async_copy(parts[0].at[pl.ds(0, count), rows], target, sem).wait()


def margin_kernel(*refs):
    me, *asked = refs[:3]
    refs = refs[3:]
    refs, (stage, sems) = refs[:-2], refs[-2:]
    gathered, outs = (refs[:PARTS], refs[PARTS : 2 * PARTS]), refs[2 * PARTS :]
    slots = outs[0].shape[0]
    copies = []
    for channel, parts in enumerate(gathered):
        for side in range(2):
            rows = pl.ds(RIM, RIM) if side == 0 else pl.ds(0, RIM)
            for slot in range(slots):
                item = side * slots + slot
                waits = []
                for which, (_, count, to) in enumerate(WINDOWS):
                    target = stage.at[channel, item, pl.ds(to, count)]
                    sem = sems.at[channel, item, which]
                    place = window_place(which, asked[side][slot], me[0], channel == 0)
                    copy_window(parts, which, place, rows, target, sem)
                    waits.append((parts, which, rows, target, sem))
                out = pltpu.make_async_copy(
                    stage.at[channel, item],
                    outs[2 * channel + side].at[slot],
                    sems.at[channel, item, 3],
                )
                copies.append((waits, out))
    for waits, out in copies:
        for item in waits:
            wait_window(*item)
        out.start()
    for _, out in copies:
        out.wait()


PARTS = 5


def margins(gathered, me, above, below):
    slots = above.shape[0]
    hbm, smem = pl.BlockSpec(memory_space=pltpu.HBM), pl.BlockSpec(memory_space=pltpu.SMEM)
    return pl.pallas_call(
        margin_kernel,
        in_specs=[smem] * 3 + [hbm] * (2 * PARTS),
        out_specs=[hbm] * 4,
        out_shape=[pltpu.HBM((slots, WIN, RIM, 128), BF16)] * 4,
        scratch_shapes=[
            pltpu.VMEM((2, 2 * slots, WIN, RIM, 128), BF16),
            pltpu.SemaphoreType.DMA((2, 2 * slots, 4)),
        ],
        compiler_params=pltpu.CompilerParams(vmem_limit_bytes=4 << 20),
        name="margins",
    )(me, above, below, *gathered_memory(gathered[0]), *gathered_memory(gathered[1]))


def split(value):
    high = value.astype(BF16)
    low = (value - high.astype(F32)).astype(BF16)
    return high, low


def pair(first, second):
    (h0, l0), (h1, l1) = split(first), split(second)
    return jnp.concatenate([h0, h1], axis=1), jnp.concatenate([l0, l1], axis=1)


def three_term(matrix, high, low):
    return dot(matrix, jnp.concatenate([high, low, high], axis=0))


STEPS = 2048.0


def encode(value, level):
    code = (jnp.log2(jnp.maximum(value, 1e-37)) - level) * STEPS
    return jnp.round(jnp.clip(code, -32767.0, 32767.0)).astype(I32)


def decode(code, level):
    return jnp.exp2(code.astype(I32).astype(F32) * (1.0 / STEPS) + level)


def dot(a, b):
    return jnp.dot(a, b, preferred_element_type=F32)


def job_kernel(channel, me, bricks, views, backdrops, logs, *refs):
    parts, refs = refs[:PARTS], refs[PARTS:]
    top_ref, bottom_ref, data_ref, mz_ref, mx_ref, my_ref, myt_ref, mxt_ref, mzt_ref, out_ref = refs[:10]
    blocks, seen_data, z_high, z_low, blurred_x, back_y, back_x, sems = refs[10:]
    slot, slots = pl.program_id(0), pl.num_programs(0)
    mid = pl.ds(RIM, PADS)

    def others(which_slot, buffer):
        span = pl.ds(0, WIN)
        return (
            (top_ref.at[which_slot], blocks.at[buffer, span, pl.ds(0, RIM)], sems.at[buffer, 3]),
            (bottom_ref.at[which_slot], blocks.at[buffer, span, pl.ds(RIM + PADS, RIM)], sems.at[buffer, 4]),
            (data_ref.at[which_slot, channel], seen_data.at[buffer], sems.at[buffer, 5]),
        )

    def fetch(which_slot, buffer):
        for which, (_, count, to) in enumerate(WINDOWS):
            target = blocks.at[buffer, pl.ds(to, count), mid]
            place = window_place(which, bricks[which_slot], me[0], channel == 0)
            copy_window(parts, which, place, pl.ds(0, PADS), target, sems.at[buffer, which])
        for source, target, sem in others(which_slot, buffer):
            pltpu.make_async_copy(source, target, sem).start()

    buffer = lax.rem(slot, 2)

    @pl.when(slot == 0)
    def _():
        fetch(0, 0)
        blurred_x[WIN * PW :] = jnp.zeros_like(blurred_x[WIN * PW :])
        back_y[WIN * PS :] = jnp.zeros_like(back_y[WIN * PS :])
        back_x[SIDE * PS :] = jnp.zeros_like(back_x[SIDE * PS :])

    @pl.when(slot + 1 < slots)
    def _():
        fetch(slot + 1, 1 - buffer)

    for which, (_, count, to) in enumerate(WINDOWS):
        target = blocks.at[buffer, pl.ds(to, count), mid]
        wait_window(parts, which, pl.ds(0, PADS), target, sems.at[buffer, which])
    for source, target, sem in others(slot, buffer):
        pltpu.make_async_copy(source, target, sem).wait()

    mz, mx, my = mz_ref[0], mx_ref[0], my_ref[0]
    myt, mxt, mzt = myt_ref[0], mxt_ref[0], mzt_ref[0]
    backdrop = backdrops[views[slot]]
    level = logs[views[slot]]

    def along_z(i, carry):
        start = i * CHUNK
        rows = blocks[buffer, pl.ds(start, CHUNK)].reshape(CHUNK * PADW, 128)
        in_z = dot(jnp.concatenate([rows, rows], axis=1), mz)
        high, low = split(in_z)
        z_high[pl.ds(start, CHUNK)] = high.reshape(CHUNK, PADW, 128)
        z_low[pl.ds(start, CHUNK)] = low.reshape(CHUNK, PADW, 128)
        return carry

    lax.fori_loop(0, -(-WIN // CHUNK), along_z, 0, unroll=UZ)

    def along_x_first(i, carry):
        y = 2 * i
        high = jnp.concatenate([z_high[y], z_high[y + 1]], axis=1)
        low = jnp.concatenate([z_low[y], z_low[y + 1]], axis=1)
        in_x = three_term(mx, high, low)
        start = pl.multiple_of(y * PW, 16)
        blurred_x[pl.ds(start, PADW), :] = in_x[:, :128]
        blurred_x[pl.ds(start + PW, PADW), :] = in_x[:, 128:]
        return carry

    lax.fori_loop(0, WIN // 2, along_x_first, 0, unroll=UNROLL)

    past = jnp.zeros((PADW - WIN, 256), F32)

    def along_y(i, carry):
        u = 2 * i
        lines = [blurred_x[pl.ds(u + j, PADW, stride=PW), :] for j in range(2)]
        predicted = three_term(my, *pair(*lines)) + backdrop
        seen = jnp.concatenate([seen_data[buffer, u], seen_data[buffer, u + 1]], axis=1)
        ratio = jnp.concatenate([seen.astype(F32) / predicted[:WIN], past], axis=0)
        in_y = three_term(myt, *pair(ratio[:, :128], ratio[:, 128:]))
        start = pl.multiple_of(u * PS, 16)
        back_y[pl.ds(start, PADS), :] = in_y[:, :128]
        back_y[pl.ds(start + PS, PADS), :] = in_y[:, 128:]
        return carry

    lax.fori_loop(0, WIN // 2, along_y, 0, unroll=UNROLL)

    def along_x(i, carry):
        y = 2 * i
        lines = [back_y[pl.ds(y + j, PADW, stride=PS), :] for j in range(2)]
        in_x = three_term(mxt, *pair(*lines))
        start = pl.multiple_of(y * PS, 16)
        back_x[pl.ds(start, PADS), :] = in_x[:, :128]
        back_x[pl.ds(start + PS, PADS), :] = in_x[:, 128:]
        return carry

    lax.fori_loop(0, SIDE // 2, along_x, 0, unroll=UNROLL)

    group = 4
    for i in range(SIDE // group):
        lines = [back_x[pl.ds(group * i + j, PADS, stride=PS), :] for j in range(group)]
        high, low = split(jnp.concatenate(lines, axis=0))
        factor = encode(dot(jnp.concatenate([high, low, high], axis=1), mzt), level)
        for j in range(0, group, 2):
            rows = [factor[k * PADS : k * PADS + SIDE] for k in (j, j + 1)]
            out_ref[(group * i + j) // 2, 0] = jnp.concatenate(rows, axis=0).astype(I16)
    for k in range(SIDE // 2, 16):
        out_ref[k, 0] = jnp.zeros_like(out_ref[k, 0])


UNROLL = 29
CHUNK = 29
PEXTRA = 8
SEXTRA = 8
PW = PADW + PEXTRA
PS = PADS + SEXTRA
UZ = 1


def run_jobs(channel, parts, scalars, top, bottom, view_data, mats):
    slots = mats[0].shape[0]
    hbm = pl.BlockSpec(memory_space=pltpu.HBM)
    smem = pl.BlockSpec(memory_space=pltpu.SMEM)
    specs = [smem] * len(scalars) + [hbm] * (len(parts) + 3)
    specs += [pl.BlockSpec((1,) + m.shape[1:], lambda slot: (slot, 0, 0)) for m in mats]
    return pl.pallas_call(
        functools.partial(job_kernel, channel),
        grid=(slots,),
        in_specs=specs,
        out_specs=pl.BlockSpec((16, 1, 2 * SIDE, 128), lambda slot: (0, slot, 0, 0)),
        scratch_shapes=[
            pltpu.VMEM((2, WIN, PADW, 128), BF16),
            pltpu.VMEM((2, WIN, WIN, 128), BF16),
            pltpu.VMEM((WIN, PADW, 128), BF16),
            pltpu.VMEM((WIN, PADW, 128), BF16),
            pltpu.VMEM((PADW * PW, 128), F32),
            pltpu.VMEM((PADW * PS, 128), F32),
            pltpu.VMEM((PADS * PS, 128), F32),
            pltpu.SemaphoreType.DMA((2, 6)),
        ],
        out_shape=pltpu.HBM((16, slots, 2 * SIDE, 128), I16),
        compiler_params=pltpu.CompilerParams(vmem_limit_bytes=18 << 20),
        cost_estimate=pl.CostEstimate(
            flops=slots * 2 * 128 * (WIN * PADW * (256 + 192 + 192 + 96) + 2 * SIDE * PADS * 192),
            transcendentals=slots * WIN * PADW * 128,
            bytes_accessed=slots * (2 * WIN * PADW * 128 * 2 + 16 * 2 * SIDE * 128 * 4),
        ),
        name="jobs",
    )(*scalars, *gathered_memory(parts), *far_memory(top, bottom, view_data, *mats))


def bands(taps, positions_out, positions_in):
    offsets = positions_in[None, :] - positions_out[:, None] + HALO
    sel = offsets[None, :, :, None] == jnp.arange(taps.shape[1])[None, None, None, :]
    return jnp.sum(jnp.where(sel, taps[:, None, None, :], 0.0), axis=3)


def high_low(matrix):
    high = lax.reduce_precision(matrix, 8, 7)
    return high.astype(BF16), (matrix - high).astype(BF16)


def job_matrices(taps, bricks):
    none = -1000
    far = 1000
    line = jnp.arange(128)
    row = jnp.arange(PADW)
    win_in = jnp.where(row < WIN, row, none)
    win_out = jnp.where(row < WIN, row, far)
    short = jnp.arange(PADS)
    inner_out = jnp.where(short < SIDE, short + HALO, far)
    x_in = jnp.where(row < RIM + 16, row - 1, row - 5)
    x_in = jnp.where((row >= RIM + 16) & (row < RIM + 20), none, x_in)
    x_in = jnp.where((x_in < 0) | (x_in >= WIN), none, x_in)
    inside = (row >= HALO)[None, :] | (bricks > 0)[:, None]
    inside &= (row < HALO + SIDE)[None, :] | (bricks < RING * RING - 1)[:, None]
    forward = lambda t, out, inp: bands(t, out, inp)
    backward = lambda t, out, inp: jnp.swapaxes(bands(t, inp, out), 1, 2)
    three = lambda pair: jnp.concatenate([pair[0], pair[0], pair[1]], axis=2)
    mz = high_low(jnp.swapaxes(forward(taps[:, 2], line, line), 1, 2))
    mzt = high_low(jnp.swapaxes(backward(taps[:, 2], line, line), 1, 2))
    win_in_far = jnp.where(row < WIN, row, far)
    inner_none = jnp.where(short < SIDE, short + HALO, none)
    return (
        jnp.concatenate(mz, axis=1),
        three(high_low(forward(taps[:, 0], win_out, x_in))),
        three(high_low(jnp.where(inside[:, None, :], forward(taps[:, 1], win_out, win_in), 0.0))),
        three(high_low(backward(taps[:, 1], inner_none, win_in_far))),
        three(high_low(backward(taps[:, 0], inner_none, win_in_far))),
        jnp.concatenate([mzt[0], mzt[0], mzt[1]], axis=1),
    )


MORE = 2.6


def add_kernel(owners, views, logs, *refs):
    total, level = refs[-2:]
    out_ref = refs[-3]
    workers, slots = refs[0].shape[:2]
    jobs = range(workers * slots)
    for b in range(workers):
        level[b] = -200.0
    for i in jobs:
        level[owners[i]] = jnp.maximum(level[owners[i]], logs[views[i]] + MORE)
    for channel, parts_ref in enumerate(refs[:-3]):
        total[...] = jnp.zeros_like(total)
        for i in jobs:
            total[owners[i]] += decode(parts_ref[i // slots, i % slots], logs[views[i]])
        for b in range(workers):
            out_ref[b, channel] = encode(total[b], level[b]).astype(I16)


def add_up(owners, views, logs, parts):
    vmem, smem = pl.BlockSpec(memory_space=pltpu.VMEM), pl.BlockSpec(memory_space=pltpu.SMEM)
    workers, rows = parts[0].shape[0], parts[0].shape[2:]
    return pl.pallas_call(
        add_kernel,
        in_specs=[smem] * 3 + [vmem] * len(parts),
        out_specs=vmem,
        out_shape=pltpu.HBM((workers, len(parts)) + rows, I16),
        scratch_shapes=[pltpu.VMEM((workers,) + rows, F32), pltpu.SMEM((workers,), F32)],
        compiler_params=pltpu.CompilerParams(vmem_limit_bytes=8 << 20),
        name="add_up",
    )(owners, views, logs, *parts)


def update_kernel(met, logs, est_ref, total, out_ref):
    seen, level = jnp.int32(0), jnp.float32(-200.0)
    for v in range(met.shape[0]):
        seen += met[v]
        level = jnp.where(met[v] > 0, jnp.maximum(level, logs[v] + MORE), level)
    seen = seen.astype(F32)
    for c in range(out_ref.shape[0]):
        for k in range(SIDE // 2):
            rows = decode(total[k, c], level)
            for j in range(2):
                part = rows[j * SIDE : (j + 1) * SIDE]
                out_ref[c, 2 * k + j] = est_ref[c, 2 * k + j] * part / seen


def update(met, logs, estimate, total):
    vmem, smem = pl.BlockSpec(memory_space=pltpu.VMEM), pl.BlockSpec(memory_space=pltpu.SMEM)
    return pl.pallas_call(
        update_kernel,
        in_specs=[smem, smem, vmem, vmem],
        out_specs=vmem,
        out_shape=jax.ShapeDtypeStruct(estimate.shape, F32),
        compiler_params=pltpu.CompilerParams(vmem_limit_bytes=12 << 20),
        name="update",
    )(met, logs, estimate, total)


def on_device(estimate, view_data, psf, background, slot_brick, slot_view, intersection):
    me = lax.axis_index("tile").astype(I32).reshape(1)
    groups, workers = lax.axis_size("view"), lax.axis_size("tile")
    upward = [(i, i + 1) for i in range(groups - 1)]
    downward = [(j, i) for i, j in upward]
    bricks, views = slot_brick[0, 0], slot_view[0, 0]
    slots = bricks.shape[0]

    wire = estimate.astype(BF16).transpose(0, 2, 1, 3)
    jobs = jnp.concatenate([bricks, views])
    note = jnp.pad(jobs.astype(BF16)[None, None], ((0, 0), (0, SIDE - 1), (0, 128 - 2 * slots)))
    note = jnp.broadcast_to(note, (wire.shape[0],) + note.shape[1:])
    wire = jnp.concatenate([wire[:, :, :RIM], note[:, :, None], wire[:, :, SIDE - RIM + 1 :]], axis=2)
    near = ring_near([wire[0], wire[1]], (0, 1))
    rings = [jnp.concatenate(parts, axis=0) for parts in ring_far(near, (0, 1))]
    rings, view_data, psf, views, bricks = lax.optimization_barrier(
        (rings, view_data, psf, views, bricks)
    )
    near = ring_near(rings, (1, 0))
    above = lax.ppermute(bricks, "view", downward)
    below = lax.ppermute(bricks, "view", upward)

    chosen = views[:, None] == jnp.arange(psf.shape[0])[None, :]
    taps = jnp.sum(jnp.where(chosen[:, :, None, None], psf[None], 0.0), axis=1)
    mats = job_matrices(taps, bricks)
    data = view_data[0, 0]
    logs = jnp.log2(jnp.maximum(4.0 / background * jnp.prod(jnp.sum(psf, axis=2), axis=1), 1e-30)) - 15.9
    near, mats, data, above, below, logs = lax.optimization_barrier(
        (near, mats, data, above, below, logs)
    )
    gathered = ring_far(near, (1, 0))

    rims = margins(gathered, me, above, below)
    edges = [
        (lax.ppermute(rims[2 * c], "view", upward), lax.ppermute(rims[2 * c + 1], "view", downward))
        for c in range(2)
    ]
    edges = lax.optimization_barrier(edges)
    notes = jnp.concatenate([p[::SIDE, RIM, : 2 * slots] for p in gathered[0]], axis=0)
    places = place_of(jnp.arange(workers, dtype=I32), me[0], True)
    match = places[:, None] == jnp.arange(workers)[None, :]
    notes = jnp.sum(jnp.where(match[:, :, None], notes.astype(F32)[None], 0.0), axis=1)
    notes = notes.astype(I32)
    owners, seen_by = notes[:, :slots].reshape(-1), notes[:, slots:].reshape(-1)

    parts = []
    scalars = (me, bricks, views, background, logs)
    for channel in range(2):
        factors = run_jobs(channel, gathered[channel], scalars, *edges[channel], data, mats)
        parts.append(lax.all_to_all(factors, "tile", 0, 0, tiled=True))
    total = lax.all_to_all(add_up(owners, seen_by, logs, parts), "tile", 0, 0, tiled=True)
    return update(intersection[0, 0], logs, estimate, total)


def solution(mesh):
    placed = (
        P(None, "view", "tile", None),
        P("view", "tile", None, None, None, None, None),
        P(),
        P(),
        P("view", "tile", None),
        P("view", "tile", None),
        P("view", "tile", None),
    )
    return jax.shard_map(
        on_device,
        mesh=mesh,
        in_specs=placed,
        out_specs=P(None, "view", "tile", None),
        check_vma=False,
    )
```

```python
import functools

import jax
import jax.numpy as jnp
from jax import lax
from jax.experimental import pallas as pl
from jax.experimental.pallas import tpu as pltpu
from jax.sharding import PartitionSpec as P

F32, BF16, I32, I16 = jnp.float32, jnp.bfloat16, jnp.int32, jnp.int16
HALO = 15
SIDE = 28
WIN = SIDE + 2 * HALO
PADW = 64
PADS = 32
RIM = 16
RING = 4


def far_memory(*arrays):
    return [pltpu.with_memory_space_constraint(a, pltpu.HBM) for a in arrays]


def gathered_memory(parts):
    return [*parts[:2], *far_memory(*parts[2:])]


def torus_step(array, dx, dy):
    pairs = [
        (x * RING + y, ((x + dx) % RING) * RING + (y + dy) % RING)
        for x in range(RING)
        for y in range(RING)
    ]
    return lax.ppermute(array, "tile", pairs)


def along(axis, step):
    return (step, 0) if axis == 0 else (0, step)


def first_ring(arrays, axes):
    near = [
        (torus_step(a, *along(ax, 1)), torus_step(a, *along(ax, -1))) for a, ax in zip(arrays, axes)
    ]
    return near, [
        (
            torus_step(lower[: lower.shape[0] // 2], *along(ax, 1)),
            torus_step(upper[upper.shape[0] // 2 :], *along(ax, -1)),
        )
        for (lower, upper), ax in zip(near, axes)
    ]


def second_ring(halves, axes):
    ahead = [
        (torus_step(a, *along(ax, 1)), torus_step(b, *along(ax, -1)))
        for (a, b), ax in zip(halves, axes)
    ]
    behind = [
        (torus_step(b, *along(ax, 1)), torus_step(a, *along(ax, -1)))
        for (a, b), ax in zip(halves, axes)
    ]
    far = [
        (torus_step(la, *along(ax, 1)), torus_step(ub, *along(ax, -1)))
        for (la, ub), ax in zip(ahead, axes)
    ]
    return ahead, behind, far


def rank(delta):
    delta = lax.rem(delta + RING, RING)
    return jnp.where(delta == 3, 1, jnp.where(delta == 1, 2, jnp.where(delta == 2, 3, 0)))


def place_of(brick, me, x_first):
    in_x = rank(lax.div(brick, RING) - lax.div(me, RING))
    in_y = rank(lax.rem(brick, RING) - lax.rem(me, RING))
    return in_y * RING + in_x if x_first else in_x * RING + in_y


def window_place(which, brick, me, x_first):
    return place_of(jnp.clip(brick + which - 1, 0, RING * RING - 1), me, x_first)


WINDOWS = ((SIDE - HALO, HALO, 0), (0, SIDE, HALO), (0, HALO, HALO + SIDE))


def copy_window(parts, which, place, rows, target, sem):
    first, count, _ = WINDOWS[which]
    base = 0
    for part in parts:
        held = part.shape[0] // SIDE

        @pl.when((place >= base) & (place < base + held))
        def _(part=part, base=base):
            source = part.at[pl.ds((place - base) * SIDE + first, count), rows]
            pltpu.make_async_copy(source, target, sem).start()

        base += held


def wait_window(parts, which, rows, target, sem):
    count = WINDOWS[which][1]
    pltpu.make_async_copy(parts[0].at[pl.ds(0, count), rows], target, sem).wait()


def margin_kernel(*refs):
    me, *asked = refs[:3]
    refs = refs[3:]
    refs, (stage, sems) = refs[:-2], refs[-2:]
    gathered, outs = (refs[:PARTS], refs[PARTS : 2 * PARTS]), refs[2 * PARTS :]
    slots = outs[0].shape[0]
    copies = []
    for channel, parts in enumerate(gathered):
        for side in range(2):
            rows = pl.ds(RIM, RIM) if side == 0 else pl.ds(0, RIM)
            for slot in range(slots):
                item = side * slots + slot
                waits = []
                for which, (_, count, to) in enumerate(WINDOWS):
                    target = stage.at[channel, item, pl.ds(to, count)]
                    sem = sems.at[channel, item, which]
                    place = window_place(which, asked[side][slot], me[0], channel == 0)
                    copy_window(parts, which, place, rows, target, sem)
                    waits.append((parts, which, rows, target, sem))
                out = pltpu.make_async_copy(
                    stage.at[channel, item],
                    outs[2 * channel + side].at[slot],
                    sems.at[channel, item, 3],
                )
                copies.append((waits, out))
    for waits, out in copies:
        for item in waits:
            wait_window(*item)
        out.start()
    for _, out in copies:
        out.wait()


PARTS = 8


def margins(gathered, me, above, below):
    slots = above.shape[0]
    hbm, smem = pl.BlockSpec(memory_space=pltpu.HBM), pl.BlockSpec(memory_space=pltpu.SMEM)
    return pl.pallas_call(
        margin_kernel,
        in_specs=[smem] * 3 + [hbm] * (2 * PARTS),
        out_specs=[hbm] * 4,
        out_shape=[pltpu.HBM((slots, WIN, RIM, 128), BF16)] * 4,
        scratch_shapes=[
            pltpu.VMEM((2, 2 * slots, WIN, RIM, 128), BF16),
            pltpu.SemaphoreType.DMA((2, 2 * slots, 4)),
        ],
        compiler_params=pltpu.CompilerParams(vmem_limit_bytes=4 << 20),
        name="margins",
    )(me, above, below, *gathered_memory(gathered[0]), *gathered_memory(gathered[1]))


def split(value):
    high = value.astype(BF16)
    low = (value - high.astype(F32)).astype(BF16)
    return high, low


def pair(first, second):
    (h0, l0), (h1, l1) = split(first), split(second)
    return jnp.concatenate([h0, h1], axis=1), jnp.concatenate([l0, l1], axis=1)


def three_term(matrix, high, low):
    return dot(matrix, jnp.concatenate([high, low, high], axis=0))


STEPS = 2048.0


def encode(value, level):
    code = (jnp.log2(jnp.maximum(value, 1e-37)) - level) * STEPS
    return jnp.round(jnp.clip(code, -32767.0, 32767.0)).astype(I32)


def decode(code, level):
    return jnp.exp2(code.astype(I32).astype(F32) * (1.0 / STEPS) + level)


def dot(a, b):
    return jnp.dot(a, b, preferred_element_type=F32)


def job_kernel(channel, me, bricks, views, backdrops, logs, *refs):
    parts, refs = refs[:PARTS], refs[PARTS:]
    top_ref, bottom_ref, data_ref, mz_ref, mx_ref, my_ref, myt_ref, mxt_ref, mzt_ref, out_ref = refs[:10]
    blocks, seen_data, z_high, z_low, blurred_x, back_y, back_x, sems = refs[10:]
    slot, slots = pl.program_id(0), pl.num_programs(0)
    mid = pl.ds(RIM, PADS)

    def others(which_slot, buffer):
        span = pl.ds(0, WIN)
        return (
            (top_ref.at[which_slot], blocks.at[buffer, span, pl.ds(0, RIM)], sems.at[buffer, 3]),
            (bottom_ref.at[which_slot], blocks.at[buffer, span, pl.ds(RIM + PADS, RIM)], sems.at[buffer, 4]),
            (data_ref.at[which_slot, channel], seen_data.at[buffer], sems.at[buffer, 5]),
        )

    def fetch(which_slot, buffer):
        for which, (_, count, to) in enumerate(WINDOWS):
            target = blocks.at[buffer, pl.ds(to, count), mid]
            place = window_place(which, bricks[which_slot], me[0], channel == 0)
            copy_window(parts, which, place, pl.ds(0, PADS), target, sems.at[buffer, which])
        for source, target, sem in others(which_slot, buffer):
            pltpu.make_async_copy(source, target, sem).start()

    buffer = lax.rem(slot, 2)

    @pl.when(slot == 0)
    def _():
        fetch(0, 0)
        blurred_x[WIN * PW :] = jnp.zeros_like(blurred_x[WIN * PW :])
        back_y[WIN * PS :] = jnp.zeros_like(back_y[WIN * PS :])
        back_x[SIDE * PS :] = jnp.zeros_like(back_x[SIDE * PS :])

    @pl.when(slot + 1 < slots)
    def _():
        fetch(slot + 1, 1 - buffer)

    for which, (_, count, to) in enumerate(WINDOWS):
        target = blocks.at[buffer, pl.ds(to, count), mid]
        wait_window(parts, which, pl.ds(0, PADS), target, sems.at[buffer, which])
    for source, target, sem in others(slot, buffer):
        pltpu.make_async_copy(source, target, sem).wait()

    mz, mx, my = mz_ref[0], mx_ref[0], my_ref[0]
    myt, mxt, mzt = myt_ref[0], mxt_ref[0], mzt_ref[0]
    backdrop = backdrops[views[slot]]
    level = logs[views[slot]]

    def along_z(i, carry):
        start = i * CHUNK
        rows = blocks[buffer, pl.ds(start, CHUNK)].reshape(CHUNK * PADW, 128)
        in_z = dot(jnp.concatenate([rows, rows], axis=1), mz)
        high, low = split(in_z)
        z_high[pl.ds(start, CHUNK)] = high.reshape(CHUNK, PADW, 128)
        z_low[pl.ds(start, CHUNK)] = low.reshape(CHUNK, PADW, 128)
        return carry

    lax.fori_loop(0, -(-WIN // CHUNK), along_z, 0, unroll=UZ)

    def along_x_first(i, carry):
        y = 2 * i
        high = jnp.concatenate([z_high[y], z_high[y + 1]], axis=1)
        low = jnp.concatenate([z_low[y], z_low[y + 1]], axis=1)
        in_x = three_term(mx, high, low)
        start = pl.multiple_of(y * PW, 16)
        blurred_x[pl.ds(start, PADW), :] = in_x[:, :128]
        blurred_x[pl.ds(start + PW, PADW), :] = in_x[:, 128:]
        return carry

    lax.fori_loop(0, WIN // 2, along_x_first, 0, unroll=UNROLL)

    past = jnp.zeros((PADW - WIN, 256), F32)

    def along_y(i, carry):
        u = 2 * i
        lines = [blurred_x[pl.ds(u + j, PADW, stride=PW), :] for j in range(2)]
        predicted = three_term(my, *pair(*lines)) + backdrop
        seen = jnp.concatenate([seen_data[buffer, u], seen_data[buffer, u + 1]], axis=1)
        ratio = jnp.concatenate([seen.astype(F32) / predicted[:WIN], past], axis=0)
        in_y = three_term(myt, *pair(ratio[:, :128], ratio[:, 128:]))
        start = pl.multiple_of(u * PS, 16)
        back_y[pl.ds(start, PADS), :] = in_y[:, :128]
        back_y[pl.ds(start + PS, PADS), :] = in_y[:, 128:]
        return carry

    lax.fori_loop(0, WIN // 2, along_y, 0, unroll=UNROLL)

    def along_x(i, carry):
        y = 2 * i
        lines = [back_y[pl.ds(y + j, PADW, stride=PS), :] for j in range(2)]
        in_x = three_term(mxt, *pair(*lines))
        start = pl.multiple_of(y * PS, 16)
        back_x[pl.ds(start, PADS), :] = in_x[:, :128]
        back_x[pl.ds(start + PS, PADS), :] = in_x[:, 128:]
        return carry

    lax.fori_loop(0, SIDE // 2, along_x, 0, unroll=UNROLL)

    group = 4
    for i in range(SIDE // group):
        lines = [back_x[pl.ds(group * i + j, PADS, stride=PS), :] for j in range(group)]
        high, low = split(jnp.concatenate(lines, axis=0))
        factor = encode(dot(jnp.concatenate([high, low, high], axis=1), mzt), level)
        for j in range(0, group, 2):
            rows = [factor[k * PADS : k * PADS + SIDE] for k in (j, j + 1)]
            out_ref[(group * i + j) // 2, 0] = jnp.concatenate(rows, axis=0).astype(I16)
    for k in range(SIDE // 2, 16):
        out_ref[k, 0] = jnp.zeros_like(out_ref[k, 0])


UNROLL = 29
CHUNK = 29
PEXTRA = 8
SEXTRA = 8
PW = PADW + PEXTRA
PS = PADS + SEXTRA
UZ = 1


def run_jobs(channel, parts, scalars, top, bottom, view_data, mats):
    slots = mats[0].shape[0]
    hbm = pl.BlockSpec(memory_space=pltpu.HBM)
    smem = pl.BlockSpec(memory_space=pltpu.SMEM)
    specs = [smem] * len(scalars) + [hbm] * (len(parts) + 3)
    specs += [pl.BlockSpec((1,) + m.shape[1:], lambda slot: (slot, 0, 0)) for m in mats]
    return pl.pallas_call(
        functools.partial(job_kernel, channel),
        grid=(slots,),
        in_specs=specs,
        out_specs=pl.BlockSpec((16, 1, 2 * SIDE, 128), lambda slot: (0, slot, 0, 0)),
        scratch_shapes=[
            pltpu.VMEM((2, WIN, PADW, 128), BF16),
            pltpu.VMEM((2, WIN, WIN, 128), BF16),
            pltpu.VMEM((WIN, PADW, 128), BF16),
            pltpu.VMEM((WIN, PADW, 128), BF16),
            pltpu.VMEM((PADW * PW, 128), F32),
            pltpu.VMEM((PADW * PS, 128), F32),
            pltpu.VMEM((PADS * PS, 128), F32),
            pltpu.SemaphoreType.DMA((2, 6)),
        ],
        out_shape=pltpu.HBM((16, slots, 2 * SIDE, 128), I16),
        compiler_params=pltpu.CompilerParams(vmem_limit_bytes=18 << 20),
        cost_estimate=pl.CostEstimate(
            flops=slots * 20 * 128 * (WIN * PADW * (256 + 192 + 192 + 96) + 2 * SIDE * PADS * 192),
            transcendentals=slots * WIN * PADW * 128,
            bytes_accessed=slots * (2 * WIN * PADW * 128 * 2 + 16 * 2 * SIDE * 128 * 4),
        ),
        name="jobs",
    )(*scalars, *gathered_memory(parts), *far_memory(top, bottom, view_data, *mats))


def bands(taps, positions_out, positions_in):
    offsets = positions_in[None, :] - positions_out[:, None] + HALO
    sel = offsets[None, :, :, None] == jnp.arange(taps.shape[1])[None, None, None, :]
    return jnp.sum(jnp.where(sel, taps[:, None, None, :], 0.0), axis=3)


def high_low(matrix):
    high = lax.reduce_precision(matrix, 8, 7)
    return high.astype(BF16), (matrix - high).astype(BF16)


def job_matrices(taps, bricks):
    none = -1000
    far = 1000
    line = jnp.arange(128)
    row = jnp.arange(PADW)
    win_in = jnp.where(row < WIN, row, none)
    win_out = jnp.where(row < WIN, row, far)
    short = jnp.arange(PADS)
    inner_out = jnp.where(short < SIDE, short + HALO, far)
    x_in = jnp.where(row < RIM + 16, row - 1, row - 5)
    x_in = jnp.where((row >= RIM + 16) & (row < RIM + 20), none, x_in)
    x_in = jnp.where((x_in < 0) | (x_in >= WIN), none, x_in)
    inside = (row >= HALO)[None, :] | (bricks > 0)[:, None]
    inside &= (row < HALO + SIDE)[None, :] | (bricks < RING * RING - 1)[:, None]
    forward = lambda t, out, inp: bands(t, out, inp)
    backward = lambda t, out, inp: jnp.swapaxes(bands(t, inp, out), 1, 2)
    three = lambda pair: jnp.concatenate([pair[0], pair[0], pair[1]], axis=2)
    mz = high_low(jnp.swapaxes(forward(taps[:, 2], line, line), 1, 2))
    mzt = high_low(jnp.swapaxes(backward(taps[:, 2], line, line), 1, 2))
    win_in_far = jnp.where(row < WIN, row, far)
    inner_none = jnp.where(short < SIDE, short + HALO, none)
    return (
        jnp.concatenate(mz, axis=1),
        three(high_low(forward(taps[:, 0], win_out, x_in))),
        three(high_low(jnp.where(inside[:, None, :], forward(taps[:, 1], win_out, win_in), 0.0))),
        three(high_low(backward(taps[:, 1], inner_none, win_in_far))),
        three(high_low(backward(taps[:, 0], inner_none, win_in_far))),
        jnp.concatenate([mzt[0], mzt[0], mzt[1]], axis=1),
    )


MORE = 2.6


def add_kernel(owners, views, logs, *refs):
    total, level = refs[-2:]
    out_ref = refs[-3]
    workers, slots = refs[0].shape[:2]
    jobs = range(workers * slots)
    for b in range(workers):
        level[b] = -200.0
    for i in jobs:
        level[owners[i]] = jnp.maximum(level[owners[i]], logs[views[i]] + MORE)
    for channel, parts_ref in enumerate(refs[:-3]):
        total[...] = jnp.zeros_like(total)
        for i in jobs:
            total[owners[i]] += decode(parts_ref[i // slots, i % slots], logs[views[i]])
        for b in range(workers):
            out_ref[b, channel] = encode(total[b], level[b]).astype(I16)


def add_up(owners, views, logs, parts):
    vmem, smem = pl.BlockSpec(memory_space=pltpu.VMEM), pl.BlockSpec(memory_space=pltpu.SMEM)
    workers, rows = parts[0].shape[0], parts[0].shape[2:]
    return pl.pallas_call(
        add_kernel,
        in_specs=[smem] * 3 + [vmem] * len(parts),
        out_specs=vmem,
        out_shape=pltpu.HBM((workers, len(parts)) + rows, I16),
        scratch_shapes=[pltpu.VMEM((workers,) + rows, F32), pltpu.SMEM((workers,), F32)],
        compiler_params=pltpu.CompilerParams(vmem_limit_bytes=8 << 20),
        name="add_up",
    )(owners, views, logs, *parts)


def update_kernel(met, logs, est_ref, total, out_ref):
    seen, level = jnp.int32(0), jnp.float32(-200.0)
    for v in range(met.shape[0]):
        seen += met[v]
        level = jnp.where(met[v] > 0, jnp.maximum(level, logs[v] + MORE), level)
    seen = seen.astype(F32)
    for c in range(out_ref.shape[0]):
        for k in range(SIDE // 2):
            rows = decode(total[k, c], level)
            for j in range(2):
                part = rows[j * SIDE : (j + 1) * SIDE]
                out_ref[c, 2 * k + j] = est_ref[c, 2 * k + j] * part / seen


def update(met, logs, estimate, total):
    vmem, smem = pl.BlockSpec(memory_space=pltpu.VMEM), pl.BlockSpec(memory_space=pltpu.SMEM)
    return pl.pallas_call(
        update_kernel,
        in_specs=[smem, smem, vmem, vmem],
        out_specs=vmem,
        out_shape=jax.ShapeDtypeStruct(estimate.shape, F32),
        compiler_params=pltpu.CompilerParams(vmem_limit_bytes=12 << 20),
        name="update",
    )(met, logs, estimate, total)


def on_device(estimate, view_data, psf, background, slot_brick, slot_view, intersection):
    me = lax.axis_index("tile").astype(I32).reshape(1)
    groups, workers = lax.axis_size("view"), lax.axis_size("tile")
    upward = [(i, i + 1) for i in range(groups - 1)]
    downward = [(j, i) for i, j in upward]
    bricks, views = slot_brick[0, 0], slot_view[0, 0]
    slots = bricks.shape[0]

    wire = estimate.astype(BF16).transpose(0, 2, 1, 3)
    jobs = jnp.concatenate([bricks, views])
    note = jnp.pad(jobs.astype(BF16)[None, None], ((0, 0), (0, SIDE - 1), (0, 128 - 2 * slots)))
    note = jnp.broadcast_to(note, (wire.shape[0],) + note.shape[1:])
    wire = jnp.concatenate([wire[:, :, :RIM], note[:, :, None], wire[:, :, SIDE - RIM + 1 :]], axis=2)
    near, far = first_ring([wire[0], wire[1]], (0, 1))
    above = lax.ppermute(bricks, "view", downward)
    below = lax.ppermute(bricks, "view", upward)
    near, above, below = lax.optimization_barrier((near, above, below))
    halves = [
        (jnp.concatenate([wire[c], near[c][0]], axis=0), jnp.concatenate([near[c][1], *far[c]], axis=0))
        for c in range(2)
    ]
    halves, view_data, psf, views, bricks = lax.optimization_barrier(
        (halves, view_data, psf, views, bricks)
    )
    ahead, behind, far = second_ring(halves, (1, 0))

    chosen = views[:, None] == jnp.arange(psf.shape[0])[None, :]
    taps = jnp.sum(jnp.where(chosen[:, :, None, None], psf[None], 0.0), axis=1)
    mats = job_matrices(taps, bricks)
    data = view_data[0, 0]
    logs = jnp.log2(jnp.maximum(4.0 / background * jnp.prod(jnp.sum(psf, axis=2), axis=1), 1e-30)) - 15.9
    behind, mats, data, logs = lax.optimization_barrier((behind, mats, data, logs))
    gathered = [
        [*halves[c], ahead[c][0], behind[c][0], behind[c][1], ahead[c][1], *far[c]] for c in range(2)
    ]

    rims = margins(gathered, me, above, below)
    edges = [
        (lax.ppermute(rims[2 * c], "view", upward), lax.ppermute(rims[2 * c + 1], "view", downward))
        for c in range(2)
    ]
    notes = jnp.concatenate([p[::SIDE, RIM, : 2 * slots] for p in gathered[0]], axis=0)
    places = place_of(jnp.arange(workers, dtype=I32), me[0], True)
    match = places[:, None] == jnp.arange(workers)[None, :]
    notes = jnp.sum(jnp.where(match[:, :, None], notes.astype(F32)[None], 0.0), axis=1)
    notes = notes.astype(I32)
    owners, seen_by = notes[:, :slots].reshape(-1), notes[:, slots:].reshape(-1)

    parts = []
    scalars = (me, bricks, views, background, logs)
    for channel in range(2):
        factors = run_jobs(channel, gathered[channel], scalars, *edges[channel], data, mats)
        parts.append(lax.all_to_all(factors, "tile", 0, 0, tiled=True))
    total = lax.all_to_all(add_up(owners, seen_by, logs, parts), "tile", 0, 0, tiled=True)
    return update(intersection[0, 0], logs, estimate, total)


def solution(mesh):
    placed = (
        P(None, "view", "tile", None),
        P("view", "tile", None, None, None, None, None),
        P(),
        P(),
        P("view", "tile", None),
        P("view", "tile", None),
        P("view", "tile", None),
    )
    return jax.shard_map(
        on_device,
        mesh=mesh,
        in_specs=placed,
        out_specs=P(None, "view", "tile", None),
        check_vma=False,
    )
```

```python
import functools

import jax
import jax.numpy as jnp
from jax import lax
from jax.experimental import pallas as pl
from jax.experimental.pallas import tpu as pltpu
from jax.sharding import PartitionSpec as P

F32, BF16, I32, I16 = jnp.float32, jnp.bfloat16, jnp.int32, jnp.int16
HALO = 15
SIDE = 28
WIN = SIDE + 2 * HALO
PADW = 64
PADS = 32
RIM = 16
RING = 4


def far_memory(*arrays):
    return [pltpu.with_memory_space_constraint(a, pltpu.HBM) for a in arrays]


def gathered_memory(parts):
    return [parts[0]] + far_memory(*parts[1:])


def torus_step(array, dx, dy):
    pairs = [
        (x * RING + y, ((x + dx) % RING) * RING + (y + dy) % RING)
        for x in range(RING)
        for y in range(RING)
    ]
    return lax.ppermute(array, "tile", pairs)


def along(axis, step):
    return (step, 0) if axis == 0 else (0, step)


def ring_near(arrays, axes):
    return [
        [a, torus_step(a, *along(ax, 1)), torus_step(a, *along(ax, -1))]
        for a, ax in zip(arrays, axes)
    ]


def halves_kernel(*refs):
    stage, sems, refs = refs[-2], refs[-1], refs[:-2]
    count = len(refs) // 2
    ins, outs = [], []
    for i in range(count):
        half = refs[i].shape[0] // 2
        source = refs[i].at[pl.ds(0 if i % 2 == 0 else half, half)]
        ins.append(pltpu.make_async_copy(source, stage.at[i], sems.at[i, 0]))
        outs.append(pltpu.make_async_copy(stage.at[i], refs[count + i], sems.at[i, 1]))
        ins[i].start()
    for i in range(count):
        ins[i].wait()
        outs[i].start()
    for i in range(count):
        outs[i].wait()


def take_halves(near):
    arrays = [a for _, lower, upper in near for a in (lower, upper)]
    anywhere = pl.BlockSpec(memory_space=pl.ANY)
    shape = arrays[0].shape
    taken = pl.pallas_call(
        halves_kernel,
        in_specs=[anywhere] * len(arrays),
        out_specs=[anywhere] * len(arrays),
        out_shape=[pltpu.HBM((shape[0] // 2,) + shape[1:], BF16)] * len(arrays),
        scratch_shapes=[
            pltpu.VMEM((len(arrays), shape[0] // 2) + shape[1:], BF16),
            pltpu.SemaphoreType.DMA((len(arrays), 2)),
        ],
        compiler_params=pltpu.CompilerParams(vmem_limit_bytes=4 << 20),
        name="halves",
    )(*arrays)
    return [(taken[2 * i], taken[2 * i + 1]) for i in range(len(near))]


def ring_pass_on(near, axes):
    return [
        [*n, torus_step(low, *along(ax, 1)), torus_step(high, *along(ax, -1))]
        for n, (low, high), ax in zip(near, take_halves(near), axes)
    ]


def ring_far(near, axes):
    result = []
    for (own, lower, upper), ax in zip(near, axes):
        half = lower.shape[0] // 2
        far = [torus_step(lower[:half], *along(ax, 1)), torus_step(upper[half:], *along(ax, -1))]
        result.append([own, lower, upper, *far])
    return result


def rank(delta):
    delta = lax.rem(delta + RING, RING)
    return jnp.where(delta == 3, 1, jnp.where(delta == 1, 2, jnp.where(delta == 2, 3, 0)))


def place_of(brick, me, x_first):
    in_x = rank(lax.div(brick, RING) - lax.div(me, RING))
    in_y = rank(lax.rem(brick, RING) - lax.rem(me, RING))
    return in_y * RING + in_x if x_first else in_x * RING + in_y


def window_place(which, brick, me, x_first):
    return place_of(jnp.clip(brick + which - 1, 0, RING * RING - 1), me, x_first)


WINDOWS = ((SIDE - HALO, HALO, 0), (0, SIDE, HALO), (0, HALO, HALO + SIDE))


def copy_window(parts, which, place, rows, target, sem):
    first, count, _ = WINDOWS[which]
    base = 0
    for part in parts:
        held = part.shape[0] // SIDE

        @pl.when((place >= base) & (place < base + held))
        def _(part=part, base=base):
            source = part.at[pl.ds((place - base) * SIDE + first, count), rows]
            pltpu.make_async_copy(source, target, sem).start()

        base += held


def wait_window(parts, which, rows, target, sem):
    count = WINDOWS[which][1]
    pltpu.make_async_copy(parts[0].at[pl.ds(0, count), rows], target, sem).wait()


def margin_kernel(*refs):
    me, *asked = refs[:3]
    refs = refs[3:]
    refs, (stage, sems) = refs[:-2], refs[-2:]
    gathered, outs = (refs[:PARTS], refs[PARTS : 2 * PARTS]), refs[2 * PARTS :]
    slots = outs[0].shape[0]
    copies = []
    for channel, parts in enumerate(gathered):
        for side in range(2):
            rows = pl.ds(RIM, RIM) if side == 0 else pl.ds(0, RIM)
            for slot in range(slots):
                item = side * slots + slot
                waits = []
                for which, (_, count, to) in enumerate(WINDOWS):
                    target = stage.at[channel, item, pl.ds(to, count)]
                    sem = sems.at[channel, item, which]
                    place = window_place(which, asked[side][slot], me[0], channel == 0)
                    copy_window(parts, which, place, rows, target, sem)
                    waits.append((parts, which, rows, target, sem))
                out = pltpu.make_async_copy(
                    stage.at[channel, item],
                    outs[2 * channel + side].at[slot],
                    sems.at[channel, item, 3],
                )
                copies.append((waits, out))
    for waits, out in copies:
        for item in waits:
            wait_window(*item)
        out.start()
    for _, out in copies:
        out.wait()


PARTS = 5


def margins(gathered, me, above, below):
    slots = above.shape[0]
    hbm, smem = pl.BlockSpec(memory_space=pltpu.HBM), pl.BlockSpec(memory_space=pltpu.SMEM)
    return pl.pallas_call(
        margin_kernel,
        in_specs=[smem] * 3 + [hbm] * (2 * PARTS),
        out_specs=[hbm] * 4,
        out_shape=[pltpu.HBM((slots, WIN, RIM, 128), BF16)] * 4,
        scratch_shapes=[
            pltpu.VMEM((2, 2 * slots, WIN, RIM, 128), BF16),
            pltpu.SemaphoreType.DMA((2, 2 * slots, 4)),
        ],
        compiler_params=pltpu.CompilerParams(vmem_limit_bytes=4 << 20),
        name="margins",
    )(me, above, below, *gathered_memory(gathered[0]), *gathered_memory(gathered[1]))


def split(value):
    high = value.astype(BF16)
    low = (value - high.astype(F32)).astype(BF16)
    return high, low


def pair(first, second):
    (h0, l0), (h1, l1) = split(first), split(second)
    return jnp.concatenate([h0, h1], axis=1), jnp.concatenate([l0, l1], axis=1)


def three_term(matrix, high, low):
    return dot(matrix, jnp.concatenate([high, low, high], axis=0))


STEPS = 2048.0


def encode(value, level):
    code = (jnp.log2(jnp.maximum(value, 1e-37)) - level) * STEPS
    return jnp.round(jnp.clip(code, -32767.0, 32767.0)).astype(I32)


def decode(code, level):
    return jnp.exp2(code.astype(I32).astype(F32) * (1.0 / STEPS) + level)


def dot(a, b):
    return jnp.dot(a, b, preferred_element_type=F32)


def job_kernel(channel, me, bricks, views, backdrops, logs, *refs):
    parts, refs = refs[:PARTS], refs[PARTS:]
    top_ref, bottom_ref, data_ref, mz_ref, mx_ref, my_ref, myt_ref, mxt_ref, mzt_ref, out_ref = refs[:10]
    blocks, seen_data, z_high, z_low, blurred_x, back_y, back_x, sems = refs[10:]
    slot, slots = pl.program_id(0), pl.num_programs(0)
    mid = pl.ds(RIM, PADS)

    def others(which_slot, buffer):
        span = pl.ds(0, WIN)
        return (
            (top_ref.at[which_slot], blocks.at[buffer, span, pl.ds(0, RIM)], sems.at[buffer, 3]),
            (bottom_ref.at[which_slot], blocks.at[buffer, span, pl.ds(RIM + PADS, RIM)], sems.at[buffer, 4]),
            (data_ref.at[which_slot, channel], seen_data.at[buffer], sems.at[buffer, 5]),
        )

    def fetch(which_slot, buffer):
        for which, (_, count, to) in enumerate(WINDOWS):
            target = blocks.at[buffer, pl.ds(to, count), mid]
            place = window_place(which, bricks[which_slot], me[0], channel == 0)
            copy_window(parts, which, place, pl.ds(0, PADS), target, sems.at[buffer, which])
        for source, target, sem in others(which_slot, buffer):
            pltpu.make_async_copy(source, target, sem).start()

    buffer = lax.rem(slot, 2)

    @pl.when(slot == 0)
    def _():
        fetch(0, 0)
        blurred_x[WIN * PW :] = jnp.zeros_like(blurred_x[WIN * PW :])
        back_y[WIN * PS :] = jnp.zeros_like(back_y[WIN * PS :])
        back_x[SIDE * PS :] = jnp.zeros_like(back_x[SIDE * PS :])

    @pl.when(slot + 1 < slots)
    def _():
        fetch(slot + 1, 1 - buffer)

    for which, (_, count, to) in enumerate(WINDOWS):
        target = blocks.at[buffer, pl.ds(to, count), mid]
        wait_window(parts, which, pl.ds(0, PADS), target, sems.at[buffer, which])
    for source, target, sem in others(slot, buffer):
        pltpu.make_async_copy(source, target, sem).wait()

    mz, mx, my = mz_ref[0], mx_ref[0], my_ref[0]
    myt, mxt, mzt = myt_ref[0], mxt_ref[0], mzt_ref[0]
    backdrop = backdrops[views[slot]]
    level = logs[views[slot]]

    def along_z(i, carry):
        start = i * CHUNK
        rows = blocks[buffer, pl.ds(start, CHUNK)].reshape(CHUNK * PADW, 128)
        in_z = dot(jnp.concatenate([rows, rows], axis=1), mz)
        high, low = split(in_z)
        z_high[pl.ds(start, CHUNK)] = high.reshape(CHUNK, PADW, 128)
        z_low[pl.ds(start, CHUNK)] = low.reshape(CHUNK, PADW, 128)
        return carry

    lax.fori_loop(0, -(-WIN // CHUNK), along_z, 0, unroll=UZ)

    def along_x_first(i, carry):
        y = 2 * i
        high = jnp.concatenate([z_high[y], z_high[y + 1]], axis=1)
        low = jnp.concatenate([z_low[y], z_low[y + 1]], axis=1)
        in_x = three_term(mx, high, low)
        start = pl.multiple_of(y * PW, 16)
        blurred_x[pl.ds(start, PADW), :] = in_x[:, :128]
        blurred_x[pl.ds(start + PW, PADW), :] = in_x[:, 128:]
        return carry

    lax.fori_loop(0, WIN // 2, along_x_first, 0, unroll=UNROLL)

    past = jnp.zeros((PADW - WIN, 256), F32)

    def along_y(i, carry):
        u = 2 * i
        lines = [blurred_x[pl.ds(u + j, PADW, stride=PW), :] for j in range(2)]
        predicted = three_term(my, *pair(*lines)) + backdrop
        seen = jnp.concatenate([seen_data[buffer, u], seen_data[buffer, u + 1]], axis=1)
        ratio = jnp.concatenate([seen.astype(F32) / predicted[:WIN], past], axis=0)
        in_y = three_term(myt, *pair(ratio[:, :128], ratio[:, 128:]))
        start = pl.multiple_of(u * PS, 16)
        back_y[pl.ds(start, PADS), :] = in_y[:, :128]
        back_y[pl.ds(start + PS, PADS), :] = in_y[:, 128:]
        return carry

    lax.fori_loop(0, WIN // 2, along_y, 0, unroll=UNROLL)

    def along_x(i, carry):
        y = 2 * i
        lines = [back_y[pl.ds(y + j, PADW, stride=PS), :] for j in range(2)]
        in_x = three_term(mxt, *pair(*lines))
        start = pl.multiple_of(y * PS, 16)
        back_x[pl.ds(start, PADS), :] = in_x[:, :128]
        back_x[pl.ds(start + PS, PADS), :] = in_x[:, 128:]
        return carry

    lax.fori_loop(0, SIDE // 2, along_x, 0, unroll=UNROLL)

    group = 4
    for i in range(SIDE // group):
        lines = [back_x[pl.ds(group * i + j, PADS, stride=PS), :] for j in range(group)]
        high, low = split(jnp.concatenate(lines, axis=0))
        factor = encode(dot(jnp.concatenate([high, low, high], axis=1), mzt), level)
        for j in range(0, group, 2):
            rows = [factor[k * PADS : k * PADS + SIDE] for k in (j, j + 1)]
            out_ref[(group * i + j) // 2, 0] = jnp.concatenate(rows, axis=0).astype(I16)
    for k in range(SIDE // 2, 16):
        out_ref[k, 0] = jnp.zeros_like(out_ref[k, 0])


UNROLL = 29
CHUNK = 29
PEXTRA = 8
SEXTRA = 8
PW = PADW + PEXTRA
PS = PADS + SEXTRA
UZ = 1


def run_jobs(channel, parts, scalars, top, bottom, view_data, mats):
    slots = mats[0].shape[0]
    hbm = pl.BlockSpec(memory_space=pltpu.HBM)
    smem = pl.BlockSpec(memory_space=pltpu.SMEM)
    specs = [smem] * len(scalars) + [hbm] * (len(parts) + 3)
    specs += [pl.BlockSpec((1,) + m.shape[1:], lambda slot: (slot, 0, 0)) for m in mats]
    return pl.pallas_call(
        functools.partial(job_kernel, channel),
        grid=(slots,),
        in_specs=specs,
        out_specs=pl.BlockSpec((16, 1, 2 * SIDE, 128), lambda slot: (0, slot, 0, 0)),
        scratch_shapes=[
            pltpu.VMEM((2, WIN, PADW, 128), BF16),
            pltpu.VMEM((2, WIN, WIN, 128), BF16),
            pltpu.VMEM((WIN, PADW, 128), BF16),
            pltpu.VMEM((WIN, PADW, 128), BF16),
            pltpu.VMEM((PADW * PW, 128), F32),
            pltpu.VMEM((PADW * PS, 128), F32),
            pltpu.VMEM((PADS * PS, 128), F32),
            pltpu.SemaphoreType.DMA((2, 6)),
        ],
        out_shape=pltpu.HBM((16, slots, 2 * SIDE, 128), I16),
        compiler_params=pltpu.CompilerParams(vmem_limit_bytes=18 << 20),
        cost_estimate=pl.CostEstimate(
            flops=slots * 20 * 128 * (WIN * PADW * (256 + 192 + 192 + 96) + 2 * SIDE * PADS * 192),
            transcendentals=slots * WIN * PADW * 128,
            bytes_accessed=slots * (2 * WIN * PADW * 128 * 2 + 16 * 2 * SIDE * 128 * 4),
        ),
        name="jobs",
    )(*scalars, *gathered_memory(parts), *far_memory(top, bottom, view_data, *mats))


def bands(taps, positions_out, positions_in):
    offsets = positions_in[None, :] - positions_out[:, None] + HALO
    sel = offsets[None, :, :, None] == jnp.arange(taps.shape[1])[None, None, None, :]
    return jnp.sum(jnp.where(sel, taps[:, None, None, :], 0.0), axis=3)


def high_low(matrix):
    high = lax.reduce_precision(matrix, 8, 7)
    return high.astype(BF16), (matrix - high).astype(BF16)


def job_matrices(taps, bricks):
    none = -1000
    far = 1000
    line = jnp.arange(128)
    row = jnp.arange(PADW)
    win_in = jnp.where(row < WIN, row, none)
    win_out = jnp.where(row < WIN, row, far)
    short = jnp.arange(PADS)
    inner_out = jnp.where(short < SIDE, short + HALO, far)
    x_in = jnp.where(row < RIM + 16, row - 1, row - 5)
    x_in = jnp.where((row >= RIM + 16) & (row < RIM + 20), none, x_in)
    x_in = jnp.where((x_in < 0) | (x_in >= WIN), none, x_in)
    inside = (row >= HALO)[None, :] | (bricks > 0)[:, None]
    inside &= (row < HALO + SIDE)[None, :] | (bricks < RING * RING - 1)[:, None]
    forward = lambda t, out, inp: bands(t, out, inp)
    backward = lambda t, out, inp: jnp.swapaxes(bands(t, inp, out), 1, 2)
    three = lambda pair: jnp.concatenate([pair[0], pair[0], pair[1]], axis=2)
    mz = high_low(jnp.swapaxes(forward(taps[:, 2], line, line), 1, 2))
    mzt = high_low(jnp.swapaxes(backward(taps[:, 2], line, line), 1, 2))
    win_in_far = jnp.where(row < WIN, row, far)
    inner_none = jnp.where(short < SIDE, short + HALO, none)
    return (
        jnp.concatenate(mz, axis=1),
        three(high_low(forward(taps[:, 0], win_out, x_in))),
        three(high_low(jnp.where(inside[:, None, :], forward(taps[:, 1], win_out, win_in), 0.0))),
        three(high_low(backward(taps[:, 1], inner_none, win_in_far))),
        three(high_low(backward(taps[:, 0], inner_none, win_in_far))),
        jnp.concatenate([mzt[0], mzt[0], mzt[1]], axis=1),
    )


MORE = 2.6


def add_kernel(owners, views, logs, *refs):
    total, level = refs[-2:]
    out_ref = refs[-3]
    workers, slots = refs[0].shape[:2]
    jobs = range(workers * slots)
    for b in range(workers):
        level[b] = -200.0
    for i in jobs:
        level[owners[i]] = jnp.maximum(level[owners[i]], logs[views[i]] + MORE)
    for channel, parts_ref in enumerate(refs[:-3]):
        total[...] = jnp.zeros_like(total)
        for i in jobs:
            total[owners[i]] += decode(parts_ref[i // slots, i % slots], logs[views[i]])
        for b in range(workers):
            out_ref[b, channel] = encode(total[b], level[b]).astype(I16)


def add_up(owners, views, logs, parts):
    vmem, smem = pl.BlockSpec(memory_space=pltpu.VMEM), pl.BlockSpec(memory_space=pltpu.SMEM)
    workers, rows = parts[0].shape[0], parts[0].shape[2:]
    return pl.pallas_call(
        add_kernel,
        in_specs=[smem] * 3 + [vmem] * len(parts),
        out_specs=vmem,
        out_shape=pltpu.HBM((workers, len(parts)) + rows, I16),
        scratch_shapes=[pltpu.VMEM((workers,) + rows, F32), pltpu.SMEM((workers,), F32)],
        compiler_params=pltpu.CompilerParams(vmem_limit_bytes=8 << 20),
        name="add_up",
    )(owners, views, logs, *parts)


def update_kernel(met, logs, est_ref, total, out_ref):
    seen, level = jnp.int32(0), jnp.float32(-200.0)
    for v in range(met.shape[0]):
        seen += met[v]
        level = jnp.where(met[v] > 0, jnp.maximum(level, logs[v] + MORE), level)
    seen = seen.astype(F32)
    for c in range(out_ref.shape[0]):
        for k in range(SIDE // 2):
            rows = decode(total[k, c], level)
            for j in range(2):
                part = rows[j * SIDE : (j + 1) * SIDE]
                out_ref[c, 2 * k + j] = est_ref[c, 2 * k + j] * part / seen


def update(met, logs, estimate, total):
    vmem, smem = pl.BlockSpec(memory_space=pltpu.VMEM), pl.BlockSpec(memory_space=pltpu.SMEM)
    return pl.pallas_call(
        update_kernel,
        in_specs=[smem, smem, vmem, vmem],
        out_specs=vmem,
        out_shape=jax.ShapeDtypeStruct(estimate.shape, F32),
        compiler_params=pltpu.CompilerParams(vmem_limit_bytes=12 << 20),
        name="update",
    )(met, logs, estimate, total)


def on_device(estimate, view_data, psf, background, slot_brick, slot_view, intersection):
    me = lax.axis_index("tile").astype(I32).reshape(1)
    groups, workers = lax.axis_size("view"), lax.axis_size("tile")
    upward = [(i, i + 1) for i in range(groups - 1)]
    downward = [(j, i) for i, j in upward]
    bricks, views = slot_brick[0, 0], slot_view[0, 0]
    slots = bricks.shape[0]

    wire = estimate.astype(BF16).transpose(0, 2, 1, 3)
    jobs = jnp.concatenate([bricks, views])
    note = jnp.pad(jobs.astype(BF16)[None, None], ((0, 0), (0, SIDE - 1), (0, 128 - 2 * slots)))
    note = jnp.broadcast_to(note, (wire.shape[0],) + note.shape[1:])
    wire = jnp.concatenate([wire[:, :, :RIM], note[:, :, None], wire[:, :, SIDE - RIM + 1 :]], axis=2)
    near = ring_near([wire[0], wire[1]], (0, 1))
    above = lax.ppermute(bricks, "view", downward)
    below = lax.ppermute(bricks, "view", upward)
    near, above, below = lax.optimization_barrier((near, above, below))
    rings = [jnp.concatenate(parts, axis=0) for parts in ring_far(near, (0, 1))]
    rings, view_data, psf, views, bricks = lax.optimization_barrier(
        (rings, view_data, psf, views, bricks)
    )
    near = ring_near(rings, (1, 0))

    chosen = views[:, None] == jnp.arange(psf.shape[0])[None, :]
    taps = jnp.sum(jnp.where(chosen[:, :, None, None], psf[None], 0.0), axis=1)
    mats = job_matrices(taps, bricks)
    data = view_data[0, 0]
    logs = jnp.log2(jnp.maximum(4.0 / background * jnp.prod(jnp.sum(psf, axis=2), axis=1), 1e-30)) - 15.9
    near, mats, data, logs = lax.optimization_barrier((near, mats, data, logs))
    gathered = ring_pass_on(near, (1, 0))

    rims = margins(gathered, me, above, below)
    edges = [
        (lax.ppermute(rims[2 * c], "view", upward), lax.ppermute(rims[2 * c + 1], "view", downward))
        for c in range(2)
    ]
    notes = jnp.concatenate([p[::SIDE, RIM, : 2 * slots] for p in gathered[0]], axis=0)
    places = place_of(jnp.arange(workers, dtype=I32), me[0], True)
    match = places[:, None] == jnp.arange(workers)[None, :]
    notes = jnp.sum(jnp.where(match[:, :, None], notes.astype(F32)[None], 0.0), axis=1)
    notes = notes.astype(I32)
    owners, seen_by = notes[:, :slots].reshape(-1), notes[:, slots:].reshape(-1)

    parts = []
    scalars = (me, bricks, views, background, logs)
    for channel in range(2):
        factors = run_jobs(channel, gathered[channel], scalars, *edges[channel], data, mats)
        parts.append(lax.all_to_all(factors, "tile", 0, 0, tiled=True))
    total = lax.all_to_all(add_up(owners, seen_by, logs, parts), "tile", 0, 0, tiled=True)
    return update(intersection[0, 0], logs, estimate, total)


def solution(mesh):
    placed = (
        P(None, "view", "tile", None),
        P("view", "tile", None, None, None, None, None),
        P(),
        P(),
        P("view", "tile", None),
        P("view", "tile", None),
        P("view", "tile", None),
    )
    return jax.shard_map(
        on_device,
        mesh=mesh,
        in_specs=placed,
        out_specs=P(None, "view", "tile", None),
        check_vma=False,
    )
```

```python
import functools

import jax
import jax.numpy as jnp
from jax import lax
from jax.experimental import pallas as pl
from jax.experimental.pallas import tpu as pltpu
from jax.sharding import PartitionSpec as P

F32, BF16, I32, I16 = jnp.float32, jnp.bfloat16, jnp.int32, jnp.int16
HALO = 15
SIDE = 28
WIN = SIDE + 2 * HALO
PADW = 64
PADS = 32
RIM = 16
RING = 4


def far_memory(*arrays):
    return [pltpu.with_memory_space_constraint(a, pltpu.HBM) for a in arrays]


def gathered_memory(parts):
    return far_memory(*parts)


def torus_step(array, dx, dy):
    pairs = [
        (x * RING + y, ((x + dx) % RING) * RING + (y + dy) % RING)
        for x in range(RING)
        for y in range(RING)
    ]
    return lax.ppermute(array, "tile", pairs)


def along(axis, step):
    return (step, 0) if axis == 0 else (0, step)


def ring_near(arrays, axes):
    return [
        [a, torus_step(a, *along(ax, 1)), torus_step(a, *along(ax, -1))]
        for a, ax in zip(arrays, axes)
    ]


def ring_whole(arrays, axes):
    return [
        [a] + [torus_step(a, *along(ax, d)) for d in (1, -1, 2)] for a, ax in zip(arrays, axes)
    ]


def join_kernel(*refs):
    stage, sems, refs = refs[-2], refs[-1], refs[:-2]
    outs, refs = refs[-2:], refs[:-2]
    each = len(refs) // len(outs)
    rows = refs[0].shape[0]
    ins = []
    for i, ref in enumerate(refs):
        target = stage.at[i // each, pl.ds(i % each * rows, rows)]
        ins.append(pltpu.make_async_copy(ref, target, sems.at[i]))
        ins[i].start()
    sends = []
    for i, out in enumerate(outs):
        for copy in ins[i * each : (i + 1) * each]:
            copy.wait()
        sends.append(pltpu.make_async_copy(stage.at[i], out, sems.at[len(refs) + i]))
        sends[i].start()
    for send in sends:
        send.wait()


def join(rings):
    arrays = [a for ring in rings for a in ring]
    whole = (len(rings[0]) * arrays[0].shape[0],) + arrays[0].shape[1:]
    return pl.pallas_call(
        join_kernel,
        in_specs=[pl.BlockSpec(memory_space=pl.ANY)] * len(arrays),
        out_specs=[pl.BlockSpec(memory_space=pltpu.HBM)] * len(rings),
        out_shape=[pltpu.HBM(whole, BF16)] * len(rings),
        scratch_shapes=[
            pltpu.VMEM((len(rings),) + whole, BF16),
            pltpu.SemaphoreType.DMA((len(arrays) + len(rings),)),
        ],
        compiler_params=pltpu.CompilerParams(vmem_limit_bytes=4 << 20),
        name="join",
    )(*arrays)


def halves_kernel(*refs):
    stage, sems, refs = refs[-2], refs[-1], refs[:-2]
    count = len(refs) // 2
    ins, outs = [], []
    for i in range(count):
        half = refs[i].shape[0] // 2
        source = refs[i].at[pl.ds(0 if i % 2 == 0 else half, half)]
        ins.append(pltpu.make_async_copy(source, stage.at[i], sems.at[i, 0]))
        outs.append(pltpu.make_async_copy(stage.at[i], refs[count + i], sems.at[i, 1]))
        ins[i].start()
    for i in range(count):
        ins[i].wait()
        outs[i].start()
    for i in range(count):
        outs[i].wait()


def take_halves(near):
    arrays = [a for _, lower, upper in near for a in (lower, upper)]
    anywhere = pl.BlockSpec(memory_space=pl.ANY)
    shape = arrays[0].shape
    taken = pl.pallas_call(
        halves_kernel,
        in_specs=[anywhere] * len(arrays),
        out_specs=[anywhere] * len(arrays),
        out_shape=[pltpu.HBM((shape[0] // 2,) + shape[1:], BF16)] * len(arrays),
        scratch_shapes=[
            pltpu.VMEM((len(arrays), shape[0] // 2) + shape[1:], BF16),
            pltpu.SemaphoreType.DMA((len(arrays), 2)),
        ],
        compiler_params=pltpu.CompilerParams(vmem_limit_bytes=4 << 20),
        name="halves",
    )(*arrays)
    return [(taken[2 * i], taken[2 * i + 1]) for i in range(len(near))]


def ring_pass_on(near, axes):
    return [
        [*n, torus_step(low, *along(ax, 1)), torus_step(high, *along(ax, -1))]
        for n, (low, high), ax in zip(near, take_halves(near), axes)
    ]


def rank(delta):
    delta = lax.rem(delta + RING, RING)
    return jnp.where(delta == 3, 1, jnp.where(delta == 1, 2, jnp.where(delta == 2, 3, 0)))


def place_of(brick, me, x_first):
    in_x = rank(lax.div(brick, RING) - lax.div(me, RING))
    in_y = rank(lax.rem(brick, RING) - lax.rem(me, RING))
    return in_y * RING + in_x if x_first else in_x * RING + in_y


def window_place(which, brick, me, x_first):
    return place_of(jnp.clip(brick + which - 1, 0, RING * RING - 1), me, x_first)


WINDOWS = ((SIDE - HALO, HALO, 0), (0, SIDE, HALO), (0, HALO, HALO + SIDE))


def copy_window(parts, which, place, rows, target, sem):
    first, count, _ = WINDOWS[which]
    base = 0
    for part in parts:
        held = part.shape[0] // SIDE

        @pl.when((place >= base) & (place < base + held))
        def _(part=part, base=base):
            source = part.at[pl.ds((place - base) * SIDE + first, count), rows]
            pltpu.make_async_copy(source, target, sem).start()

        base += held


def wait_window(parts, which, rows, target, sem):
    count = WINDOWS[which][1]
    pltpu.make_async_copy(parts[0].at[pl.ds(0, count), rows], target, sem).wait()


def margin_kernel(*refs):
    me, *asked = refs[:3]
    refs = refs[3:]
    refs, (stage, sems) = refs[:-2], refs[-2:]
    gathered, outs = (refs[:PARTS], refs[PARTS : 2 * PARTS]), refs[2 * PARTS :]
    slots = outs[0].shape[0]
    copies = []
    for channel, parts in enumerate(gathered):
        for side in range(2):
            rows = pl.ds(RIM, RIM) if side == 0 else pl.ds(0, RIM)
            for slot in range(slots):
                item = side * slots + slot
                waits = []
                for which, (_, count, to) in enumerate(WINDOWS):
                    target = stage.at[channel, item, pl.ds(to, count)]
                    sem = sems.at[channel, item, which]
                    place = window_place(which, asked[side][slot], me[0], channel == 0)
                    copy_window(parts, which, place, rows, target, sem)
                    waits.append((parts, which, rows, target, sem))
                out = pltpu.make_async_copy(
                    stage.at[channel, item],
                    outs[2 * channel + side].at[slot],
                    sems.at[channel, item, 3],
                )
                copies.append((waits, out))
    for waits, out in copies:
        for item in waits:
            wait_window(*item)
        out.start()
    for _, out in copies:
        out.wait()


PARTS = 5


def margins(gathered, me, above, below):
    slots = above.shape[0]
    hbm, smem = pl.BlockSpec(memory_space=pltpu.HBM), pl.BlockSpec(memory_space=pltpu.SMEM)
    return pl.pallas_call(
        margin_kernel,
        in_specs=[smem] * 3 + [hbm] * (2 * PARTS),
        out_specs=[hbm] * 4,
        out_shape=[pltpu.HBM((slots, WIN, RIM, 128), BF16)] * 4,
        scratch_shapes=[
            pltpu.VMEM((2, 2 * slots, WIN, RIM, 128), BF16),
            pltpu.SemaphoreType.DMA((2, 2 * slots, 4)),
        ],
        compiler_params=pltpu.CompilerParams(vmem_limit_bytes=4 << 20),
        name="margins",
    )(me, above, below, *gathered_memory(gathered[0]), *gathered_memory(gathered[1]))


def split(value):
    high = value.astype(BF16)
    low = (value - high.astype(F32)).astype(BF16)
    return high, low


def pair(first, second):
    (h0, l0), (h1, l1) = split(first), split(second)
    return jnp.concatenate([h0, h1], axis=1), jnp.concatenate([l0, l1], axis=1)


def three_term(matrix, high, low):
    return dot(matrix, jnp.concatenate([high, low, high], axis=0))


STEPS = 2048.0


def encode(value, level):
    code = (jnp.log2(jnp.maximum(value, 1e-37)) - level) * STEPS
    return jnp.round(jnp.clip(code, -32767.0, 32767.0)).astype(I32)


def decode(code, level):
    return jnp.exp2(code.astype(I32).astype(F32) * (1.0 / STEPS) + level)


def dot(a, b):
    return jnp.dot(a, b, preferred_element_type=F32)


def job_kernel(channel, me, bricks, views, backdrops, logs, *refs):
    parts, refs = refs[:PARTS], refs[PARTS:]
    top_ref, bottom_ref, data_ref, mz_ref, mx_ref, my_ref, myt_ref, mxt_ref, mzt_ref, out_ref = refs[:10]
    blocks, seen_data, z_high, z_low, blurred_x, back_y, back_x, sems = refs[10:]
    slot, slots = pl.program_id(0), pl.num_programs(0)
    mid = pl.ds(RIM, PADS)

    def others(which_slot, buffer):
        span = pl.ds(0, WIN)
        return (
            (top_ref.at[which_slot], blocks.at[buffer, span, pl.ds(0, RIM)], sems.at[buffer, 3]),
            (bottom_ref.at[which_slot], blocks.at[buffer, span, pl.ds(RIM + PADS, RIM)], sems.at[buffer, 4]),
            (data_ref.at[which_slot, channel], seen_data.at[buffer], sems.at[buffer, 5]),
        )

    def fetch(which_slot, buffer):
        for which, (_, count, to) in enumerate(WINDOWS):
            target = blocks.at[buffer, pl.ds(to, count), mid]
            place = window_place(which, bricks[which_slot], me[0], channel == 0)
            copy_window(parts, which, place, pl.ds(0, PADS), target, sems.at[buffer, which])
        for source, target, sem in others(which_slot, buffer):
            pltpu.make_async_copy(source, target, sem).start()

    buffer = lax.rem(slot, 2)

    @pl.when(slot == 0)
    def _():
        fetch(0, 0)
        blurred_x[WIN * PW :] = jnp.zeros_like(blurred_x[WIN * PW :])
        back_y[WIN * PS :] = jnp.zeros_like(back_y[WIN * PS :])
        back_x[SIDE * PS :] = jnp.zeros_like(back_x[SIDE * PS :])

    @pl.when(slot + 1 < slots)
    def _():
        fetch(slot + 1, 1 - buffer)

    for which, (_, count, to) in enumerate(WINDOWS):
        target = blocks.at[buffer, pl.ds(to, count), mid]
        wait_window(parts, which, pl.ds(0, PADS), target, sems.at[buffer, which])
    for source, target, sem in others(slot, buffer):
        pltpu.make_async_copy(source, target, sem).wait()

    mz, mx, my = mz_ref[0], mx_ref[0], my_ref[0]
    myt, mxt, mzt = myt_ref[0], mxt_ref[0], mzt_ref[0]
    backdrop = backdrops[views[slot]]
    level = logs[views[slot]]

    def along_z(i, carry):
        start = i * CHUNK
        rows = blocks[buffer, pl.ds(start, CHUNK)].reshape(CHUNK * PADW, 128)
        in_z = dot(jnp.concatenate([rows, rows], axis=1), mz)
        high, low = split(in_z)
        z_high[pl.ds(start, CHUNK)] = high.reshape(CHUNK, PADW, 128)
        z_low[pl.ds(start, CHUNK)] = low.reshape(CHUNK, PADW, 128)
        return carry

    lax.fori_loop(0, -(-WIN // CHUNK), along_z, 0, unroll=UZ)

    def along_x_first(i, carry):
        y = 2 * i
        high = jnp.concatenate([z_high[y], z_high[y + 1]], axis=1)
        low = jnp.concatenate([z_low[y], z_low[y + 1]], axis=1)
        in_x = three_term(mx, high, low)
        start = pl.multiple_of(y * PW, 16)
        blurred_x[pl.ds(start, PADW), :] = in_x[:, :128]
        blurred_x[pl.ds(start + PW, PADW), :] = in_x[:, 128:]
        return carry

    lax.fori_loop(0, WIN // 2, along_x_first, 0, unroll=UNROLL)

    past = jnp.zeros((PADW - WIN, 256), F32)

    def along_y(i, carry):
        u = 2 * i
        lines = [blurred_x[pl.ds(u + j, PADW, stride=PW), :] for j in range(2)]
        predicted = three_term(my, *pair(*lines)) + backdrop
        seen = jnp.concatenate([seen_data[buffer, u], seen_data[buffer, u + 1]], axis=1)
        ratio = jnp.concatenate([seen.astype(F32) / predicted[:WIN], past], axis=0)
        in_y = three_term(myt, *pair(ratio[:, :128], ratio[:, 128:]))
        start = pl.multiple_of(u * PS, 16)
        back_y[pl.ds(start, PADS), :] = in_y[:, :128]
        back_y[pl.ds(start + PS, PADS), :] = in_y[:, 128:]
        return carry

    lax.fori_loop(0, WIN // 2, along_y, 0, unroll=UNROLL)

    def along_x(i, carry):
        y = 2 * i
        lines = [back_y[pl.ds(y + j, PADW, stride=PS), :] for j in range(2)]
        in_x = three_term(mxt, *pair(*lines))
        start = pl.multiple_of(y * PS, 16)
        back_x[pl.ds(start, PADS), :] = in_x[:, :128]
        back_x[pl.ds(start + PS, PADS), :] = in_x[:, 128:]
        return carry

    lax.fori_loop(0, SIDE // 2, along_x, 0, unroll=UNROLL)

    group = 4
    for i in range(SIDE // group):
        lines = [back_x[pl.ds(group * i + j, PADS, stride=PS), :] for j in range(group)]
        high, low = split(jnp.concatenate(lines, axis=0))
        factor = encode(dot(jnp.concatenate([high, low, high], axis=1), mzt), level)
        for j in range(0, group, 2):
            rows = [factor[k * PADS : k * PADS + SIDE] for k in (j, j + 1)]
            out_ref[(group * i + j) // 2, 0] = jnp.concatenate(rows, axis=0).astype(I16)
    for k in range(SIDE // 2, 16):
        out_ref[k, 0] = jnp.zeros_like(out_ref[k, 0])


UNROLL = 29
CHUNK = 29
PEXTRA = 8
SEXTRA = 8
PW = PADW + PEXTRA
PS = PADS + SEXTRA
UZ = 1


def run_jobs(channel, parts, scalars, top, bottom, view_data, mats):
    slots = mats[0].shape[0]
    hbm = pl.BlockSpec(memory_space=pltpu.HBM)
    smem = pl.BlockSpec(memory_space=pltpu.SMEM)
    specs = [smem] * len(scalars) + [hbm] * (len(parts) + 3)
    specs += [pl.BlockSpec((1,) + m.shape[1:], lambda slot: (slot, 0, 0)) for m in mats]
    return pl.pallas_call(
        functools.partial(job_kernel, channel),
        grid=(slots,),
        in_specs=specs,
        out_specs=pl.BlockSpec((16, 1, 2 * SIDE, 128), lambda slot: (0, slot, 0, 0)),
        scratch_shapes=[
            pltpu.VMEM((2, WIN, PADW, 128), BF16),
            pltpu.VMEM((2, WIN, WIN, 128), BF16),
            pltpu.VMEM((WIN, PADW, 128), BF16),
            pltpu.VMEM((WIN, PADW, 128), BF16),
            pltpu.VMEM((PADW * PW, 128), F32),
            pltpu.VMEM((PADW * PS, 128), F32),
            pltpu.VMEM((PADS * PS, 128), F32),
            pltpu.SemaphoreType.DMA((2, 6)),
        ],
        out_shape=pltpu.HBM((16, slots, 2 * SIDE, 128), I16),
        compiler_params=pltpu.CompilerParams(vmem_limit_bytes=18 << 20),
        cost_estimate=pl.CostEstimate(
            flops=slots * 20 * 128 * (WIN * PADW * (256 + 192 + 192 + 96) + 2 * SIDE * PADS * 192),
            transcendentals=slots * WIN * PADW * 128,
            bytes_accessed=slots * (2 * WIN * PADW * 128 * 2 + 16 * 2 * SIDE * 128 * 4),
        ),
        name="jobs",
    )(*scalars, *gathered_memory(parts), top, bottom, *far_memory(view_data, *mats))


def bands(taps, positions_out, positions_in):
    offsets = positions_in[None, :] - positions_out[:, None] + HALO
    sel = offsets[None, :, :, None] == jnp.arange(taps.shape[1])[None, None, None, :]
    return jnp.sum(jnp.where(sel, taps[:, None, None, :], 0.0), axis=3)


def high_low(matrix):
    high = lax.reduce_precision(matrix, 8, 7)
    return high.astype(BF16), (matrix - high).astype(BF16)


def job_matrices(taps, bricks):
    none = -1000
    far = 1000
    line = jnp.arange(128)
    row = jnp.arange(PADW)
    win_in = jnp.where(row < WIN, row, none)
    win_out = jnp.where(row < WIN, row, far)
    short = jnp.arange(PADS)
    inner_out = jnp.where(short < SIDE, short + HALO, far)
    x_in = jnp.where(row < RIM + 16, row - 1, row - 5)
    x_in = jnp.where((row >= RIM + 16) & (row < RIM + 20), none, x_in)
    x_in = jnp.where((x_in < 0) | (x_in >= WIN), none, x_in)
    inside = (row >= HALO)[None, :] | (bricks > 0)[:, None]
    inside &= (row < HALO + SIDE)[None, :] | (bricks < RING * RING - 1)[:, None]
    forward = lambda t, out, inp: bands(t, out, inp)
    backward = lambda t, out, inp: jnp.swapaxes(bands(t, inp, out), 1, 2)
    three = lambda pair: jnp.concatenate([pair[0], pair[0], pair[1]], axis=2)
    mz = high_low(jnp.swapaxes(forward(taps[:, 2], line, line), 1, 2))
    mzt = high_low(jnp.swapaxes(backward(taps[:, 2], line, line), 1, 2))
    win_in_far = jnp.where(row < WIN, row, far)
    inner_none = jnp.where(short < SIDE, short + HALO, none)
    return (
        jnp.concatenate(mz, axis=1),
        three(high_low(forward(taps[:, 0], win_out, x_in))),
        three(high_low(jnp.where(inside[:, None, :], forward(taps[:, 1], win_out, win_in), 0.0))),
        three(high_low(backward(taps[:, 1], inner_none, win_in_far))),
        three(high_low(backward(taps[:, 0], inner_none, win_in_far))),
        jnp.concatenate([mzt[0], mzt[0], mzt[1]], axis=1),
    )


MORE = 2.6


def add_kernel(owners, views, logs, *refs):
    total, level = refs[-2:]
    out_ref = refs[-3]
    workers, slots = refs[0].shape[:2]
    jobs = range(workers * slots)
    for b in range(workers):
        level[b] = -200.0
    for i in jobs:
        level[owners[i]] = jnp.maximum(level[owners[i]], logs[views[i]] + MORE)
    for channel, parts_ref in enumerate(refs[:-3]):
        total[...] = jnp.zeros_like(total)
        for i in jobs:
            total[owners[i]] += decode(parts_ref[i // slots, i % slots], logs[views[i]])
        for b in range(workers):
            out_ref[b, channel] = encode(total[b], level[b]).astype(I16)


def add_up(owners, views, logs, parts):
    vmem, smem = pl.BlockSpec(memory_space=pltpu.VMEM), pl.BlockSpec(memory_space=pltpu.SMEM)
    workers, rows = parts[0].shape[0], parts[0].shape[2:]
    return pl.pallas_call(
        add_kernel,
        in_specs=[smem] * 3 + [vmem] * len(parts),
        out_specs=vmem,
        out_shape=pltpu.HBM((workers, len(parts)) + rows, I16),
        scratch_shapes=[pltpu.VMEM((workers,) + rows, F32), pltpu.SMEM((workers,), F32)],
        compiler_params=pltpu.CompilerParams(vmem_limit_bytes=8 << 20),
        name="add_up",
    )(owners, views, logs, *parts)


def update_kernel(met, logs, est_ref, total, out_ref):
    seen, level = jnp.int32(0), jnp.float32(-200.0)
    for v in range(met.shape[0]):
        seen += met[v]
        level = jnp.where(met[v] > 0, jnp.maximum(level, logs[v] + MORE), level)
    seen = seen.astype(F32)
    for c in range(out_ref.shape[0]):
        for k in range(SIDE // 2):
            rows = decode(total[k, c], level)
            for j in range(2):
                part = rows[j * SIDE : (j + 1) * SIDE]
                out_ref[c, 2 * k + j] = est_ref[c, 2 * k + j] * part / seen


def update(met, logs, estimate, total):
    vmem, smem = pl.BlockSpec(memory_space=pltpu.VMEM), pl.BlockSpec(memory_space=pltpu.SMEM)
    return pl.pallas_call(
        update_kernel,
        in_specs=[smem, smem, vmem, vmem],
        out_specs=vmem,
        out_shape=jax.ShapeDtypeStruct(estimate.shape, F32),
        compiler_params=pltpu.CompilerParams(vmem_limit_bytes=12 << 20),
        name="update",
    )(met, logs, estimate, total)


def on_device(estimate, view_data, psf, background, slot_brick, slot_view, intersection):
    me = lax.axis_index("tile").astype(I32).reshape(1)
    groups, workers = lax.axis_size("view"), lax.axis_size("tile")
    upward = [(i, i + 1) for i in range(groups - 1)]
    downward = [(j, i) for i, j in upward]
    bricks, views = slot_brick[0, 0], slot_view[0, 0]
    slots = bricks.shape[0]

    wire = estimate.astype(BF16).transpose(0, 2, 1, 3)
    jobs = lax.optimization_barrier(jnp.concatenate([bricks, views]))
    note = jnp.pad(jobs.astype(BF16)[None, None], ((0, 0), (0, SIDE - 1), (0, 128 - 2 * slots)))
    note = jnp.broadcast_to(note, (wire.shape[0],) + note.shape[1:])
    wire = jnp.concatenate([wire[:, :, :RIM], note[:, :, None], wire[:, :, SIDE - RIM + 1 :]], axis=2)
    rings = join(ring_whole([wire[0], wire[1]], (0, 1)))
    rings, view_data, psf, views, bricks = lax.optimization_barrier(
        (rings, view_data, psf, views, bricks)
    )
    near = ring_near(rings, (1, 0))

    chosen = views[:, None] == jnp.arange(psf.shape[0])[None, :]
    taps = jnp.sum(jnp.where(chosen[:, :, None, None], psf[None], 0.0), axis=1)
    mats = job_matrices(taps, bricks)
    data = view_data[0, 0]
    logs = jnp.log2(jnp.maximum(4.0 / background * jnp.prod(jnp.sum(psf, axis=2), axis=1), 1e-30)) - 15.9
    mats, bricks = lax.optimization_barrier((mats, bricks))
    above = lax.ppermute(bricks, "view", downward)
    below = lax.ppermute(bricks, "view", upward)
    near, mats, data, above, below, logs = lax.optimization_barrier(
        (near, mats, data, above, below, logs)
    )
    gathered = ring_pass_on(near, (1, 0))

    rims = margins(gathered, me, above, below)
    edges = [
        (lax.ppermute(rims[2 * c], "view", upward), lax.ppermute(rims[2 * c + 1], "view", downward))
        for c in range(2)
    ]
    notes = jnp.concatenate([p[::SIDE, RIM, : 2 * slots] for p in gathered[0]], axis=0)
    places = place_of(jnp.arange(workers, dtype=I32), me[0], True)
    match = places[:, None] == jnp.arange(workers)[None, :]
    notes = jnp.sum(jnp.where(match[:, :, None], notes.astype(F32)[None], 0.0), axis=1)
    notes = notes.astype(I32)
    owners, seen_by = notes[:, :slots].reshape(-1), notes[:, slots:].reshape(-1)

    parts = []
    scalars = (me, bricks, views, background, logs)
    for channel in range(2):
        factors = run_jobs(channel, gathered[channel], scalars, *edges[channel], data, mats)
        parts.append(lax.all_to_all(factors, "tile", 0, 0, tiled=True))
    total = lax.all_to_all(add_up(owners, seen_by, logs, parts), "tile", 0, 0, tiled=True)
    return update(intersection[0, 0], logs, estimate, total)


def solution(mesh):
    placed = (
        P(None, "view", "tile", None),
        P("view", "tile", None, None, None, None, None),
        P(),
        P(),
        P("view", "tile", None),
        P("view", "tile", None),
        P("view", "tile", None),
    )
    return jax.shard_map(
        on_device,
        mesh=mesh,
        in_specs=placed,
        out_specs=P(None, "view", "tile", None),
        check_vma=False,
    )
```

```python
import functools

import jax
import jax.numpy as jnp
from jax import lax
from jax.experimental import pallas as pl
from jax.experimental.pallas import tpu as pltpu
from jax.sharding import PartitionSpec as P

F32, BF16, I32, I16 = jnp.float32, jnp.bfloat16, jnp.int32, jnp.int16
HALO = 15
SIDE = 28
WIN = SIDE + 2 * HALO
PADW = 64
PADS = 32
RIM = 16
RING = 4


def far_memory(*arrays):
    return [pltpu.with_memory_space_constraint(a, pltpu.HBM) for a in arrays]


def gathered_memory(parts):
    return far_memory(*parts)


def torus_step(array, dx, dy):
    pairs = [
        (x * RING + y, ((x + dx) % RING) * RING + (y + dy) % RING)
        for x in range(RING)
        for y in range(RING)
    ]
    return lax.ppermute(array, "tile", pairs)


def along(axis, step):
    return (step, 0) if axis == 0 else (0, step)


def ring_near(arrays, axes):
    return [
        [a, torus_step(a, *along(ax, 1)), torus_step(a, *along(ax, -1))]
        for a, ax in zip(arrays, axes)
    ]


def ring_whole(arrays, axes):
    return [
        [a] + [torus_step(a, *along(ax, d)) for d in (1, -1, 2)] for a, ax in zip(arrays, axes)
    ]


def join_kernel(*refs):
    stage, sems, refs = refs[-2], refs[-1], refs[:-2]
    outs, refs = refs[-2:], refs[:-2]
    each = len(refs) // len(outs)
    rows = refs[0].shape[0]
    ins = []
    for i, ref in enumerate(refs):
        target = stage.at[i // each, pl.ds(i % each * rows, rows)]
        ins.append(pltpu.make_async_copy(ref, target, sems.at[i]))
        ins[i].start()
    sends = []
    for i, out in enumerate(outs):
        for copy in ins[i * each : (i + 1) * each]:
            copy.wait()
        sends.append(pltpu.make_async_copy(stage.at[i], out, sems.at[len(refs) + i]))
        sends[i].start()
    for send in sends:
        send.wait()


def join(rings):
    arrays = [a for ring in rings for a in ring]
    whole = (len(rings[0]) * arrays[0].shape[0],) + arrays[0].shape[1:]
    return pl.pallas_call(
        join_kernel,
        in_specs=[pl.BlockSpec(memory_space=pl.ANY)] * len(arrays),
        out_specs=[pl.BlockSpec(memory_space=pltpu.HBM)] * len(rings),
        out_shape=[pltpu.HBM(whole, BF16)] * len(rings),
        scratch_shapes=[
            pltpu.VMEM((len(rings),) + whole, BF16),
            pltpu.SemaphoreType.DMA((len(arrays) + len(rings),)),
        ],
        compiler_params=pltpu.CompilerParams(vmem_limit_bytes=4 << 20),
        name="join",
    )(*arrays)


def halves_kernel(*refs):
    stage, sems, refs = refs[-2], refs[-1], refs[:-2]
    count = len(refs) // 2
    ins, outs = [], []
    for i in range(count):
        half = refs[i].shape[0] // 2
        source = refs[i].at[pl.ds(0 if i % 2 == 0 else half, half)]
        ins.append(pltpu.make_async_copy(source, stage.at[i], sems.at[i, 0]))
        outs.append(pltpu.make_async_copy(stage.at[i], refs[count + i], sems.at[i, 1]))
        ins[i].start()
    for i in range(count):
        ins[i].wait()
        outs[i].start()
    for i in range(count):
        outs[i].wait()


def take_halves(near):
    arrays = [a for _, lower, upper in near for a in (lower, upper)]
    anywhere = pl.BlockSpec(memory_space=pl.ANY)
    shape = arrays[0].shape
    taken = pl.pallas_call(
        halves_kernel,
        in_specs=[anywhere] * len(arrays),
        out_specs=[anywhere] * len(arrays),
        out_shape=[pltpu.HBM((shape[0] // 2,) + shape[1:], BF16)] * len(arrays),
        scratch_shapes=[
            pltpu.VMEM((len(arrays), shape[0] // 2) + shape[1:], BF16),
            pltpu.SemaphoreType.DMA((len(arrays), 2)),
        ],
        compiler_params=pltpu.CompilerParams(vmem_limit_bytes=4 << 20),
        name="halves",
    )(*arrays)
    return [(taken[2 * i], taken[2 * i + 1]) for i in range(len(near))]


def ring_pass_on(near, axes):
    return [
        [*n, torus_step(low, *along(ax, 1)), torus_step(high, *along(ax, -1))]
        for n, (low, high), ax in zip(near, take_halves(near), axes)
    ]


def rank(delta):
    delta = lax.rem(delta + RING, RING)
    return jnp.where(delta == 3, 1, jnp.where(delta == 1, 2, jnp.where(delta == 2, 3, 0)))


def place_of(brick, me, x_first):
    in_x = rank(lax.div(brick, RING) - lax.div(me, RING))
    in_y = rank(lax.rem(brick, RING) - lax.rem(me, RING))
    return in_y * RING + in_x if x_first else in_x * RING + in_y


def window_place(which, brick, me, x_first):
    return place_of(jnp.clip(brick + which - 1, 0, RING * RING - 1), me, x_first)


WINDOWS = ((SIDE - HALO, HALO, 0), (0, SIDE, HALO), (0, HALO, HALO + SIDE))


def copy_window(parts, which, place, rows, target, sem):
    first, count, _ = WINDOWS[which]
    base = 0
    for part in parts:
        held = part.shape[0] // SIDE

        @pl.when((place >= base) & (place < base + held))
        def _(part=part, base=base):
            source = part.at[pl.ds((place - base) * SIDE + first, count), rows]
            pltpu.make_async_copy(source, target, sem).start()

        base += held


def wait_window(parts, which, rows, target, sem):
    count = WINDOWS[which][1]
    pltpu.make_async_copy(parts[0].at[pl.ds(0, count), rows], target, sem).wait()


def margin_kernel(*refs):
    me, *asked = refs[:3]
    refs = refs[3:]
    refs, (stage, sems) = refs[:-2], refs[-2:]
    gathered, outs = (refs[:PARTS], refs[PARTS : 2 * PARTS]), refs[2 * PARTS :]
    slots = outs[0].shape[0]
    copies = []
    for channel, parts in enumerate(gathered):
        for side in range(2):
            rows = pl.ds(RIM, RIM) if side == 0 else pl.ds(0, RIM)
            for slot in range(slots):
                item = side * slots + slot
                waits = []
                for which, (_, count, to) in enumerate(WINDOWS):
                    target = stage.at[channel, item, pl.ds(to, count)]
                    sem = sems.at[channel, item, which]
                    place = window_place(which, asked[side][slot], me[0], channel == 0)
                    copy_window(parts, which, place, rows, target, sem)
                    waits.append((parts, which, rows, target, sem))
                out = pltpu.make_async_copy(
                    stage.at[channel, item],
                    outs[2 * channel + side].at[slot],
                    sems.at[channel, item, 3],
                )
                copies.append((waits, out))
    for waits, out in copies:
        for item in waits:
            wait_window(*item)
        out.start()
    for _, out in copies:
        out.wait()


PARTS = 5


def margins(gathered, me, above, below):
    slots = above.shape[0]
    hbm, smem = pl.BlockSpec(memory_space=pltpu.HBM), pl.BlockSpec(memory_space=pltpu.SMEM)
    return pl.pallas_call(
        margin_kernel,
        in_specs=[smem] * 3 + [hbm] * (2 * PARTS),
        out_specs=[hbm] * 4,
        out_shape=[pltpu.HBM((slots, WIN, RIM, 128), BF16)] * 4,
        scratch_shapes=[
            pltpu.VMEM((2, 2 * slots, WIN, RIM, 128), BF16),
            pltpu.SemaphoreType.DMA((2, 2 * slots, 4)),
        ],
        compiler_params=pltpu.CompilerParams(vmem_limit_bytes=4 << 20),
        name="margins",
    )(me, above, below, *gathered_memory(gathered[0]), *gathered_memory(gathered[1]))


def split(value):
    high = value.astype(BF16)
    low = (value - high.astype(F32)).astype(BF16)
    return high, low


def pair(first, second):
    (h0, l0), (h1, l1) = split(first), split(second)
    return jnp.concatenate([h0, h1], axis=1), jnp.concatenate([l0, l1], axis=1)


def three_term(matrix, high, low):
    return dot(matrix, jnp.concatenate([high, low, high], axis=0))


STEPS = 2048.0


def encode(value, level):
    code = (jnp.log2(jnp.maximum(value, 1e-37)) - level) * STEPS
    return jnp.round(jnp.clip(code, -32767.0, 32767.0)).astype(I32)


def decode(code, level):
    return jnp.exp2(code.astype(I32).astype(F32) * (1.0 / STEPS) + level)


def dot(a, b):
    return jnp.dot(a, b, preferred_element_type=F32)


def job_kernel(channel, me, bricks, views, backdrops, logs, *refs):
    parts, refs = refs[:PARTS], refs[PARTS:]
    top_ref, bottom_ref, data_ref, mz_ref, mx_ref, my_ref, myt_ref, mxt_ref, mzt_ref, out_ref = refs[:10]
    blocks, seen_data, z_high, z_low, blurred_x, back_y, back_x, sems = refs[10:]
    slot, slots = pl.program_id(0), pl.num_programs(0)
    mid = pl.ds(RIM, PADS)

    def others(which_slot, buffer):
        span = pl.ds(0, WIN)
        return (
            (top_ref.at[which_slot], blocks.at[buffer, span, pl.ds(0, RIM)], sems.at[buffer, 3]),
            (bottom_ref.at[which_slot], blocks.at[buffer, span, pl.ds(RIM + PADS, RIM)], sems.at[buffer, 4]),
            (data_ref.at[which_slot, channel], seen_data.at[buffer], sems.at[buffer, 5]),
        )

    def fetch(which_slot, buffer):
        for which, (_, count, to) in enumerate(WINDOWS):
            target = blocks.at[buffer, pl.ds(to, count), mid]
            place = window_place(which, bricks[which_slot], me[0], channel == 0)
            copy_window(parts, which, place, pl.ds(0, PADS), target, sems.at[buffer, which])
        for source, target, sem in others(which_slot, buffer):
            pltpu.make_async_copy(source, target, sem).start()

    buffer = lax.rem(slot, 2)

    @pl.when(slot == 0)
    def _():
        fetch(0, 0)
        blurred_x[WIN * PW :] = jnp.zeros_like(blurred_x[WIN * PW :])
        back_y[WIN * PS :] = jnp.zeros_like(back_y[WIN * PS :])
        back_x[SIDE * PS :] = jnp.zeros_like(back_x[SIDE * PS :])

    @pl.when(slot + 1 < slots)
    def _():
        fetch(slot + 1, 1 - buffer)

    for which, (_, count, to) in enumerate(WINDOWS):
        target = blocks.at[buffer, pl.ds(to, count), mid]
        wait_window(parts, which, pl.ds(0, PADS), target, sems.at[buffer, which])
    for source, target, sem in others(slot, buffer):
        pltpu.make_async_copy(source, target, sem).wait()

    mz, mx, my = mz_ref[0], mx_ref[0], my_ref[0]
    myt, mxt, mzt = myt_ref[0], mxt_ref[0], mzt_ref[0]
    backdrop = backdrops[views[slot]]
    level = logs[views[slot]]

    def along_z(i, carry):
        start = i * CHUNK
        rows = blocks[buffer, pl.ds(start, CHUNK)].reshape(CHUNK * PADW, 128)
        in_z = dot(jnp.concatenate([rows, rows], axis=1), mz)
        high, low = split(in_z)
        z_high[pl.ds(start, CHUNK)] = high.reshape(CHUNK, PADW, 128)
        z_low[pl.ds(start, CHUNK)] = low.reshape(CHUNK, PADW, 128)
        return carry

    lax.fori_loop(0, WIN // CHUNK, along_z, 0, unroll=WIN // CHUNK)

    def along_x_first(i, carry):
        y = 2 * i
        high = jnp.concatenate([z_high[y], z_high[y + 1]], axis=1)
        low = jnp.concatenate([z_low[y], z_low[y + 1]], axis=1)
        in_x = three_term(mx, high, low)
        start = pl.multiple_of(y * PW, 16)
        blurred_x[pl.ds(start, PADW), :] = in_x[:, :128]
        blurred_x[pl.ds(start + PW, PADW), :] = in_x[:, 128:]
        return carry

    lax.fori_loop(0, WIN // 2, along_x_first, 0, unroll=WIN // 2)

    past = jnp.zeros((PADW - WIN, 256), F32)

    def along_y(i, carry):
        u = 2 * i
        lines = [blurred_x[pl.ds(u + j, PADW, stride=PW), :] for j in range(2)]
        predicted = three_term(my, *pair(*lines)) + backdrop
        seen = jnp.concatenate([seen_data[buffer, u], seen_data[buffer, u + 1]], axis=1)
        ratio = jnp.concatenate([seen.astype(F32) / predicted[:WIN], past], axis=0)
        in_y = three_term(myt, *pair(ratio[:, :128], ratio[:, 128:]))
        start = pl.multiple_of(u * PS, 16)
        back_y[pl.ds(start, PADS), :] = in_y[:, :128]
        back_y[pl.ds(start + PS, PADS), :] = in_y[:, 128:]
        return carry

    lax.fori_loop(0, WIN // 2, along_y, 0, unroll=WIN // 2)

    def along_x(i, carry):
        y = 2 * i
        lines = [back_y[pl.ds(y + j, PADW, stride=PS), :] for j in range(2)]
        in_x = three_term(mxt, *pair(*lines))
        start = pl.multiple_of(y * PS, 16)
        back_x[pl.ds(start, PADS), :] = in_x[:, :128]
        back_x[pl.ds(start + PS, PADS), :] = in_x[:, 128:]
        return carry

    lax.fori_loop(0, SIDE // 2, along_x, 0, unroll=SIDE // 2)

    group = 4
    for i in range(SIDE // group):
        lines = [back_x[pl.ds(group * i + j, PADS, stride=PS), :] for j in range(group)]
        high, low = split(jnp.concatenate(lines, axis=0))
        factor = encode(dot(jnp.concatenate([high, low, high], axis=1), mzt), level)
        for j in range(0, group, 2):
            rows = [factor[k * PADS : k * PADS + SIDE] for k in (j, j + 1)]
            out_ref[(group * i + j) // 2, 0] = jnp.concatenate(rows, axis=0).astype(I16)
    for k in range(SIDE // 2, 16):
        out_ref[k, 0] = jnp.zeros_like(out_ref[k, 0])


CHUNK = 29
PEXTRA = 8
SEXTRA = 8
PW = PADW + PEXTRA
PS = PADS + SEXTRA


def run_jobs(channel, parts, scalars, top, bottom, view_data, mats):
    slots = mats[0].shape[0]
    hbm = pl.BlockSpec(memory_space=pltpu.HBM)
    smem = pl.BlockSpec(memory_space=pltpu.SMEM)
    specs = [smem] * len(scalars) + [hbm] * (len(parts) + 3)
    specs += [pl.BlockSpec((1,) + m.shape[1:], lambda slot: (slot, 0, 0)) for m in mats]
    return pl.pallas_call(
        functools.partial(job_kernel, channel),
        grid=(slots,),
        in_specs=specs,
        out_specs=pl.BlockSpec((16, 1, 2 * SIDE, 128), lambda slot: (0, slot, 0, 0)),
        scratch_shapes=[
            pltpu.VMEM((2, WIN, PADW, 128), BF16),
            pltpu.VMEM((2, WIN, WIN, 128), BF16),
            pltpu.VMEM((WIN, PADW, 128), BF16),
            pltpu.VMEM((WIN, PADW, 128), BF16),
            pltpu.VMEM((PADW * PW, 128), F32),
            pltpu.VMEM((PADW * PS, 128), F32),
            pltpu.VMEM((PADS * PS, 128), F32),
            pltpu.SemaphoreType.DMA((2, 6)),
        ],
        out_shape=pltpu.HBM((16, slots, 2 * SIDE, 128), I16),
        compiler_params=pltpu.CompilerParams(vmem_limit_bytes=18 << 20),
        cost_estimate=pl.CostEstimate(
            flops=slots * 20 * 128 * (WIN * PADW * (256 + 192 + 192 + 96) + 2 * SIDE * PADS * 192),
            transcendentals=slots * WIN * PADW * 128,
            bytes_accessed=slots * (2 * WIN * PADW * 128 * 2 + 16 * 2 * SIDE * 128 * 4),
        ),
        name="jobs",
    )(*scalars, *gathered_memory(parts), top, bottom, *far_memory(view_data, *mats))


def bands(taps, positions_out, positions_in):
    offsets = positions_in[None, :] - positions_out[:, None] + HALO
    sel = offsets[None, :, :, None] == jnp.arange(taps.shape[1])[None, None, None, :]
    return jnp.sum(jnp.where(sel, taps[:, None, None, :], 0.0), axis=3)


def high_low(matrix):
    high = lax.reduce_precision(matrix, 8, 7)
    return high.astype(BF16), (matrix - high).astype(BF16)


def job_matrices(taps, bricks):
    none = -1000
    far = 1000
    line = jnp.arange(128)
    row = jnp.arange(PADW)
    win_in = jnp.where(row < WIN, row, none)
    win_out = jnp.where(row < WIN, row, far)
    short = jnp.arange(PADS)
    inner_out = jnp.where(short < SIDE, short + HALO, far)
    x_in = jnp.where(row < RIM + 16, row - 1, row - 5)
    x_in = jnp.where((row >= RIM + 16) & (row < RIM + 20), none, x_in)
    x_in = jnp.where((x_in < 0) | (x_in >= WIN), none, x_in)
    inside = (row >= HALO)[None, :] | (bricks > 0)[:, None]
    inside &= (row < HALO + SIDE)[None, :] | (bricks < RING * RING - 1)[:, None]
    forward = lambda t, out, inp: bands(t, out, inp)
    backward = lambda t, out, inp: jnp.swapaxes(bands(t, inp, out), 1, 2)
    three = lambda pair: jnp.concatenate([pair[0], pair[0], pair[1]], axis=2)
    mz = high_low(jnp.swapaxes(forward(taps[:, 2], line, line), 1, 2))
    mzt = high_low(jnp.swapaxes(backward(taps[:, 2], line, line), 1, 2))
    win_in_far = jnp.where(row < WIN, row, far)
    inner_none = jnp.where(short < SIDE, short + HALO, none)
    return (
        jnp.concatenate(mz, axis=1),
        three(high_low(forward(taps[:, 0], win_out, x_in))),
        three(high_low(jnp.where(inside[:, None, :], forward(taps[:, 1], win_out, win_in), 0.0))),
        three(high_low(backward(taps[:, 1], inner_none, win_in_far))),
        three(high_low(backward(taps[:, 0], inner_none, win_in_far))),
        jnp.concatenate([mzt[0], mzt[0], mzt[1]], axis=1),
    )


MORE = 2.6


def add_kernel(owners, views, logs, *refs):
    total, level = refs[-2:]
    out_ref = refs[-3]
    workers, slots = refs[0].shape[:2]
    jobs = range(workers * slots)
    for b in range(workers):
        level[b] = -200.0
    for i in jobs:
        level[owners[i]] = jnp.maximum(level[owners[i]], logs[views[i]] + MORE)
    for channel, parts_ref in enumerate(refs[:-3]):
        total[...] = jnp.zeros_like(total)
        for i in jobs:
            total[owners[i]] += decode(parts_ref[i // slots, i % slots], logs[views[i]])
        for b in range(workers):
            out_ref[b, channel] = encode(total[b], level[b]).astype(I16)


def add_up(owners, views, logs, parts):
    vmem, smem = pl.BlockSpec(memory_space=pltpu.VMEM), pl.BlockSpec(memory_space=pltpu.SMEM)
    workers, rows = parts[0].shape[0], parts[0].shape[2:]
    return pl.pallas_call(
        add_kernel,
        in_specs=[smem] * 3 + [vmem] * len(parts),
        out_specs=vmem,
        out_shape=pltpu.HBM((workers, len(parts)) + rows, I16),
        scratch_shapes=[pltpu.VMEM((workers,) + rows, F32), pltpu.SMEM((workers,), F32)],
        compiler_params=pltpu.CompilerParams(vmem_limit_bytes=8 << 20),
        name="add_up",
    )(owners, views, logs, *parts)


def update_kernel(met, logs, est_ref, total, out_ref):
    seen, level = jnp.int32(0), jnp.float32(-200.0)
    for v in range(met.shape[0]):
        seen += met[v]
        level = jnp.where(met[v] > 0, jnp.maximum(level, logs[v] + MORE), level)
    seen = seen.astype(F32)
    for c in range(out_ref.shape[0]):
        for k in range(SIDE // 2):
            rows = decode(total[k, c], level)
            for j in range(2):
                part = rows[j * SIDE : (j + 1) * SIDE]
                out_ref[c, 2 * k + j] = est_ref[c, 2 * k + j] * part / seen


def update(met, logs, estimate, total):
    vmem, smem = pl.BlockSpec(memory_space=pltpu.VMEM), pl.BlockSpec(memory_space=pltpu.SMEM)
    return pl.pallas_call(
        update_kernel,
        in_specs=[smem, smem, vmem, vmem],
        out_specs=vmem,
        out_shape=jax.ShapeDtypeStruct(estimate.shape, F32),
        compiler_params=pltpu.CompilerParams(vmem_limit_bytes=12 << 20),
        name="update",
    )(met, logs, estimate, total)


def on_device(estimate, view_data, psf, background, slot_brick, slot_view, intersection):
    me = lax.axis_index("tile").astype(I32).reshape(1)
    groups, workers = lax.axis_size("view"), lax.axis_size("tile")
    upward = [(i, i + 1) for i in range(groups - 1)]
    downward = [(j, i) for i, j in upward]
    bricks, views = slot_brick[0, 0], slot_view[0, 0]
    slots = bricks.shape[0]

    wire = estimate.astype(BF16).transpose(0, 2, 1, 3)
    jobs = lax.optimization_barrier(jnp.concatenate([bricks, views]))
    note = jnp.pad(jobs.astype(BF16)[None, None], ((0, 0), (0, SIDE - 1), (0, 128 - 2 * slots)))
    note = jnp.broadcast_to(note, (wire.shape[0],) + note.shape[1:])
    wire = jnp.concatenate([wire[:, :, :RIM], note[:, :, None], wire[:, :, SIDE - RIM + 1 :]], axis=2)
    rings = join(ring_whole([wire[0], wire[1]], (0, 1)))
    rings, view_data, psf, views, bricks = lax.optimization_barrier(
        (rings, view_data, psf, views, bricks)
    )
    near = ring_near(rings, (1, 0))

    chosen = views[:, None] == jnp.arange(psf.shape[0])[None, :]
    taps = jnp.sum(jnp.where(chosen[:, :, None, None], psf[None], 0.0), axis=1)
    mats = job_matrices(taps, bricks)
    data = view_data[0, 0]
    logs = jnp.log2(jnp.maximum(4.0 / background * jnp.prod(jnp.sum(psf, axis=2), axis=1), 1e-30)) - 15.9
    mats, bricks = lax.optimization_barrier((mats, bricks))
    above = lax.ppermute(bricks, "view", downward)
    below = lax.ppermute(bricks, "view", upward)
    near, mats, data, above, below, logs = lax.optimization_barrier(
        (near, mats, data, above, below, logs)
    )
    gathered = ring_pass_on(near, (1, 0))

    rims = margins(gathered, me, above, below)
    edges = [
        (lax.ppermute(rims[2 * c], "view", upward), lax.ppermute(rims[2 * c + 1], "view", downward))
        for c in range(2)
    ]
    notes = jnp.concatenate([p[::SIDE, RIM, : 2 * slots] for p in gathered[0]], axis=0)
    places = place_of(jnp.arange(workers, dtype=I32), me[0], True)
    match = places[:, None] == jnp.arange(workers)[None, :]
    notes = jnp.sum(jnp.where(match[:, :, None], notes.astype(F32)[None], 0.0), axis=1)
    notes = notes.astype(I32)
    owners, seen_by = notes[:, :slots].reshape(-1), notes[:, slots:].reshape(-1)

    parts = []
    scalars = (me, bricks, views, background, logs)
    for channel in range(2):
        factors = run_jobs(channel, gathered[channel], scalars, *edges[channel], data, mats)
        parts.append(lax.all_to_all(factors, "tile", 0, 0, tiled=True))
    total = lax.all_to_all(add_up(owners, seen_by, logs, parts), "tile", 0, 0, tiled=True)
    return update(intersection[0, 0], logs, estimate, total)


def solution(mesh):
    placed = (
        P(None, "view", "tile", None),
        P("view", "tile", None, None, None, None, None),
        P(),
        P(),
        P("view", "tile", None),
        P("view", "tile", None),
        P("view", "tile", None),
    )
    return jax.shard_map(
        on_device,
        mesh=mesh,
        in_specs=placed,
        out_specs=P(None, "view", "tile", None),
        check_vma=False,
    )
```

```python
import functools

import jax
import jax.numpy as jnp
from jax import lax
from jax.experimental import pallas as pl
from jax.experimental.pallas import tpu as pltpu
from jax.sharding import PartitionSpec as P

F32, BF16, I32, I16 = jnp.float32, jnp.bfloat16, jnp.int32, jnp.int16
HALO = 15
SIDE = 28
WIN = SIDE + 2 * HALO
PADW = 64
PADS = 32
RIM = 16
RING = 4


def far_memory(*arrays):
    return [pltpu.with_memory_space_constraint(a, pltpu.HBM) for a in arrays]


def gathered_memory(parts):
    return far_memory(*parts)


def torus_step(array, dx, dy):
    pairs = [
        (x * RING + y, ((x + dx) % RING) * RING + (y + dy) % RING)
        for x in range(RING)
        for y in range(RING)
    ]
    return lax.ppermute(array, "tile", pairs)


def along(axis, step):
    return (step, 0) if axis == 0 else (0, step)


def ring_near(arrays, axes):
    return [
        [a, torus_step(a, *along(ax, 1)), torus_step(a, *along(ax, -1))]
        for a, ax in zip(arrays, axes)
    ]


def ring_whole(arrays, axes):
    return [
        [a] + [torus_step(a, *along(ax, d)) for d in (1, -1, 2)] for a, ax in zip(arrays, axes)
    ]


def join_kernel(*refs):
    stage, sems, refs = refs[-2], refs[-1], refs[:-2]
    outs, refs = refs[-2:], refs[:-2]
    each = len(refs) // len(outs)
    rows = refs[0].shape[0]
    ins = []
    for i, ref in enumerate(refs):
        target = stage.at[i // each, pl.ds(i % each * rows, rows)]
        ins.append(pltpu.make_async_copy(ref, target, sems.at[i]))
        ins[i].start()
    sends = []
    for i, out in enumerate(outs):
        for copy in ins[i * each : (i + 1) * each]:
            copy.wait()
        sends.append(pltpu.make_async_copy(stage.at[i], out, sems.at[len(refs) + i]))
        sends[i].start()
    for send in sends:
        send.wait()


def join(rings):
    arrays = [a for ring in rings for a in ring]
    whole = (len(rings[0]) * arrays[0].shape[0],) + arrays[0].shape[1:]
    return pl.pallas_call(
        join_kernel,
        in_specs=[pl.BlockSpec(memory_space=pl.ANY)] * len(arrays),
        out_specs=[pl.BlockSpec(memory_space=pltpu.HBM)] * len(rings),
        out_shape=[pltpu.HBM(whole, BF16)] * len(rings),
        scratch_shapes=[
            pltpu.VMEM((len(rings),) + whole, BF16),
            pltpu.SemaphoreType.DMA((len(arrays) + len(rings),)),
        ],
        compiler_params=pltpu.CompilerParams(vmem_limit_bytes=4 << 20),
        name="join",
    )(*arrays)


def halves_kernel(*refs):
    stage, sems, refs = refs[-2], refs[-1], refs[:-2]
    count = len(refs) // 2
    ins, outs = [], []
    for i in range(count):
        half = refs[i].shape[0] // 2
        source = refs[i].at[pl.ds(0 if i % 2 == 0 else half, half)]
        ins.append(pltpu.make_async_copy(source, stage.at[i], sems.at[i, 0]))
        outs.append(pltpu.make_async_copy(stage.at[i], refs[count + i], sems.at[i, 1]))
        ins[i].start()
    for i in range(count):
        ins[i].wait()
        outs[i].start()
    for i in range(count):
        outs[i].wait()


def take_halves(near):
    arrays = [a for _, lower, upper in near for a in (lower, upper)]
    anywhere = pl.BlockSpec(memory_space=pl.ANY)
    shape = arrays[0].shape
    taken = pl.pallas_call(
        halves_kernel,
        in_specs=[anywhere] * len(arrays),
        out_specs=[anywhere] * len(arrays),
        out_shape=[pltpu.HBM((shape[0] // 2,) + shape[1:], BF16)] * len(arrays),
        scratch_shapes=[
            pltpu.VMEM((len(arrays), shape[0] // 2) + shape[1:], BF16),
            pltpu.SemaphoreType.DMA((len(arrays), 2)),
        ],
        compiler_params=pltpu.CompilerParams(vmem_limit_bytes=4 << 20),
        name="halves",
    )(*arrays)
    return [(taken[2 * i], taken[2 * i + 1]) for i in range(len(near))]


def ring_pass_on(near, axes):
    return [
        [*n, torus_step(low, *along(ax, 1)), torus_step(high, *along(ax, -1))]
        for n, (low, high), ax in zip(near, take_halves(near), axes)
    ]


def rank(delta):
    delta = lax.rem(delta + RING, RING)
    return jnp.where(delta == 3, 1, jnp.where(delta == 1, 2, jnp.where(delta == 2, 3, 0)))


def place_of(brick, me, x_first):
    in_x = rank(lax.div(brick, RING) - lax.div(me, RING))
    in_y = rank(lax.rem(brick, RING) - lax.rem(me, RING))
    return in_y * RING + in_x if x_first else in_x * RING + in_y


def window_place(which, brick, me, x_first):
    return place_of(jnp.clip(brick + which - 1, 0, RING * RING - 1), me, x_first)


WINDOWS = ((SIDE - HALO, HALO, 0), (0, SIDE, HALO), (0, HALO, HALO + SIDE))


def copy_window(parts, which, place, rows, target, sem):
    first, count, _ = WINDOWS[which]
    base = 0
    for part in parts:
        held = part.shape[0] // SIDE

        @pl.when((place >= base) & (place < base + held))
        def _(part=part, base=base):
            source = part.at[pl.ds((place - base) * SIDE + first, count), rows]
            pltpu.make_async_copy(source, target, sem).start()

        base += held


def wait_window(parts, which, rows, target, sem):
    count = WINDOWS[which][1]
    pltpu.make_async_copy(parts[0].at[pl.ds(0, count), rows], target, sem).wait()


def margin_kernel(*refs):
    me, *asked = refs[:3]
    refs = refs[3:]
    refs, (stage, sems) = refs[:-2], refs[-2:]
    gathered, outs = (refs[:PARTS], refs[PARTS : 2 * PARTS]), refs[2 * PARTS :]
    slots = outs[0].shape[0]
    copies = []
    for channel, parts in enumerate(gathered):
        for side in range(2):
            rows = pl.ds(RIM, RIM) if side == 0 else pl.ds(0, RIM)
            for slot in range(slots):
                item = side * slots + slot
                waits = []
                for which, (_, count, to) in enumerate(WINDOWS):
                    target = stage.at[channel, item, pl.ds(to, count)]
                    sem = sems.at[channel, item, which]
                    place = window_place(which, asked[side][slot], me[0], channel == 0)
                    copy_window(parts, which, place, rows, target, sem)
                    waits.append((parts, which, rows, target, sem))
                out = pltpu.make_async_copy(
                    stage.at[channel, item],
                    outs[2 * channel + side].at[slot],
                    sems.at[channel, item, 3],
                )
                copies.append((waits, out))
    for waits, out in copies:
        for item in waits:
            wait_window(*item)
        out.start()
    for _, out in copies:
        out.wait()


PARTS = 5


def margins(gathered, me, above, below):
    slots = above.shape[0]
    hbm, smem = pl.BlockSpec(memory_space=pltpu.HBM), pl.BlockSpec(memory_space=pltpu.SMEM)
    return pl.pallas_call(
        margin_kernel,
        in_specs=[smem] * 3 + [hbm] * (2 * PARTS),
        out_specs=[hbm] * 4,
        out_shape=[pltpu.HBM((slots, WIN, RIM, 128), BF16)] * 4,
        scratch_shapes=[
            pltpu.VMEM((2, 2 * slots, WIN, RIM, 128), BF16),
            pltpu.SemaphoreType.DMA((2, 2 * slots, 4)),
        ],
        compiler_params=pltpu.CompilerParams(vmem_limit_bytes=4 << 20),
        name="margins",
    )(me, above, below, *gathered_memory(gathered[0]), *gathered_memory(gathered[1]))


def split(value):
    high = value.astype(BF16)
    low = (value - high.astype(F32)).astype(BF16)
    return high, low


def pair(first, second):
    (h0, l0), (h1, l1) = split(first), split(second)
    return jnp.concatenate([h0, h1], axis=1), jnp.concatenate([l0, l1], axis=1)


def three_term(matrix, high, low):
    return dot(matrix, jnp.concatenate([high, low, high], axis=0))


STEPS = 2048.0


def encode(value, level):
    code = (jnp.log2(jnp.maximum(value, 1e-37)) - level) * STEPS
    return jnp.round(jnp.clip(code, -32767.0, 32767.0)).astype(I32)


def decode(code, level):
    return jnp.exp2(code.astype(I32).astype(F32) * (1.0 / STEPS) + level)


def dot(a, b):
    return jnp.dot(a, b, preferred_element_type=F32)


def job_kernel(channel, me, bricks, views, backdrops, logs, *refs):
    parts, refs = refs[:PARTS], refs[PARTS:]
    top_ref, bottom_ref, data_ref, mz_ref, mx_ref, my_ref, myt_ref, mxt_ref, mzt_ref, out_ref = refs[:10]
    blocks, seen_data, z_high, z_low, blurred_x, back_y, back_x, sems = refs[10:]
    slot, slots = pl.program_id(0), pl.num_programs(0)
    mid = pl.ds(RIM, PADS)

    def others(which_slot, buffer):
        span = pl.ds(0, WIN)
        return (
            (top_ref.at[which_slot], blocks.at[buffer, span, pl.ds(0, RIM)], sems.at[buffer, 3]),
            (bottom_ref.at[which_slot], blocks.at[buffer, span, pl.ds(RIM + PADS, RIM)], sems.at[buffer, 4]),
            (data_ref.at[which_slot, channel], seen_data.at[buffer], sems.at[buffer, 5]),
        )

    def fetch(which_slot, buffer):
        for which, (_, count, to) in enumerate(WINDOWS):
            target = blocks.at[buffer, pl.ds(to, count), mid]
            place = window_place(which, bricks[which_slot], me[0], channel == 0)
            copy_window(parts, which, place, pl.ds(0, PADS), target, sems.at[buffer, which])
        for source, target, sem in others(which_slot, buffer):
            pltpu.make_async_copy(source, target, sem).start()

    buffer = lax.rem(slot, 2)

    @pl.when(slot == 0)
    def _():
        fetch(0, 0)
        blurred_x[WIN * PW :] = jnp.zeros_like(blurred_x[WIN * PW :])
        back_y[WIN * PS :] = jnp.zeros_like(back_y[WIN * PS :])
        back_x[SIDE * PS :] = jnp.zeros_like(back_x[SIDE * PS :])

    @pl.when(slot + 1 < slots)
    def _():
        fetch(slot + 1, 1 - buffer)

    for which, (_, count, to) in enumerate(WINDOWS):
        target = blocks.at[buffer, pl.ds(to, count), mid]
        wait_window(parts, which, pl.ds(0, PADS), target, sems.at[buffer, which])
    for source, target, sem in others(slot, buffer):
        pltpu.make_async_copy(source, target, sem).wait()

    mz, mx, my = mz_ref[0], mx_ref[0], my_ref[0]
    myt, mxt, mzt = myt_ref[0], mxt_ref[0], mzt_ref[0]
    backdrop = backdrops[views[slot]]
    level = logs[views[slot]]

    def along_z(i, carry):
        start = i * CHUNK
        rows = blocks[buffer, pl.ds(start, CHUNK)].reshape(CHUNK * PADW, 128)
        in_z = dot(jnp.concatenate([rows, rows], axis=1), mz)
        high, low = split(in_z)
        z_high[pl.ds(start, CHUNK)] = high.reshape(CHUNK, PADW, 128)
        z_low[pl.ds(start, CHUNK)] = low.reshape(CHUNK, PADW, 128)
        return carry

    lax.fori_loop(0, WIN // CHUNK, along_z, 0, unroll=WIN // CHUNK)

    def along_x_first(i, carry):
        y = 2 * i
        high = jnp.concatenate([z_high[y], z_high[y + 1]], axis=1)
        low = jnp.concatenate([z_low[y], z_low[y + 1]], axis=1)
        in_x = three_term(mx, high, low)
        start = pl.multiple_of(y * PW, 16)
        blurred_x[pl.ds(start, PADW), :] = in_x[:, :128]
        blurred_x[pl.ds(start + PW, PADW), :] = in_x[:, 128:]
        return carry

    lax.fori_loop(0, WIN // 2, along_x_first, 0, unroll=WIN // 2)

    past = jnp.zeros((PADW - WIN, 256), F32)

    def along_y(i, carry):
        u = 2 * i
        lines = [blurred_x[pl.ds(u + j, PADW, stride=PW), :] for j in range(2)]
        predicted = three_term(my, *pair(*lines)) + backdrop
        seen = jnp.concatenate([seen_data[buffer, u], seen_data[buffer, u + 1]], axis=1)
        ratio = jnp.concatenate([seen.astype(F32) / predicted[:WIN], past], axis=0)
        in_y = three_term(myt, *pair(ratio[:, :128], ratio[:, 128:]))
        start = pl.multiple_of(u * PS, 16)
        back_y[pl.ds(start, PADS), :] = in_y[:, :128]
        back_y[pl.ds(start + PS, PADS), :] = in_y[:, 128:]
        return carry

    lax.fori_loop(0, WIN // 2, along_y, 0, unroll=WIN // 2)

    def along_x(i, carry):
        y = 2 * i
        lines = [back_y[pl.ds(y + j, PADW, stride=PS), :] for j in range(2)]
        in_x = three_term(mxt, *pair(*lines))
        start = pl.multiple_of(y * PS, 16)
        back_x[pl.ds(start, PADS), :] = in_x[:, :128]
        back_x[pl.ds(start + PS, PADS), :] = in_x[:, 128:]
        return carry

    lax.fori_loop(0, SIDE // 2, along_x, 0, unroll=SIDE // 2)

    group = 4
    for i in range(SIDE // group):
        lines = [back_x[pl.ds(group * i + j, PADS, stride=PS), :] for j in range(group)]
        high, low = split(jnp.concatenate(lines, axis=0))
        factor = encode(dot(jnp.concatenate([high, low, high], axis=1), mzt), level)
        for j in range(0, group, 2):
            rows = [factor[k * PADS : k * PADS + SIDE] for k in (j, j + 1)]
            out_ref[(group * i + j) // 2, 0] = jnp.concatenate(rows, axis=0).astype(I16)
    for k in range(SIDE // 2, 16):
        out_ref[k, 0] = jnp.zeros_like(out_ref[k, 0])


CHUNK = 29
PEXTRA = 8
SEXTRA = 8
PW = PADW + PEXTRA
PS = PADS + SEXTRA


def run_jobs(channel, parts, scalars, top, bottom, view_data, mats):
    slots = mats[0].shape[0]
    hbm = pl.BlockSpec(memory_space=pltpu.HBM)
    smem = pl.BlockSpec(memory_space=pltpu.SMEM)
    specs = [smem] * len(scalars) + [hbm] * (len(parts) + 3)
    specs += [pl.BlockSpec((1,) + m.shape[1:], lambda slot: (slot, 0, 0)) for m in mats]
    return pl.pallas_call(
        functools.partial(job_kernel, channel),
        grid=(slots,),
        in_specs=specs,
        out_specs=pl.BlockSpec((16, 1, 2 * SIDE, 128), lambda slot: (0, slot, 0, 0)),
        scratch_shapes=[
            pltpu.VMEM((2, WIN, PADW, 128), BF16),
            pltpu.VMEM((2, WIN, WIN, 128), BF16),
            pltpu.VMEM((WIN, PADW, 128), BF16),
            pltpu.VMEM((WIN, PADW, 128), BF16),
            pltpu.VMEM((PADW * PW, 128), F32),
            pltpu.VMEM((PADW * PS, 128), F32),
            pltpu.VMEM((PADS * PS, 128), F32),
            pltpu.SemaphoreType.DMA((2, 6)),
        ],
        out_shape=pltpu.HBM((16, slots, 2 * SIDE, 128), I16),
        compiler_params=pltpu.CompilerParams(vmem_limit_bytes=18 << 20),
        cost_estimate=pl.CostEstimate(
            flops=slots * 20 * 128 * (WIN * PADW * (256 + 192 + 192 + 96) + 2 * SIDE * PADS * 192),
            transcendentals=slots * WIN * PADW * 128,
            bytes_accessed=slots * (2 * WIN * PADW * 128 * 2 + 16 * 2 * SIDE * 128 * 4),
        ),
        name="jobs",
    )(*scalars, *gathered_memory(parts), top, bottom, *far_memory(view_data, *mats))


def bands(taps, positions_out, positions_in):
    offsets = positions_in[None, :] - positions_out[:, None] + HALO
    sel = offsets[None, :, :, None] == jnp.arange(taps.shape[1])[None, None, None, :]
    return jnp.sum(jnp.where(sel, taps[:, None, None, :], 0.0), axis=3)


def high_low(matrix):
    high = lax.reduce_precision(matrix, 8, 7)
    return high.astype(BF16), (matrix - high).astype(BF16)


def job_matrices(taps, bricks):
    none = -1000
    far = 1000
    line = jnp.arange(128)
    row = jnp.arange(PADW)
    win_in = jnp.where(row < WIN, row, none)
    win_out = jnp.where(row < WIN, row, far)
    short = jnp.arange(PADS)
    inner_out = jnp.where(short < SIDE, short + HALO, far)
    x_in = jnp.where(row < RIM + 16, row - 1, row - 5)
    x_in = jnp.where((row >= RIM + 16) & (row < RIM + 20), none, x_in)
    x_in = jnp.where((x_in < 0) | (x_in >= WIN), none, x_in)
    inside = (row >= HALO)[None, :] | (bricks > 0)[:, None]
    inside &= (row < HALO + SIDE)[None, :] | (bricks < RING * RING - 1)[:, None]
    forward = lambda t, out, inp: bands(t, out, inp)
    backward = lambda t, out, inp: jnp.swapaxes(bands(t, inp, out), 1, 2)
    three = lambda pair: jnp.concatenate([pair[0], pair[0], pair[1]], axis=2)
    mz = high_low(jnp.swapaxes(forward(taps[:, 2], line, line), 1, 2))
    mzt = high_low(jnp.swapaxes(backward(taps[:, 2], line, line), 1, 2))
    win_in_far = jnp.where(row < WIN, row, far)
    inner_none = jnp.where(short < SIDE, short + HALO, none)
    return (
        jnp.concatenate(mz, axis=1),
        three(high_low(forward(taps[:, 0], win_out, x_in))),
        three(high_low(jnp.where(inside[:, None, :], forward(taps[:, 1], win_out, win_in), 0.0))),
        three(high_low(backward(taps[:, 1], inner_none, win_in_far))),
        three(high_low(backward(taps[:, 0], inner_none, win_in_far))),
        jnp.concatenate([mzt[0], mzt[0], mzt[1]], axis=1),
    )


MORE = 2.6


def add_kernel(owners, views, logs, *refs):
    total, level = refs[-2:]
    out_ref = refs[-3]
    workers, slots = refs[0].shape[:2]
    jobs = range(workers * slots)
    for b in range(workers):
        level[b] = -200.0
    for i in jobs:
        level[owners[i]] = jnp.maximum(level[owners[i]], logs[views[i]] + MORE)
    for channel, parts_ref in enumerate(refs[:-3]):
        total[...] = jnp.zeros_like(total)
        for i in jobs:
            total[owners[i]] += decode(parts_ref[i // slots, i % slots], logs[views[i]])
        for b in range(workers):
            out_ref[b, channel] = encode(total[b], level[b]).astype(I16)


def add_up(owners, views, logs, parts):
    vmem, smem = pl.BlockSpec(memory_space=pltpu.VMEM), pl.BlockSpec(memory_space=pltpu.SMEM)
    workers, rows = parts[0].shape[0], parts[0].shape[2:]
    return pl.pallas_call(
        add_kernel,
        in_specs=[smem] * 3 + [vmem] * len(parts),
        out_specs=vmem,
        out_shape=pltpu.HBM((workers, len(parts)) + rows, I16),
        scratch_shapes=[pltpu.VMEM((workers,) + rows, F32), pltpu.SMEM((workers,), F32)],
        compiler_params=pltpu.CompilerParams(vmem_limit_bytes=8 << 20),
        name="add_up",
    )(owners, views, logs, *parts)


def update_kernel(met, logs, est_ref, total, out_ref):
    seen, level = jnp.int32(0), jnp.float32(-200.0)
    for v in range(met.shape[0]):
        seen += met[v]
        level = jnp.where(met[v] > 0, jnp.maximum(level, logs[v] + MORE), level)
    seen = seen.astype(F32)
    for c in range(out_ref.shape[0]):
        for k in range(SIDE // 2):
            rows = decode(total[k, c], level)
            for j in range(2):
                part = rows[j * SIDE : (j + 1) * SIDE]
                out_ref[c, 2 * k + j] = est_ref[c, 2 * k + j] * part / seen


def update(met, logs, estimate, total):
    vmem, smem = pl.BlockSpec(memory_space=pltpu.VMEM), pl.BlockSpec(memory_space=pltpu.SMEM)
    return pl.pallas_call(
        update_kernel,
        in_specs=[smem, smem, vmem, vmem],
        out_specs=vmem,
        out_shape=jax.ShapeDtypeStruct(estimate.shape, F32),
        compiler_params=pltpu.CompilerParams(vmem_limit_bytes=12 << 20),
        name="update",
    )(met, logs, estimate, total)


def on_device(estimate, view_data, psf, background, slot_brick, slot_view, intersection):
    me = lax.axis_index("tile").astype(I32).reshape(1)
    groups, workers = lax.axis_size("view"), lax.axis_size("tile")
    upward = [(i, i + 1) for i in range(groups - 1)]
    downward = [(j, i) for i, j in upward]
    bricks, views = slot_brick[0, 0], slot_view[0, 0]
    slots = bricks.shape[0]

    wire = estimate.astype(BF16).transpose(0, 2, 1, 3)
    jobs = lax.optimization_barrier(jnp.concatenate([bricks, views]))
    note = jnp.pad(jobs.astype(BF16)[None, None], ((0, 0), (0, SIDE - 1), (0, 128 - 2 * slots)))
    note = jnp.broadcast_to(note, (wire.shape[0],) + note.shape[1:])
    wire = jnp.concatenate([wire[:, :, :RIM], note[:, :, None], wire[:, :, SIDE - RIM + 1 :]], axis=2)
    rings = ring_whole([wire[0], wire[1]], (0, 1))
    rings[0][1], psf, views = lax.optimization_barrier((rings[0][1], psf, views))
    chosen = views[:, None] == jnp.arange(psf.shape[0])[None, :]
    taps = jnp.sum(jnp.where(chosen[:, :, None, None], psf[None], 0.0), axis=1)
    mats = job_matrices(taps, bricks)
    logs = jnp.log2(jnp.maximum(4.0 / background * jnp.prod(jnp.sum(psf, axis=2), axis=1), 1e-30)) - 15.9
    rings, mats, logs = lax.optimization_barrier((rings, mats, logs))
    rings, view_data, bricks = lax.optimization_barrier((join(rings), view_data, bricks))
    near = ring_near(rings, (1, 0))
    above = lax.ppermute(bricks, "view", downward)
    below = lax.ppermute(bricks, "view", upward)
    data = view_data[0, 0]
    near, data, above, below = lax.optimization_barrier((near, data, above, below))
    gathered = ring_pass_on(near, (1, 0))

    rims = margins(gathered, me, above, below)
    edges = [
        (lax.ppermute(rims[2 * c], "view", upward), lax.ppermute(rims[2 * c + 1], "view", downward))
        for c in range(2)
    ]
    notes = jnp.concatenate([p[::SIDE, RIM, : 2 * slots] for p in gathered[0]], axis=0)
    places = place_of(jnp.arange(workers, dtype=I32), me[0], True)
    match = places[:, None] == jnp.arange(workers)[None, :]
    notes = jnp.sum(jnp.where(match[:, :, None], notes.astype(F32)[None], 0.0), axis=1)
    notes = notes.astype(I32)
    owners, seen_by = notes[:, :slots].reshape(-1), notes[:, slots:].reshape(-1)

    parts = []
    scalars = (me, bricks, views, background, logs)
    for channel in range(2):
        factors = run_jobs(channel, gathered[channel], scalars, *edges[channel], data, mats)
        parts.append(lax.all_to_all(factors, "tile", 0, 0, tiled=True))
    total = lax.all_to_all(add_up(owners, seen_by, logs, parts), "tile", 0, 0, tiled=True)
    return update(intersection[0, 0], logs, estimate, total)


def solution(mesh):
    placed = (
        P(None, "view", "tile", None),
        P("view", "tile", None, None, None, None, None),
        P(),
        P(),
        P("view", "tile", None),
        P("view", "tile", None),
        P("view", "tile", None),
    )
    return jax.shard_map(
        on_device,
        mesh=mesh,
        in_specs=placed,
        out_specs=P(None, "view", "tile", None),
        check_vma=False,
    )
```

```python
import functools

import jax
import jax.numpy as jnp
from jax import lax
from jax.experimental import pallas as pl
from jax.experimental.pallas import tpu as pltpu
from jax.sharding import PartitionSpec as P

F32, BF16, I32, I16 = jnp.float32, jnp.bfloat16, jnp.int32, jnp.int16
HALO = 15
SIDE = 28
WIN = SIDE + 2 * HALO
PADW = 64
PADS = 32
RIM = 16
RING = 4


def far_memory(*arrays):
    return [pltpu.with_memory_space_constraint(a, pltpu.HBM) for a in arrays]


def gathered_memory(parts):
    return far_memory(*parts)


def torus_step(array, dx, dy):
    pairs = [
        (x * RING + y, ((x + dx) % RING) * RING + (y + dy) % RING)
        for x in range(RING)
        for y in range(RING)
    ]
    return lax.ppermute(array, "tile", pairs)


def along(axis, step):
    return (step, 0) if axis == 0 else (0, step)


def ring_near(arrays, axes):
    return [
        [a, torus_step(a, *along(ax, 1)), torus_step(a, *along(ax, -1))]
        for a, ax in zip(arrays, axes)
    ]


def ring_whole(arrays, axes):
    return [
        [a] + [torus_step(a, *along(ax, d)) for d in (1, -1, 2)] for a, ax in zip(arrays, axes)
    ]


def join_kernel(*refs):
    stage, sems, refs = refs[-2], refs[-1], refs[:-2]
    outs, refs = refs[-2:], refs[:-2]
    each = len(refs) // len(outs)
    rows = refs[0].shape[0]
    ins = []
    for i, ref in enumerate(refs):
        target = stage.at[i // each, pl.ds(i % each * rows, rows)]
        ins.append(pltpu.make_async_copy(ref, target, sems.at[i]))
        ins[i].start()
    sends = []
    for i, out in enumerate(outs):
        for copy in ins[i * each : (i + 1) * each]:
            copy.wait()
        sends.append(pltpu.make_async_copy(stage.at[i], out, sems.at[len(refs) + i]))
        sends[i].start()
    for send in sends:
        send.wait()


def join(rings):
    arrays = [a for ring in rings for a in ring]
    whole = (len(rings[0]) * arrays[0].shape[0],) + arrays[0].shape[1:]
    return pl.pallas_call(
        join_kernel,
        in_specs=[pl.BlockSpec(memory_space=pl.ANY)] * len(arrays),
        out_specs=[pl.BlockSpec(memory_space=pltpu.HBM)] * len(rings),
        out_shape=[pltpu.HBM(whole, BF16)] * len(rings),
        scratch_shapes=[
            pltpu.VMEM((len(rings),) + whole, BF16),
            pltpu.SemaphoreType.DMA((len(arrays) + len(rings),)),
        ],
        compiler_params=pltpu.CompilerParams(vmem_limit_bytes=4 << 20),
        name="join",
    )(*arrays)


def halves_kernel(*refs):
    stage, sems, refs = refs[-2], refs[-1], refs[:-2]
    count = len(refs) // 2
    ins, outs = [], []
    for i in range(count):
        half = refs[i].shape[0] // 2
        source = refs[i].at[pl.ds(0 if i % 2 == 0 else half, half)]
        ins.append(pltpu.make_async_copy(source, stage.at[i], sems.at[i, 0]))
        outs.append(pltpu.make_async_copy(stage.at[i], refs[count + i], sems.at[i, 1]))
        ins[i].start()
    for i in range(count):
        ins[i].wait()
        outs[i].start()
    for i in range(count):
        outs[i].wait()


def take_halves(near):
    arrays = [a for _, lower, upper in near for a in (lower, upper)]
    anywhere = pl.BlockSpec(memory_space=pl.ANY)
    shape = arrays[0].shape
    taken = pl.pallas_call(
        halves_kernel,
        in_specs=[anywhere] * len(arrays),
        out_specs=[anywhere] * len(arrays),
        out_shape=[pltpu.HBM((shape[0] // 2,) + shape[1:], BF16)] * len(arrays),
        scratch_shapes=[
            pltpu.VMEM((len(arrays), shape[0] // 2) + shape[1:], BF16),
            pltpu.SemaphoreType.DMA((len(arrays), 2)),
        ],
        compiler_params=pltpu.CompilerParams(vmem_limit_bytes=4 << 20),
        name="halves",
    )(*arrays)
    return [(taken[2 * i], taken[2 * i + 1]) for i in range(len(near))]


def ring_pass_on(near, axes):
    return [
        [*n, torus_step(low, *along(ax, 1)), torus_step(high, *along(ax, -1))]
        for n, (low, high), ax in zip(near, take_halves(near), axes)
    ]


def rank(delta):
    delta = lax.rem(delta + RING, RING)
    return jnp.where(delta == 3, 1, jnp.where(delta == 1, 2, jnp.where(delta == 2, 3, 0)))


def place_of(brick, me, x_first):
    in_x = rank(lax.div(brick, RING) - lax.div(me, RING))
    in_y = rank(lax.rem(brick, RING) - lax.rem(me, RING))
    return in_y * RING + in_x if x_first else in_x * RING + in_y


def window_place(which, brick, me, x_first):
    return place_of(jnp.clip(brick + which - 1, 0, RING * RING - 1), me, x_first)


WINDOWS = ((SIDE - HALO, HALO, 0), (0, SIDE, HALO), (0, HALO, HALO + SIDE))


def copy_window(parts, which, place, rows, target, sem):
    first, count, _ = WINDOWS[which]
    base = 0
    for part in parts:
        held = part.shape[0] // SIDE

        @pl.when((place >= base) & (place < base + held))
        def _(part=part, base=base):
            source = part.at[pl.ds((place - base) * SIDE + first, count), rows]
            pltpu.make_async_copy(source, target, sem).start()

        base += held


def wait_window(parts, which, rows, target, sem):
    count = WINDOWS[which][1]
    pltpu.make_async_copy(parts[0].at[pl.ds(0, count), rows], target, sem).wait()


def margin_kernel(*refs):
    me, *asked = refs[:3]
    refs = refs[3:]
    refs, (stage, sems) = refs[:-2], refs[-2:]
    gathered, outs = (refs[:PARTS], refs[PARTS : 2 * PARTS]), refs[2 * PARTS :]
    slots = outs[0].shape[0]
    copies = []
    for channel, parts in enumerate(gathered):
        for side in range(2):
            rows = pl.ds(RIM, RIM) if side == 0 else pl.ds(0, RIM)
            for slot in range(slots):
                item = side * slots + slot
                waits = []
                for which, (_, count, to) in enumerate(WINDOWS):
                    target = stage.at[channel, item, pl.ds(to, count)]
                    sem = sems.at[channel, item, which]
                    place = window_place(which, asked[side][slot], me[0], channel == 0)
                    copy_window(parts, which, place, rows, target, sem)
                    waits.append((parts, which, rows, target, sem))
                out = pltpu.make_async_copy(
                    stage.at[channel, item],
                    outs[2 * channel + side].at[slot],
                    sems.at[channel, item, 3],
                )
                copies.append((waits, out))
    for waits, out in copies:
        for item in waits:
            wait_window(*item)
        out.start()
    for _, out in copies:
        out.wait()


PARTS = 5


def margins(gathered, me, above, below):
    slots = above.shape[0]
    hbm, smem = pl.BlockSpec(memory_space=pltpu.HBM), pl.BlockSpec(memory_space=pltpu.SMEM)
    return pl.pallas_call(
        margin_kernel,
        in_specs=[smem] * 3 + [hbm] * (2 * PARTS),
        out_specs=[hbm] * 4,
        out_shape=[pltpu.HBM((slots, WIN, RIM, 128), BF16)] * 4,
        scratch_shapes=[
            pltpu.VMEM((2, 2 * slots, WIN, RIM, 128), BF16),
            pltpu.SemaphoreType.DMA((2, 2 * slots, 4)),
        ],
        compiler_params=pltpu.CompilerParams(vmem_limit_bytes=4 << 20),
        name="margins",
    )(me, above, below, *gathered_memory(gathered[0]), *gathered_memory(gathered[1]))


def split(value):
    high = value.astype(BF16)
    low = (value - high.astype(F32)).astype(BF16)
    return high, low


def pair(first, second):
    (h0, l0), (h1, l1) = split(first), split(second)
    return jnp.concatenate([h0, h1], axis=1), jnp.concatenate([l0, l1], axis=1)


def three_term(matrix, high, low):
    return dot(matrix, jnp.concatenate([high, low, high], axis=0))


STEPS = 2048.0


def encode(value, level):
    code = (jnp.log2(jnp.maximum(value, 1e-37)) - level) * STEPS
    return jnp.round(jnp.clip(code, -32767.0, 32767.0)).astype(I32)


def decode(code, level):
    return jnp.exp2(code.astype(I32).astype(F32) * (1.0 / STEPS) + level)


def dot(a, b):
    return jnp.dot(a, b, preferred_element_type=F32)


def job_kernel(channel, me, bricks, views, backdrops, logs, *refs):
    if channel:
        refs = refs[1:]
    parts, refs = refs[:PARTS], refs[PARTS:]
    top_ref, bottom_ref, data_ref, mz_ref, mx_ref, my_ref, myt_ref, mxt_ref, mzt_ref, out_ref = refs[:10]
    blocks, seen_data, z_high, z_low, blurred_x, back_y, back_x, sems = refs[10:]
    slot, slots = pl.program_id(0), pl.num_programs(0)
    mid = pl.ds(RIM, PADS)

    def others(which_slot, buffer):
        span = pl.ds(0, WIN)
        return (
            (top_ref.at[which_slot], blocks.at[buffer, span, pl.ds(0, RIM)], sems.at[buffer, 3]),
            (bottom_ref.at[which_slot], blocks.at[buffer, span, pl.ds(RIM + PADS, RIM)], sems.at[buffer, 4]),
            (data_ref.at[which_slot, channel], seen_data.at[buffer], sems.at[buffer, 5]),
        )

    def fetch(which_slot, buffer):
        for which, (_, count, to) in enumerate(WINDOWS):
            target = blocks.at[buffer, pl.ds(to, count), mid]
            place = window_place(which, bricks[which_slot], me[0], channel == 0)
            copy_window(parts, which, place, pl.ds(0, PADS), target, sems.at[buffer, which])
        for source, target, sem in others(which_slot, buffer):
            pltpu.make_async_copy(source, target, sem).start()

    buffer = lax.rem(slot, 2)

    @pl.when(slot == 0)
    def _():
        fetch(0, 0)
        blurred_x[WIN * PW :] = jnp.zeros_like(blurred_x[WIN * PW :])
        back_y[WIN * PS :] = jnp.zeros_like(back_y[WIN * PS :])
        back_x[SIDE * PS :] = jnp.zeros_like(back_x[SIDE * PS :])

    @pl.when(slot + 1 < slots)
    def _():
        fetch(slot + 1, 1 - buffer)

    for which, (_, count, to) in enumerate(WINDOWS):
        target = blocks.at[buffer, pl.ds(to, count), mid]
        wait_window(parts, which, pl.ds(0, PADS), target, sems.at[buffer, which])
    for source, target, sem in others(slot, buffer):
        pltpu.make_async_copy(source, target, sem).wait()

    mz, mx, my = mz_ref[0], mx_ref[0], my_ref[0]
    myt, mxt, mzt = myt_ref[0], mxt_ref[0], mzt_ref[0]
    backdrop = backdrops[views[slot]]
    level = logs[views[slot]]

    def along_z(i, carry):
        start = i * CHUNK
        rows = blocks[buffer, pl.ds(start, CHUNK)].reshape(CHUNK * PADW, 128)
        in_z = dot(jnp.concatenate([rows, rows], axis=1), mz)
        high, low = split(in_z)
        z_high[pl.ds(start, CHUNK)] = high.reshape(CHUNK, PADW, 128)
        z_low[pl.ds(start, CHUNK)] = low.reshape(CHUNK, PADW, 128)
        return carry

    lax.fori_loop(0, WIN // CHUNK, along_z, 0, unroll=WIN // CHUNK)

    def along_x_first(i, carry):
        y = 2 * i
        high = jnp.concatenate([z_high[y], z_high[y + 1]], axis=1)
        low = jnp.concatenate([z_low[y], z_low[y + 1]], axis=1)
        in_x = three_term(mx, high, low)
        start = pl.multiple_of(y * PW, 16)
        blurred_x[pl.ds(start, PADW), :] = in_x[:, :128]
        blurred_x[pl.ds(start + PW, PADW), :] = in_x[:, 128:]
        return carry

    lax.fori_loop(0, WIN // 2, along_x_first, 0, unroll=WIN // 2)

    past = jnp.zeros((PADW - WIN, 256), F32)

    def along_y(i, carry):
        u = 2 * i
        lines = [blurred_x[pl.ds(u + j, PADW, stride=PW), :] for j in range(2)]
        predicted = three_term(my, *pair(*lines)) + backdrop
        seen = jnp.concatenate([seen_data[buffer, u], seen_data[buffer, u + 1]], axis=1)
        ratio = jnp.concatenate([seen.astype(F32) / predicted[:WIN], past], axis=0)
        in_y = three_term(myt, *pair(ratio[:, :128], ratio[:, 128:]))
        start = pl.multiple_of(u * PS, 16)
        back_y[pl.ds(start, PADS), :] = in_y[:, :128]
        back_y[pl.ds(start + PS, PADS), :] = in_y[:, 128:]
        return carry

    lax.fori_loop(0, WIN // 2, along_y, 0, unroll=WIN // 2)

    def along_x(i, carry):
        y = 2 * i
        lines = [back_y[pl.ds(y + j, PADW, stride=PS), :] for j in range(2)]
        in_x = three_term(mxt, *pair(*lines))
        start = pl.multiple_of(y * PS, 16)
        back_x[pl.ds(start, PADS), :] = in_x[:, :128]
        back_x[pl.ds(start + PS, PADS), :] = in_x[:, 128:]
        return carry

    lax.fori_loop(0, SIDE // 2, along_x, 0, unroll=SIDE // 2)

    group = 4
    for i in range(SIDE // group):
        lines = [back_x[pl.ds(group * i + j, PADS, stride=PS), :] for j in range(group)]
        high, low = split(jnp.concatenate(lines, axis=0))
        factor = encode(dot(jnp.concatenate([high, low, high], axis=1), mzt), level)
        for j in range(0, group, 2):
            rows = [factor[k * PADS : k * PADS + SIDE] for k in (j, j + 1)]
            out_ref[(group * i + j) // 2, 0, 0] = jnp.concatenate(rows, axis=0).astype(I16)
    for k in range(SIDE // 2, 16):
        out_ref[k, 0, 0] = jnp.zeros_like(out_ref[k, 0, 0])


CHUNK = 29
PEXTRA = 8
SEXTRA = 8
PW = PADW + PEXTRA
PS = PADS + SEXTRA


def run_jobs(channel, before, parts, scalars, top, bottom, view_data, mats):
    slots = mats[0].shape[0]
    hbm = pl.BlockSpec(memory_space=pltpu.HBM)
    smem = pl.BlockSpec(memory_space=pltpu.SMEM)
    specs = [smem] * len(scalars) + [hbm] * (len(before) + len(parts) + 3)
    specs += [pl.BlockSpec((1,) + m.shape[1:], lambda slot: (slot, 0, 0)) for m in mats]
    return pl.pallas_call(
        functools.partial(job_kernel, channel),
        grid=(slots,),
        in_specs=specs,
        out_specs=pl.BlockSpec(
            (16, 1, 1, 2 * SIDE, 128), lambda slot: (0, channel, slot, 0, 0)
        ),
        input_output_aliases={len(scalars): 0} if before else {},
        scratch_shapes=[
            pltpu.VMEM((2, WIN, PADW, 128), BF16),
            pltpu.VMEM((2, WIN, WIN, 128), BF16),
            pltpu.VMEM((WIN, PADW, 128), BF16),
            pltpu.VMEM((WIN, PADW, 128), BF16),
            pltpu.VMEM((PADW * PW, 128), F32),
            pltpu.VMEM((PADW * PS, 128), F32),
            pltpu.VMEM((PADS * PS, 128), F32),
            pltpu.SemaphoreType.DMA((2, 6)),
        ],
        out_shape=pltpu.HBM((16, 2, slots, 2 * SIDE, 128), I16),
        compiler_params=pltpu.CompilerParams(vmem_limit_bytes=18 << 20),
        cost_estimate=pl.CostEstimate(
            flops=slots * 20 * 128 * (WIN * PADW * (256 + 192 + 192 + 96) + 2 * SIDE * PADS * 192),
            transcendentals=slots * WIN * PADW * 128,
            bytes_accessed=slots * (2 * WIN * PADW * 128 * 2 + 16 * 2 * SIDE * 128 * 4),
        ),
        name="jobs",
    )(*scalars, *before, *gathered_memory(parts), top, bottom, *far_memory(view_data, *mats))


def bands(taps, positions_out, positions_in):
    offsets = positions_in[None, :] - positions_out[:, None] + HALO
    sel = offsets[None, :, :, None] == jnp.arange(taps.shape[1])[None, None, None, :]
    return jnp.sum(jnp.where(sel, taps[:, None, None, :], 0.0), axis=3)


def high_low(matrix):
    high = lax.reduce_precision(matrix, 8, 7)
    return high.astype(BF16), (matrix - high).astype(BF16)


def job_matrices(taps, bricks):
    none = -1000
    far = 1000
    line = jnp.arange(128)
    row = jnp.arange(PADW)
    win_in = jnp.where(row < WIN, row, none)
    win_out = jnp.where(row < WIN, row, far)
    short = jnp.arange(PADS)
    inner_out = jnp.where(short < SIDE, short + HALO, far)
    x_in = jnp.where(row < RIM + 16, row - 1, row - 5)
    x_in = jnp.where((row >= RIM + 16) & (row < RIM + 20), none, x_in)
    x_in = jnp.where((x_in < 0) | (x_in >= WIN), none, x_in)
    inside = (row >= HALO)[None, :] | (bricks > 0)[:, None]
    inside &= (row < HALO + SIDE)[None, :] | (bricks < RING * RING - 1)[:, None]
    forward = lambda t, out, inp: bands(t, out, inp)
    backward = lambda t, out, inp: jnp.swapaxes(bands(t, inp, out), 1, 2)
    three = lambda pair: jnp.concatenate([pair[0], pair[0], pair[1]], axis=2)
    mz = high_low(jnp.swapaxes(forward(taps[:, 2], line, line), 1, 2))
    mzt = high_low(jnp.swapaxes(backward(taps[:, 2], line, line), 1, 2))
    win_in_far = jnp.where(row < WIN, row, far)
    inner_none = jnp.where(short < SIDE, short + HALO, none)
    return (
        jnp.concatenate(mz, axis=1),
        three(high_low(forward(taps[:, 0], win_out, x_in))),
        three(high_low(jnp.where(inside[:, None, :], forward(taps[:, 1], win_out, win_in), 0.0))),
        three(high_low(backward(taps[:, 1], inner_none, win_in_far))),
        three(high_low(backward(taps[:, 0], inner_none, win_in_far))),
        jnp.concatenate([mzt[0], mzt[0], mzt[1]], axis=1),
    )


MORE = 2.6


def add_kernel(owners, views, logs, *refs):
    total, level = refs[-2:]
    out_ref = refs[-3]
    parts_ref = refs[0]
    workers, channels, slots = parts_ref.shape[:3]
    jobs = range(workers * slots)
    for b in range(workers):
        level[b] = -200.0
    for i in jobs:
        level[owners[i]] = jnp.maximum(level[owners[i]], logs[views[i]] + MORE)
    for channel in range(channels):
        total[...] = jnp.zeros_like(total)
        for i in jobs:
            total[owners[i]] += decode(parts_ref[i // slots, channel, i % slots], logs[views[i]])
        for b in range(workers):
            out_ref[b, channel] = encode(total[b], level[b]).astype(I16)


def add_up(owners, views, logs, parts):
    vmem, smem = pl.BlockSpec(memory_space=pltpu.VMEM), pl.BlockSpec(memory_space=pltpu.SMEM)
    workers, channels, _, *rows = parts.shape
    rows = tuple(rows)
    return pl.pallas_call(
        add_kernel,
        in_specs=[smem] * 3 + [vmem],
        out_specs=vmem,
        out_shape=pltpu.HBM((workers, channels) + rows, I16),
        scratch_shapes=[pltpu.VMEM((workers,) + rows, F32), pltpu.SMEM((workers,), F32)],
        compiler_params=pltpu.CompilerParams(vmem_limit_bytes=8 << 20),
        name="add_up",
    )(owners, views, logs, parts)


def update_kernel(met, logs, est_ref, total, out_ref):
    seen, level = jnp.int32(0), jnp.float32(-200.0)
    for v in range(met.shape[0]):
        seen += met[v]
        level = jnp.where(met[v] > 0, jnp.maximum(level, logs[v] + MORE), level)
    seen = seen.astype(F32)
    for c in range(out_ref.shape[0]):
        for k in range(SIDE // 2):
            rows = decode(total[k, c], level)
            for j in range(2):
                part = rows[j * SIDE : (j + 1) * SIDE]
                out_ref[c, 2 * k + j] = est_ref[c, 2 * k + j] * part / seen


def update(met, logs, estimate, total):
    vmem, smem = pl.BlockSpec(memory_space=pltpu.VMEM), pl.BlockSpec(memory_space=pltpu.SMEM)
    return pl.pallas_call(
        update_kernel,
        in_specs=[smem, smem, vmem, vmem],
        out_specs=vmem,
        out_shape=jax.ShapeDtypeStruct(estimate.shape, F32),
        compiler_params=pltpu.CompilerParams(vmem_limit_bytes=12 << 20),
        name="update",
    )(met, logs, estimate, total)


def on_device(estimate, view_data, psf, background, slot_brick, slot_view, intersection):
    me = lax.axis_index("tile").astype(I32).reshape(1)
    groups, workers = lax.axis_size("view"), lax.axis_size("tile")
    upward = [(i, i + 1) for i in range(groups - 1)]
    downward = [(j, i) for i, j in upward]
    bricks, views = slot_brick[0, 0], slot_view[0, 0]
    slots = bricks.shape[0]

    wire = estimate.astype(BF16).transpose(0, 2, 1, 3)
    jobs = lax.optimization_barrier(jnp.concatenate([bricks, views]))
    note = jnp.pad(jobs.astype(BF16)[None, None], ((0, 0), (0, SIDE - 1), (0, 128 - 2 * slots)))
    note = jnp.broadcast_to(note, (wire.shape[0],) + note.shape[1:])
    wire = jnp.concatenate([wire[:, :, :RIM], note[:, :, None], wire[:, :, SIDE - RIM + 1 :]], axis=2)
    rings = ring_whole([wire[0], wire[1]], (0, 1))
    rings[0][1], psf, views = lax.optimization_barrier((rings[0][1], psf, views))
    chosen = views[:, None] == jnp.arange(psf.shape[0])[None, :]
    taps = jnp.sum(jnp.where(chosen[:, :, None, None], psf[None], 0.0), axis=1)
    mats = job_matrices(taps, bricks)
    logs = jnp.log2(jnp.maximum(4.0 / background * jnp.prod(jnp.sum(psf, axis=2), axis=1), 1e-30)) - 15.9
    rings, mats, logs = lax.optimization_barrier((rings, mats, logs))
    rings, view_data, bricks = lax.optimization_barrier((join(rings), view_data, bricks))
    near = ring_near(rings, (1, 0))
    above = lax.ppermute(bricks, "view", downward)
    below = lax.ppermute(bricks, "view", upward)
    data = view_data[0, 0]
    near, data, above, below = lax.optimization_barrier((near, data, above, below))
    gathered = ring_pass_on(near, (1, 0))

    rims = margins(gathered, me, above, below)
    edges = [
        (lax.ppermute(rims[2 * c], "view", upward), lax.ppermute(rims[2 * c + 1], "view", downward))
        for c in range(2)
    ]
    notes = jnp.concatenate([p[::SIDE, RIM, : 2 * slots] for p in gathered[0]], axis=0)
    places = place_of(jnp.arange(workers, dtype=I32), me[0], True)
    match = places[:, None] == jnp.arange(workers)[None, :]
    notes = jnp.sum(jnp.where(match[:, :, None], notes.astype(F32)[None], 0.0), axis=1)
    notes = notes.astype(I32)
    owners, seen_by = notes[:, :slots].reshape(-1), notes[:, slots:].reshape(-1)

    factors = []
    scalars = (me, bricks, views, background, logs)
    for channel in range(2):
        factors = [
            run_jobs(
                channel, factors, gathered[channel], scalars, *edges[channel], data, mats
            )
        ]
    parts = lax.all_to_all(factors[0], "tile", 0, 0, tiled=True)
    total = lax.all_to_all(add_up(owners, seen_by, logs, parts), "tile", 0, 0, tiled=True)
    return update(intersection[0, 0], logs, estimate, total)


def solution(mesh):
    placed = (
        P(None, "view", "tile", None),
        P("view", "tile", None, None, None, None, None),
        P(),
        P(),
        P("view", "tile", None),
        P("view", "tile", None),
        P("view", "tile", None),
    )
    return jax.shard_map(
        on_device,
        mesh=mesh,
        in_specs=placed,
        out_specs=P(None, "view", "tile", None),
        check_vma=False,
    )
```

```python
import functools

import jax
import jax.numpy as jnp
from jax import lax
from jax.experimental import pallas as pl
from jax.experimental.pallas import tpu as pltpu
from jax.sharding import PartitionSpec as P

F32, BF16, I32, I16 = jnp.float32, jnp.bfloat16, jnp.int32, jnp.int16
HALO = 15
SIDE = 28
WIN = SIDE + 2 * HALO
PADW = 64
PADS = 32
RIM = 16
RING = 4


def far_memory(*arrays):
    return [pltpu.with_memory_space_constraint(a, pltpu.HBM) for a in arrays]


def gathered_memory(parts):
    return far_memory(*parts)


def torus_step(array, dx, dy):
    pairs = [
        (x * RING + y, ((x + dx) % RING) * RING + (y + dy) % RING)
        for x in range(RING)
        for y in range(RING)
    ]
    return lax.ppermute(array, "tile", pairs)


def along(axis, step):
    return (step, 0) if axis == 0 else (0, step)


def ring_near(arrays, axes):
    return [
        [a, torus_step(a, *along(ax, 1)), torus_step(a, *along(ax, -1))]
        for a, ax in zip(arrays, axes)
    ]


def ring_whole(arrays, axes):
    return [
        [a] + [torus_step(a, *along(ax, d)) for d in (1, -1, 2)] for a, ax in zip(arrays, axes)
    ]


def join_kernel(*refs):
    sems, refs = refs[-1], refs[:-1]
    outs, refs = refs[-2:], refs[:-2]
    each = len(refs) // len(outs)
    rows = refs[0].shape[0]
    copies = []
    for i, ref in enumerate(refs):
        target = outs[i // each].at[pl.ds(i % each * rows, rows)]
        copies.append(pltpu.make_async_copy(ref, target, sems.at[i]))
        copies[i].start()
    for copy in copies:
        copy.wait()


def join(rings):
    arrays = [a for ring in rings for a in ring]
    whole = (len(rings[0]) * arrays[0].shape[0],) + arrays[0].shape[1:]
    return pl.pallas_call(
        join_kernel,
        in_specs=[pl.BlockSpec(memory_space=pl.ANY)] * len(arrays),
        out_specs=[pl.BlockSpec(memory_space=pltpu.HBM)] * len(rings),
        out_shape=[pltpu.HBM(whole, BF16)] * len(rings),
        scratch_shapes=[pltpu.SemaphoreType.DMA((len(arrays),))],
        compiler_params=pltpu.CompilerParams(vmem_limit_bytes=1 << 20),
        name="join",
    )(*arrays)


def halves_kernel(*refs):
    sems, refs = refs[-1], refs[:-1]
    count = len(refs) // 2
    copies = []
    for i in range(count):
        half = refs[i].shape[0] // 2
        source = refs[i].at[pl.ds(0 if i % 2 == 0 else half, half)]
        copies.append(pltpu.make_async_copy(source, refs[count + i], sems.at[i]))
        copies[i].start()
    for copy in copies:
        copy.wait()


def take_halves(near):
    arrays = [a for _, lower, upper in near for a in (lower, upper)]
    anywhere = pl.BlockSpec(memory_space=pl.ANY)
    shape = arrays[0].shape
    taken = pl.pallas_call(
        halves_kernel,
        in_specs=[anywhere] * len(arrays),
        out_specs=[anywhere] * len(arrays),
        out_shape=[pltpu.HBM((shape[0] // 2,) + shape[1:], BF16)] * len(arrays),
        scratch_shapes=[pltpu.SemaphoreType.DMA((len(arrays),))],
        compiler_params=pltpu.CompilerParams(vmem_limit_bytes=1 << 20),
        name="halves",
    )(*arrays)
    return [(taken[2 * i], taken[2 * i + 1]) for i in range(len(near))]


def ring_pass_on(near, axes):
    return [
        [*n, torus_step(low, *along(ax, 1)), torus_step(high, *along(ax, -1))]
        for n, (low, high), ax in zip(near, take_halves(near), axes)
    ]


def rank(delta):
    delta = lax.rem(delta + RING, RING)
    return jnp.where(delta == 3, 1, jnp.where(delta == 1, 2, jnp.where(delta == 2, 3, 0)))


def place_of(brick, me, x_first):
    in_x = rank(lax.div(brick, RING) - lax.div(me, RING))
    in_y = rank(lax.rem(brick, RING) - lax.rem(me, RING))
    return in_y * RING + in_x if x_first else in_x * RING + in_y


def window_place(which, brick, me, x_first):
    return place_of(jnp.clip(brick + which - 1, 0, RING * RING - 1), me, x_first)


WINDOWS = ((SIDE - HALO, HALO, 0), (0, SIDE, HALO), (0, HALO, HALO + SIDE))


def copy_window(parts, which, place, rows, target, sem):
    first, count, _ = WINDOWS[which]
    base = 0
    for part in parts:
        held = part.shape[0] // SIDE

        @pl.when((place >= base) & (place < base + held))
        def _(part=part, base=base):
            source = part.at[pl.ds((place - base) * SIDE + first, count), rows]
            pltpu.make_async_copy(source, target, sem).start()

        base += held


def wait_window(parts, which, rows, target, sem):
    count = WINDOWS[which][1]
    pltpu.make_async_copy(parts[0].at[pl.ds(0, count), rows], target, sem).wait()


def margin_kernel(*refs):
    me, *asked = refs[:3]
    refs = refs[3:]
    refs, (stage, sems) = refs[:-2], refs[-2:]
    gathered, outs = (refs[:PARTS], refs[PARTS : 2 * PARTS]), refs[2 * PARTS :]
    slots = outs[0].shape[0]
    copies = []
    for channel, parts in enumerate(gathered):
        for side in range(2):
            rows = pl.ds(RIM, RIM) if side == 0 else pl.ds(0, RIM)
            for slot in range(slots):
                item = side * slots + slot
                waits = []
                for which, (_, count, to) in enumerate(WINDOWS):
                    target = stage.at[channel, item, pl.ds(to, count)]
                    sem = sems.at[channel, item, which]
                    place = window_place(which, asked[side][slot], me[0], channel == 0)
                    copy_window(parts, which, place, rows, target, sem)
                    waits.append((parts, which, rows, target, sem))
                out = pltpu.make_async_copy(
                    stage.at[channel, item],
                    outs[2 * channel + side].at[slot],
                    sems.at[channel, item, 3],
                )
                copies.append((waits, out))
    for waits, out in copies:
        for item in waits:
            wait_window(*item)
        out.start()
    for _, out in copies:
        out.wait()


PARTS = 5


def margins(gathered, me, above, below):
    slots = above.shape[0]
    hbm, smem = pl.BlockSpec(memory_space=pltpu.HBM), pl.BlockSpec(memory_space=pltpu.SMEM)
    return pl.pallas_call(
        margin_kernel,
        in_specs=[smem] * 3 + [hbm] * (2 * PARTS),
        out_specs=[hbm] * 4,
        out_shape=[pltpu.HBM((slots, WIN, RIM, 128), BF16)] * 4,
        scratch_shapes=[
            pltpu.VMEM((2, 2 * slots, WIN, RIM, 128), BF16),
            pltpu.SemaphoreType.DMA((2, 2 * slots, 4)),
        ],
        compiler_params=pltpu.CompilerParams(vmem_limit_bytes=4 << 20),
        name="margins",
    )(me, above, below, *gathered_memory(gathered[0]), *gathered_memory(gathered[1]))


def split(value):
    high = value.astype(BF16)
    low = (value - high.astype(F32)).astype(BF16)
    return high, low


def pair(first, second):
    (h0, l0), (h1, l1) = split(first), split(second)
    return jnp.concatenate([h0, h1], axis=1), jnp.concatenate([l0, l1], axis=1)


def three_term(matrix, high, low):
    return dot(matrix, jnp.concatenate([high, low, high], axis=0))


STEPS = 2048.0


def encode(value, level):
    code = (jnp.log2(jnp.maximum(value, 1e-37)) - level) * STEPS
    return jnp.round(jnp.clip(code, -32767.0, 32767.0)).astype(I32)


def decode(code, level):
    return jnp.exp2(code.astype(I32).astype(F32) * (1.0 / STEPS) + level)


def dot(a, b):
    return jnp.dot(a, b, preferred_element_type=F32)


def job_kernel(channel, me, bricks, views, backdrops, logs, *refs):
    parts, refs = refs[:PARTS], refs[PARTS:]
    top_ref, bottom_ref, data_ref, mz_ref, mx_ref, my_ref, myt_ref, mxt_ref, mzt_ref, out_ref = refs[:10]
    blocks, seen_data, z_high, z_low, blurred_x, back_y, back_x, sems = refs[10:]
    slot, slots = pl.program_id(0), pl.num_programs(0)
    mid = pl.ds(RIM, PADS)

    def others(which_slot, buffer):
        span = pl.ds(0, WIN)
        return (
            (top_ref.at[which_slot], blocks.at[buffer, span, pl.ds(0, RIM)], sems.at[buffer, 3]),
            (bottom_ref.at[which_slot], blocks.at[buffer, span, pl.ds(RIM + PADS, RIM)], sems.at[buffer, 4]),
            (data_ref.at[which_slot, channel], seen_data.at[buffer], sems.at[buffer, 5]),
        )

    def fetch(which_slot, buffer):
        for which, (_, count, to) in enumerate(WINDOWS):
            target = blocks.at[buffer, pl.ds(to, count), mid]
            place = window_place(which, bricks[which_slot], me[0], channel == 0)
            copy_window(parts, which, place, pl.ds(0, PADS), target, sems.at[buffer, which])
        for source, target, sem in others(which_slot, buffer):
            pltpu.make_async_copy(source, target, sem).start()

    buffer = lax.rem(slot, 2)

    @pl.when(slot == 0)
    def _():
        fetch(0, 0)
        blurred_x[WIN * PW :] = jnp.zeros_like(blurred_x[WIN * PW :])
        back_y[WIN * PS :] = jnp.zeros_like(back_y[WIN * PS :])
        back_x[SIDE * PS :] = jnp.zeros_like(back_x[SIDE * PS :])

    @pl.when(slot + 1 < slots)
    def _():
        fetch(slot + 1, 1 - buffer)

    for which, (_, count, to) in enumerate(WINDOWS):
        target = blocks.at[buffer, pl.ds(to, count), mid]
        wait_window(parts, which, pl.ds(0, PADS), target, sems.at[buffer, which])
    for source, target, sem in others(slot, buffer):
        pltpu.make_async_copy(source, target, sem).wait()

    mz, mx, my = mz_ref[0], mx_ref[0], my_ref[0]
    myt, mxt, mzt = myt_ref[0], mxt_ref[0], mzt_ref[0]
    backdrop = backdrops[views[slot]]
    level = logs[views[slot]]

    def along_z(i, carry):
        start = i * CHUNK
        rows = blocks[buffer, pl.ds(start, CHUNK)].reshape(CHUNK * PADW, 128)
        in_z = dot(jnp.concatenate([rows, rows], axis=1), mz)
        high, low = split(in_z)
        z_high[pl.ds(start, CHUNK)] = high.reshape(CHUNK, PADW, 128)
        z_low[pl.ds(start, CHUNK)] = low.reshape(CHUNK, PADW, 128)
        return carry

    lax.fori_loop(0, WIN // CHUNK, along_z, 0, unroll=WIN // CHUNK)

    def along_x_first(i, carry):
        y = 2 * i
        high = jnp.concatenate([z_high[y], z_high[y + 1]], axis=1)
        low = jnp.concatenate([z_low[y], z_low[y + 1]], axis=1)
        in_x = three_term(mx, high, low)
        start = pl.multiple_of(y * PW, 16)
        blurred_x[pl.ds(start, PADW), :] = in_x[:, :128]
        blurred_x[pl.ds(start + PW, PADW), :] = in_x[:, 128:]
        return carry

    lax.fori_loop(0, WIN // 2, along_x_first, 0, unroll=WIN // 2)

    past = jnp.zeros((PADW - WIN, 256), F32)

    def along_y(i, carry):
        u = 2 * i
        lines = [blurred_x[pl.ds(u + j, PADW, stride=PW), :] for j in range(2)]
        predicted = three_term(my, *pair(*lines)) + backdrop
        seen = jnp.concatenate([seen_data[buffer, u], seen_data[buffer, u + 1]], axis=1)
        ratio = jnp.concatenate([seen.astype(F32) / predicted[:WIN], past], axis=0)
        in_y = three_term(myt, *pair(ratio[:, :128], ratio[:, 128:]))
        start = pl.multiple_of(u * PS, 16)
        back_y[pl.ds(start, PADS), :] = in_y[:, :128]
        back_y[pl.ds(start + PS, PADS), :] = in_y[:, 128:]
        return carry

    lax.fori_loop(0, WIN // 2, along_y, 0, unroll=WIN // 2)

    def along_x(i, carry):
        y = 2 * i
        lines = [back_y[pl.ds(y + j, PADW, stride=PS), :] for j in range(2)]
        in_x = three_term(mxt, *pair(*lines))
        start = pl.multiple_of(y * PS, 16)
        back_x[pl.ds(start, PADS), :] = in_x[:, :128]
        back_x[pl.ds(start + PS, PADS), :] = in_x[:, 128:]
        return carry

    lax.fori_loop(0, SIDE // 2, along_x, 0, unroll=SIDE // 2)

    group = 4
    for i in range(SIDE // group):
        lines = [back_x[pl.ds(group * i + j, PADS, stride=PS), :] for j in range(group)]
        high, low = split(jnp.concatenate(lines, axis=0))
        factor = encode(dot(jnp.concatenate([high, low, high], axis=1), mzt), level)
        for j in range(0, group, 2):
            rows = [factor[k * PADS : k * PADS + SIDE] for k in (j, j + 1)]
            out_ref[(group * i + j) // 2, 0] = jnp.concatenate(rows, axis=0).astype(I16)
    for k in range(SIDE // 2, 16):
        out_ref[k, 0] = jnp.zeros_like(out_ref[k, 0])


CHUNK = 29
PEXTRA = 8
SEXTRA = 8
PW = PADW + PEXTRA
PS = PADS + SEXTRA


def run_jobs(channel, parts, scalars, top, bottom, view_data, mats):
    slots = mats[0].shape[0]
    hbm = pl.BlockSpec(memory_space=pltpu.HBM)
    smem = pl.BlockSpec(memory_space=pltpu.SMEM)
    specs = [smem] * len(scalars) + [hbm] * (len(parts) + 3)
    specs += [pl.BlockSpec((1,) + m.shape[1:], lambda slot: (slot, 0, 0)) for m in mats]
    return pl.pallas_call(
        functools.partial(job_kernel, channel),
        grid=(slots,),
        in_specs=specs,
        out_specs=pl.BlockSpec((16, 1, 2 * SIDE, 128), lambda slot: (0, slot, 0, 0)),
        scratch_shapes=[
            pltpu.VMEM((2, WIN, PADW, 128), BF16),
            pltpu.VMEM((2, WIN, WIN, 128), BF16),
            pltpu.VMEM((WIN, PADW, 128), BF16),
            pltpu.VMEM((WIN, PADW, 128), BF16),
            pltpu.VMEM((PADW * PW, 128), F32),
            pltpu.VMEM((PADW * PS, 128), F32),
            pltpu.VMEM((PADS * PS, 128), F32),
            pltpu.SemaphoreType.DMA((2, 6)),
        ],
        out_shape=pltpu.HBM((16, slots, 2 * SIDE, 128), I16),
        compiler_params=pltpu.CompilerParams(vmem_limit_bytes=18 << 20),
        cost_estimate=pl.CostEstimate(
            flops=slots * 20 * 128 * (WIN * PADW * (256 + 192 + 192 + 96) + 2 * SIDE * PADS * 192),
            transcendentals=slots * WIN * PADW * 128,
            bytes_accessed=slots * (2 * WIN * PADW * 128 * 2 + 16 * 2 * SIDE * 128 * 4),
        ),
        name="jobs",
    )(*scalars, *gathered_memory(parts), top, bottom, *far_memory(view_data, *mats))


def bands(taps, positions_out, positions_in):
    offsets = positions_in[None, :] - positions_out[:, None] + HALO
    sel = offsets[None, :, :, None] == jnp.arange(taps.shape[1])[None, None, None, :]
    return jnp.sum(jnp.where(sel, taps[:, None, None, :], 0.0), axis=3)


def high_low(matrix):
    high = lax.reduce_precision(matrix, 8, 7)
    return high.astype(BF16), (matrix - high).astype(BF16)


def job_matrices(taps, bricks):
    none = -1000
    far = 1000
    line = jnp.arange(128)
    row = jnp.arange(PADW)
    win_in = jnp.where(row < WIN, row, none)
    win_out = jnp.where(row < WIN, row, far)
    short = jnp.arange(PADS)
    inner_out = jnp.where(short < SIDE, short + HALO, far)
    x_in = jnp.where(row < RIM + 16, row - 1, row - 5)
    x_in = jnp.where((row >= RIM + 16) & (row < RIM + 20), none, x_in)
    x_in = jnp.where((x_in < 0) | (x_in >= WIN), none, x_in)
    inside = (row >= HALO)[None, :] | (bricks > 0)[:, None]
    inside &= (row < HALO + SIDE)[None, :] | (bricks < RING * RING - 1)[:, None]
    forward = lambda t, out, inp: bands(t, out, inp)
    backward = lambda t, out, inp: jnp.swapaxes(bands(t, inp, out), 1, 2)
    three = lambda pair: jnp.concatenate([pair[0], pair[0], pair[1]], axis=2)
    mz = high_low(jnp.swapaxes(forward(taps[:, 2], line, line), 1, 2))
    mzt = high_low(jnp.swapaxes(backward(taps[:, 2], line, line), 1, 2))
    win_in_far = jnp.where(row < WIN, row, far)
    inner_none = jnp.where(short < SIDE, short + HALO, none)
    return (
        jnp.concatenate(mz, axis=1),
        three(high_low(forward(taps[:, 0], win_out, x_in))),
        three(high_low(jnp.where(inside[:, None, :], forward(taps[:, 1], win_out, win_in), 0.0))),
        three(high_low(backward(taps[:, 1], inner_none, win_in_far))),
        three(high_low(backward(taps[:, 0], inner_none, win_in_far))),
        jnp.concatenate([mzt[0], mzt[0], mzt[1]], axis=1),
    )


MORE = 2.6


def add_kernel(owners, views, logs, *refs):
    total, level = refs[-2:]
    out_ref = refs[-3]
    workers, slots = refs[0].shape[:2]
    jobs = range(workers * slots)
    for b in range(workers):
        level[b] = -200.0
    for i in jobs:
        level[owners[i]] = jnp.maximum(level[owners[i]], logs[views[i]] + MORE)
    for channel, parts_ref in enumerate(refs[:-3]):
        total[...] = jnp.zeros_like(total)
        for i in jobs:
            total[owners[i]] += decode(parts_ref[i // slots, i % slots], logs[views[i]])
        for b in range(workers):
            out_ref[b, channel] = encode(total[b], level[b]).astype(I16)


def add_up(owners, views, logs, parts):
    vmem, smem = pl.BlockSpec(memory_space=pltpu.VMEM), pl.BlockSpec(memory_space=pltpu.SMEM)
    workers, rows = parts[0].shape[0], parts[0].shape[2:]
    return pl.pallas_call(
        add_kernel,
        in_specs=[smem] * 3 + [vmem] * len(parts),
        out_specs=vmem,
        out_shape=pltpu.HBM((workers, len(parts)) + rows, I16),
        scratch_shapes=[pltpu.VMEM((workers,) + rows, F32), pltpu.SMEM((workers,), F32)],
        compiler_params=pltpu.CompilerParams(vmem_limit_bytes=8 << 20),
        name="add_up",
    )(owners, views, logs, *parts)


def update_kernel(met, logs, est_ref, total, out_ref):
    seen, level = jnp.int32(0), jnp.float32(-200.0)
    for v in range(met.shape[0]):
        seen += met[v]
        level = jnp.where(met[v] > 0, jnp.maximum(level, logs[v] + MORE), level)
    seen = seen.astype(F32)
    for c in range(out_ref.shape[0]):
        for k in range(SIDE // 2):
            rows = decode(total[k, c], level)
            for j in range(2):
                part = rows[j * SIDE : (j + 1) * SIDE]
                out_ref[c, 2 * k + j] = est_ref[c, 2 * k + j] * part / seen


def update(met, logs, estimate, total):
    vmem, smem = pl.BlockSpec(memory_space=pltpu.VMEM), pl.BlockSpec(memory_space=pltpu.SMEM)
    return pl.pallas_call(
        update_kernel,
        in_specs=[smem, smem, vmem, vmem],
        out_specs=vmem,
        out_shape=jax.ShapeDtypeStruct(estimate.shape, F32),
        compiler_params=pltpu.CompilerParams(vmem_limit_bytes=12 << 20),
        name="update",
    )(met, logs, estimate, total)


def on_device(estimate, view_data, psf, background, slot_brick, slot_view, intersection):
    me = lax.axis_index("tile").astype(I32).reshape(1)
    groups, workers = lax.axis_size("view"), lax.axis_size("tile")
    upward = [(i, i + 1) for i in range(groups - 1)]
    downward = [(j, i) for i, j in upward]
    bricks, views = slot_brick[0, 0], slot_view[0, 0]
    slots = bricks.shape[0]

    wire = estimate.astype(BF16).transpose(0, 2, 1, 3)
    jobs = lax.optimization_barrier(jnp.concatenate([bricks, views]))
    note = jnp.pad(jobs.astype(BF16)[None, None], ((0, 0), (0, SIDE - 1), (0, 128 - 2 * slots)))
    note = jnp.broadcast_to(note, (wire.shape[0],) + note.shape[1:])
    wire = jnp.concatenate([wire[:, :, :RIM], note[:, :, None], wire[:, :, SIDE - RIM + 1 :]], axis=2)
    rings = ring_whole([wire[0], wire[1]], (0, 1))
    rings[0][1], psf, views = lax.optimization_barrier((rings[0][1], psf, views))
    chosen = views[:, None] == jnp.arange(psf.shape[0])[None, :]
    taps = jnp.sum(jnp.where(chosen[:, :, None, None], psf[None], 0.0), axis=1)
    mats = job_matrices(taps, bricks)
    logs = jnp.log2(jnp.maximum(4.0 / background * jnp.prod(jnp.sum(psf, axis=2), axis=1), 1e-30)) - 15.9
    rings, mats, logs = lax.optimization_barrier((rings, mats, logs))
    rings, view_data, bricks = lax.optimization_barrier((join(rings), view_data, bricks))
    near = ring_near(rings, (1, 0))
    above = lax.ppermute(bricks, "view", downward)
    below = lax.ppermute(bricks, "view", upward)
    data = view_data[0, 0]
    near, data, above, below = lax.optimization_barrier((near, data, above, below))
    gathered = ring_pass_on(near, (1, 0))

    rims = margins(gathered, me, above, below)
    edges = [
        (lax.ppermute(rims[2 * c], "view", upward), lax.ppermute(rims[2 * c + 1], "view", downward))
        for c in range(2)
    ]
    notes = jnp.concatenate([p[::SIDE, RIM, : 2 * slots] for p in gathered[0]], axis=0)
    places = place_of(jnp.arange(workers, dtype=I32), me[0], True)
    match = places[:, None] == jnp.arange(workers)[None, :]
    notes = jnp.sum(jnp.where(match[:, :, None], notes.astype(F32)[None], 0.0), axis=1)
    notes = notes.astype(I32)
    owners, seen_by = notes[:, :slots].reshape(-1), notes[:, slots:].reshape(-1)

    parts = []
    scalars = (me, bricks, views, background, logs)
    for channel in range(2):
        factors = run_jobs(channel, gathered[channel], scalars, *edges[channel], data, mats)
        parts.append(lax.all_to_all(factors, "tile", 0, 0, tiled=True))
    total = lax.all_to_all(add_up(owners, seen_by, logs, parts), "tile", 0, 0, tiled=True)
    return update(intersection[0, 0], logs, estimate, total)


def solution(mesh):
    placed = (
        P(None, "view", "tile", None),
        P("view", "tile", None, None, None, None, None),
        P(),
        P(),
        P("view", "tile", None),
        P("view", "tile", None),
        P("view", "tile", None),
    )
    return jax.shard_map(
        on_device,
        mesh=mesh,
        in_specs=placed,
        out_specs=P(None, "view", "tile", None),
        check_vma=False,
    )
```
